32 devices in a mesh: groups: 2 (over y), ctx: 4 (over z), head: 2 (over x), sub: 2 (over core).
Axes of the slice: x: 2, y: 2, z: 4, core: 2. Of those that a mesh axis runs over, the one named last changes fastest.
Arguments:
- att_query: bfloat16 [1024, 4096], P(('groups', 'ctx'), ('head', 'sub')), parts along dimension 0, may hold values from -4 to 4
- att_gate: bfloat16 [1024, 4096], P(('groups', 'ctx'), ('head', 'sub')), parts along dimension 0, may hold values from -6 to 6
- att_kv: bfloat16 [1024, 1024], P(('groups', 'ctx')), parts along dimension 0, may hold values from -4 to 4
- residual: bfloat16 [1024, 2048], P(('groups', 'ctx'), ('head', 'sub')), parts along dimension 0, may hold values from -0.19921875 to 0.19921875
- out_weight: bfloat16 [4096, 2048], P(('head', 'sub')), may hold values from -0.5 to 0.5
- norm_gain: float32 [2048], replicated, may hold values from 0.1 to 1.9
- in_weight: bfloat16 [2048, 8192], P(None, ('head', 'sub')), may hold values from -0.125 to 0.125
- beta_weight: bfloat16 [2048, 32], P(None, ('head', 'sub')), may hold values from -0.125 to 0.125
- log_decay: float32 [1024, 32], P(('groups', 'ctx'), ('head', 'sub')), parts along dimension 0, may hold values from -0.7 to 0, as said below
- delta_gain: float32 [128], replicated, may hold values from 0.1 to 1.9
Outputs:
- new_residual: bfloat16 [1024, 2048], P(('groups', 'ctx'), ('head', 'sub')), parts along dimension 0
- delta_out: bfloat16 [1024, 4096], P(('groups', 'ctx'), ('head', 'sub')), parts along dimension 0
The draws below stay inside these ranges and needn't reach their ends.
There are 2 independent parts, one for each index of `groups`. The reference program is written for one: setup_inputs(seed, part) draws one part's arguments, and reference() takes and returns one part's arrays. A program takes and returns all parts, laid end to end along the dimension named above; an argument that names none is the same for every part. Nothing has to cross between parts.
Inputs may be any that keep to these rules, and one draw needn't show every extreme that they name: `log_decay`: negative.
All inputs are finite; a program needn't handle non-finite values.
Results may differ from the reference program's by a relative error of at most 0.035.
Values may be sent and summed in bfloat16 or wider, within the bound.
A program may use at most 64 MiB of HBM per device.

```python
import math
import jax
import jax.numpy as jnp
from jax import lax

D = 2048
HEADS = 16
KV_HEADS = 2
HD = 256
KEY_HEADS = 16
DELTA_VALUE_HEADS = 32
DK = 128
DV = 128
PROMPT_TOKENS = 512
N_CTX = 4


def draw_att_kv(key, part):
    base_key = jax.random.fold_in(key, 11)
    entries = jnp.clip(jax.random.normal(base_key, (PROMPT_TOKENS, KV_HEADS, 2, HD), jnp.float32), -4.0, 4.0)
    return entries.reshape(PROMPT_TOKENS, KV_HEADS * 2 * HD).astype(jnp.bfloat16)


def draw_att_query(key, part):
    base_key = jax.random.fold_in(key, 13)
    entries = jnp.clip(jax.random.normal(base_key, (PROMPT_TOKENS, HEADS, HD), jnp.float32), -4.0, 4.0)
    return entries.reshape(PROMPT_TOKENS, HEADS * HD).astype(jnp.bfloat16)


def draw_log_decay(key, part):
    key_sequence = jax.random.split(jax.random.fold_in(key, 17), 4)
    quick_heads = jax.random.randint(key_sequence[0], (DELTA_VALUE_HEADS,), 0, 10) >= 5
    baseline_rate = jnp.where(quick_heads, -1.0 / 40.0, -math.log(10.0) / (2.0 * PROMPT_TOKENS))
    jaggedness = jnp.exp(jax.random.uniform(key_sequence[1], (PROMPT_TOKENS, DELTA_VALUE_HEADS), jnp.float32, math.log(0.5), math.log(2.0)))
    spike_events = jax.random.randint(key_sequence[2], (PROMPT_TOKENS, DELTA_VALUE_HEADS), 0, PROMPT_TOKENS) < 2
    spike_rate = jnp.log(jax.random.uniform(key_sequence[3], (PROMPT_TOKENS, DELTA_VALUE_HEADS), jnp.float32, 0.5, 0.8))
    gentle_spike = jnp.logical_and(spike_events, jnp.logical_not(quick_heads)[None, :])
    return jnp.where(gentle_spike, spike_rate, baseline_rate[None, :] * jaggedness).astype(jnp.float32)


def raised(values, stream_key, source, target, blocks, factor):
    owner, partner = [(jnp.arange(values.shape[position]) // (values.shape[position] // blocks)).reshape([-1 if axis == position else 1 for axis in range(values.ndim)]) for position in (source, target)]
    chosen = jax.random.permutation(stream_key, blocks)[partner]
    strong = (owner == chosen) | (owner == (partner + blocks // 2) % blocks)
    return jnp.where(strong, factor * values, values)


def steps_of(own_key, extent, cuts, least, top_value):
    level, own = 1.0, jax.random.fold_in(own_key, 6)
    for axis_at, shards_of in cuts:
        heights = jnp.exp(jax.random.uniform(jax.random.fold_in(own, axis_at), (shards_of,), jnp.float32, least / len(cuts), top_value / len(cuts)))
        level = level * jnp.repeat(heights, extent[axis_at] // shards_of).reshape([-1 if axis == axis_at else 1 for axis in range(len(extent))])
    return level


def centred(key, dims, width, bound, cuts=(), held_as=jnp.bfloat16):
    drawn = width * jax.random.normal(key, dims, jnp.float32)
    if cuts:
        drawn = drawn * steps_of(key, dims, cuts, -0.22, 0.18)
    return jnp.clip(drawn, -bound, bound).astype(held_as)


def noise_with(own_key, extent, width, limit, cuts, heavy, kind=jnp.bfloat16):
    array = width * jax.random.normal(own_key, extent, jnp.float32)
    if cuts:
        array = array * steps_of(own_key, extent, cuts, -0.22, 0.18)
    return jnp.clip(raised(array, jax.random.fold_in(own_key, 3), *heavy), -limit, limit).astype(kind)


def setup_inputs(seed: int = 0, part: int = 0) -> dict:
    arg_keys = jax.random.split(jax.random.key(seed), 11)
    part_keys = jax.random.split(jax.random.fold_in(arg_keys[10], part), 11)
    att_query = draw_att_query(jax.random.fold_in(jax.random.fold_in(arg_keys[10], part), 71), part)
    att_gate = centred(part_keys[1], (PROMPT_TOKENS, HEADS * HD), 1.0, 6.0, ((0, 4), (1, 4)))
    att_kv = draw_att_kv(jax.random.fold_in(jax.random.fold_in(arg_keys[10], part), 71), part)
    residual = jnp.clip(jax.random.uniform(part_keys[3], (PROMPT_TOKENS, D), jnp.float32, -0.19921875, 0.19921875) * steps_of(part_keys[3], (PROMPT_TOKENS, D), ((0, 4), (1, 4)), -0.4, 0.0), -0.19921875, 0.19921875).astype(jnp.bfloat16)
    out_weight = noise_with(arg_keys[4], (HEADS * HD, D), HD ** -0.5, 0.5, ((0, 4),), (0, 1, 4, 2.0))
    norm_gain = jnp.clip(1.0 + 0.18 * jax.random.normal(arg_keys[5], (D,), jnp.float32), 0.1, 1.9)
    in_weight = centred(arg_keys[6], (D, KEY_HEADS * (2 * DK + 2 * DV)), D ** -0.5, 0.125, ((1, 4),))
    beta_weight = centred(arg_keys[7], (D, DELTA_VALUE_HEADS), D ** -0.5, 0.125, ((1, 4),))
    log_decay = draw_log_decay(jax.random.fold_in(jax.random.fold_in(arg_keys[10], part), 71), part)
    delta_gain = jnp.clip(1.0 + 0.18 * jax.random.normal(arg_keys[9], (DV,), jnp.float32), 0.1, 1.9)
    return {"att_query": att_query, "att_gate": att_gate, "att_kv": att_kv, "residual": residual, "out_weight": out_weight, "norm_gain": norm_gain, "in_weight": in_weight, "beta_weight": beta_weight, "log_decay": log_decay, "delta_gain": delta_gain}


TOP_PRECISION = lax.Precision.HIGHEST
EPSILON = 1e-06

def stored_positions(total_rows, ctx_devices):
    half_rows = total_rows // (2 * ctx_devices)
    row_index = jnp.arange(total_rows, dtype=jnp.int32)
    device_of = row_index // (2 * half_rows)
    within_dev = row_index % (2 * half_rows)
    block_number = jnp.where(within_dev < half_rows, device_of, 2 * ctx_devices - 1 - device_of)
    return (block_number * half_rows + within_dev % half_rows).astype(jnp.int32)

def unit_rows(matrix):
    return matrix * lax.rsqrt(lax.optimization_barrier(jnp.sum(matrix * matrix, axis=-1, keepdims=True)) + EPSILON)

def reference(att_query, att_gate, att_kv, residual, out_weight, norm_gain, in_weight, beta_weight, log_decay, delta_gain):
    places = stored_positions(PROMPT_TOKENS, N_CTX)
    visible = places[:, None] >= places[None, :]
    group_size = HEADS // KV_HEADS
    score_scale = HD ** (-0.5)

    def one_head(head_number):
        query_rows = lax.dynamic_slice_in_dim(att_query, head_number * HD, HD, 1)
        gate_rows = lax.dynamic_slice_in_dim(att_gate, head_number * HD, HD, 1)
        kv_number = head_number // group_size
        key_rows = lax.dynamic_slice_in_dim(att_kv, kv_number * 2 * HD, HD, 1)
        value_rows = lax.dynamic_slice_in_dim(att_kv, kv_number * 2 * HD + HD, HD, 1)
        scores = jnp.dot(query_rows, key_rows.T, preferred_element_type=jnp.float32) * score_scale
        scores = jnp.where(visible, scores, -1e+30)
        row_max = lax.optimization_barrier(jnp.max(scores, axis=1, keepdims=True))
        weights = jnp.where(visible, jnp.exp(scores - row_max), 0.0)
        denominator = lax.optimization_barrier(jnp.sum(weights, axis=1, keepdims=True))
        attended = jnp.dot(weights.astype(jnp.bfloat16), value_rows, preferred_element_type=jnp.float32) / denominator
        return (attended * jax.nn.sigmoid(gate_rows.astype(jnp.float32))).astype(jnp.bfloat16)
    per_head = lax.map(one_head, jnp.arange(HEADS, dtype=jnp.int32))
    att_heads = jnp.transpose(per_head, (1, 0, 2)).reshape(PROMPT_TOKENS, HEADS * HD)
    hidden = residual.astype(jnp.float32) + jnp.dot(att_heads, out_weight, preferred_element_type=jnp.float32)
    new_residual = hidden.astype(jnp.bfloat16)
    mean_square = lax.optimization_barrier(jnp.mean(hidden * hidden, axis=1, keepdims=True))
    normed = (hidden * lax.rsqrt(mean_square + EPSILON) * norm_gain).astype(jnp.bfloat16)
    projected = jnp.dot(normed, in_weight, preferred_element_type=jnp.float32)
    grouped = projected.reshape(PROMPT_TOKENS, KEY_HEADS, 2 * DK + 2 * DV)
    query_unit = jnp.repeat(unit_rows(jax.nn.silu(grouped[:, :, :DK])) * DK ** (-0.5), 2, axis=1)
    key_unit = jnp.repeat(unit_rows(jax.nn.silu(grouped[:, :, DK:2 * DK])), 2, axis=1)
    value_all = jax.nn.silu(grouped[:, :, 2 * DK:]).reshape(PROMPT_TOKENS, DELTA_VALUE_HEADS, DV)
    beta_rows = jax.nn.sigmoid(jnp.dot(normed, beta_weight, preferred_element_type=jnp.float32))
    natural_order = jnp.argsort(places).astype(jnp.int32)

    def advance(recurrent_state, inputs):
        current_query, current_key, value_now, beta_now, decay_now = inputs
        retention = jnp.exp(decay_now)[:, None]
        retrieved_values = jnp.einsum('ge,gej->gj', current_key, recurrent_state, precision=TOP_PRECISION)
        written = beta_now[:, None] * (value_now - retention * retrieved_values)
        recurrent_state = retention[:, :, None] * recurrent_state + current_key[:, :, None] * written[:, None, :]
        layer_output = jnp.einsum('ge,gej->gj', current_query, recurrent_state, precision=TOP_PRECISION)
        return (recurrent_state, layer_output)
    start_state = jnp.zeros((DELTA_VALUE_HEADS, DK, DV), jnp.float32)
    sequence_inputs = (query_unit[natural_order], key_unit[natural_order], value_all[natural_order], beta_rows[natural_order], log_decay[natural_order])
    final_state, natural_out = lax.scan(advance, start_state, sequence_inputs)
    stored_out = natural_out[places]
    out_square = lax.optimization_barrier(jnp.mean(stored_out * stored_out, axis=2, keepdims=True))
    delta_out = (stored_out * lax.rsqrt(out_square + EPSILON) * delta_gain).astype(jnp.bfloat16)
    return (new_residual, delta_out.reshape(PROMPT_TOKENS, DELTA_VALUE_HEADS * DV))
```

```python
import functools

import jax
import jax.numpy as jnp
from jax import lax
from jax.experimental import pallas as pl
from jax.experimental.pallas import tpu as pltpu
from jax.sharding import PartitionSpec as P

HEADS = 16
KV_HEADS = 2
HD = 256
DK = 128
DV = 128
EPSILON = 1e-06
NEGATIVE = -1e30
CHUNKS = 2
PIECES = 2
F32 = jnp.float32
BF16 = jnp.bfloat16
MESH = pl.DeviceIdType.MESH


def dot(a, b):
    return jnp.dot(a, b, preferred_element_type=F32)


def dot_nt(a, b):
    return lax.dot_general(a, b, (((1,), (1,)), ((), ())), preferred_element_type=F32)


def dot_tn(a, b):
    return lax.dot_general(a, b, (((0,), (0,)), ((), ())), preferred_element_type=F32)


def silu(x):
    return x * jax.nn.sigmoid(x)


def unit(x):
    return x * lax.rsqrt(jnp.sum(x * x, axis=-1, keepdims=True) + EPSILON)


def remote(src, dst, sems, index, device):
    return pltpu.make_async_remote_copy(
        src_ref=src,
        dst_ref=dst,
        send_sem=sems.at[0, index],
        recv_sem=sems.at[1, index],
        device_id=device,
        device_id_type=MESH,
    )


def kernel(
    ctx_count,
    head_count,
    query_hbm,
    gate_hbm,
    kv_hbm,
    res_hbm,
    ow_hbm,
    norm_gain_hbm,
    iw_hbm,
    bw_hbm,
    ld_hbm,
    delta_gain_hbm,
    new_res_ref,
    delta_ref,
    query_ref,
    gate_ref,
    res_ref,
    norm_gain_ref,
    bw_ref,
    ld_ref,
    delta_gain_ref,
    kv,
    ow,
    iw,
    att,
    rs_send,
    rs_recv,
    x_send,
    x_recv,
    hid,
    macc,
    trans,
    offs,
    early_in,
    late_in,
    early_out,
    late_out,
    local_out,
    read,
    load_sem,
    kv_sem,
    kvf_sem,
    rs_sem,
    x_sem,
    ag_sem,
    agf_sem,
    early_sem,
    late_sem,
    *direct,
):
    c = lax.axis_index("ctx")
    h = lax.axis_index("head")
    s = lax.axis_index("sub")
    rows = query_ref.shape[0]
    half = rows // 2
    heads_here = query_ref.shape[1] // HD
    shard = h * 2 + s
    width = res_ref.shape[1]
    partner = {"sub": 1 - s}
    kv_number = shard * heads_here // (HEADS // KV_HEADS)

    own_rows = pl.ds(pl.multiple_of(c * rows, rows), rows)
    loads = []
    for part in range(2):
        start = pl.multiple_of(kv_number * 2 * HD + part * HD, HD)
        loads.append(
            pltpu.make_async_copy(
                kv_hbm.at[:, pl.ds(start, HD)], kv.at[part, own_rows], load_sem.at[part]
            )
        )
    ow_load = pltpu.make_async_copy(ow_hbm, ow, load_sem.at[2])
    iw_load = pltpu.make_async_copy(iw_hbm, iw, load_sem.at[3])
    small = [
        pltpu.make_async_copy(source, target, load_sem.at[4 + i])
        for i, (source, target) in enumerate(
            [
                (query_hbm, query_ref),
                (gate_hbm, gate_ref),
                (res_hbm, res_ref),
                (norm_gain_hbm, norm_gain_ref),
                (bw_hbm, bw_ref),
                (ld_hbm, ld_ref),
                (delta_gain_hbm, delta_gain_ref),
            ]
        )
    ]
    for load in loads + small:
        load.start()

    @pl.when(c == 0)
    def _():
        early_in[...] = jnp.zeros_like(early_in)

    barrier = pltpu.get_barrier_semaphore()
    for d in range(1, ctx_count):
        pl.semaphore_signal(
            barrier, inc=1, device_id={"ctx": lax.rem(c + d, ctx_count)}, device_id_type=MESH
        )
    for d in range(1, head_count):
        pl.semaphore_signal(
            barrier, inc=1, device_id={"head": lax.rem(h + d, head_count)}, device_id_type=MESH
        )
    pl.semaphore_signal(barrier, inc=1, device_id=partner, device_id_type=MESH)
    pl.semaphore_wait(barrier, ctx_count + head_count - 1)

    sends = []
    for load in loads:
        load.wait()
    gathers = []
    for d in range(1, ctx_count):
        piece = kv.at[s, own_rows]
        copy = remote(piece, piece, kv_sem, d - 1, {"ctx": lax.rem(c + d, ctx_count)})
        copy.start()
        gathers.append(copy)
    ow_load.start()
    forwards = []
    for d in range(1, ctx_count):
        gathers[d - 1].wait_recv()
        source = lax.rem(c - d + ctx_count, ctx_count)
        piece = kv.at[s, pl.ds(pl.multiple_of(source * rows, rows), rows)]
        copy = remote(piece, piece, kvf_sem, d - 1, partner)
        copy.start()
        forwards.append(copy)
    iw_load.start()
    for copy in forwards:
        copy.wait_recv()
    sends += gathers + forwards

    for load in small:
        load.wait()

    total_rows = ctx_count * rows
    q_row = lax.broadcasted_iota(jnp.int32, (rows, total_rows), 0)
    k_row = lax.broadcasted_iota(jnp.int32, (rows, total_rows), 1)
    shift = rows.bit_length() - 1
    k_dev = k_row >> shift
    k_in = k_row & (rows - 1)
    last_block = 2 * ctx_count - 1
    q_pos = jnp.where(q_row < half, c, last_block - c) * half + (q_row & (half - 1))
    k_pos = jnp.where(k_in < half, k_dev, last_block - k_dev) * half + (k_in & (half - 1))
    visible = q_pos >= k_pos
    keys = kv[0]
    values = kv[1]
    for n in range(heads_here):
        cols = slice(n * HD, (n + 1) * HD)
        scores = dot_nt(query_ref[:, cols], keys) * (HD**-0.5)
        scores = jnp.where(visible, scores, NEGATIVE)
        weights = jnp.exp(scores - jnp.max(scores, axis=1, keepdims=True))
        total = jnp.sum(weights, axis=1, keepdims=True)
        mixed = dot(weights.astype(BF16), values) / total
        att[:, cols] = (mixed * jax.nn.sigmoid(gate_ref[:, cols].astype(F32))).astype(BF16)

    ow_load.wait()
    attended = att[...]

    def out_slice(number):
        return dot(attended, ow[:, pl.ds(pl.multiple_of(number * width, width), width)])

    chunks = [slice(k * rows // CHUNKS, (k + 1) * rows // CHUNKS) for k in range(CHUNKS)]
    peers = [lax.rem(h + 1 + i, head_count) for i in range(head_count)]
    pair_copies = []
    for i in range(head_count):
        rs_send[i] = out_slice(peers[i] * 2 + 1 - s).astype(BF16)
        copy = remote(rs_send.at[i], rs_recv.at[i], rs_sem, i, partner)
        copy.start()
        pair_copies.append(copy)
    head_copies = []
    for i in range(head_count):
        part = out_slice(peers[i] * 2 + s)
        pair_copies[i].wait_recv()
        part = part + rs_recv[i].astype(F32)
        if i < head_count - 1:
            x_send[i] = part.astype(BF16)
            for k, lines in enumerate(chunks):
                copy = remote(
                    x_send.at[i, lines], x_recv.at[i, lines], x_sem, i * CHUNKS + k, {"head": peers[i]}
                )
                copy.start()
                head_copies.append(copy)
    part = part + res_ref[...].astype(F32)
    sends += pair_copies + head_copies
    to_heads = []
    to_partner = []
    for k, lines in enumerate(chunks):
        own = part[lines]
        for i in range(head_count - 1):
            head_copies[i * CHUNKS + k].wait_recv()
            own = own + x_recv[i, lines].astype(F32)
        own16 = own.astype(BF16)
        new_res_ref[lines, :] = own16
        hid[shard, lines] = own16
        mine = hid.at[shard, lines]
        for i in range(head_count - 1):
            copy = remote(mine, mine, ag_sem, i * CHUNKS + k, {"head": peers[i]})
            copy.start()
            to_heads.append(copy)
        copy = remote(mine, mine, agf_sem, (head_count - 1) * CHUNKS + k, partner)
        copy.start()
        to_partner.append(copy)
    iw_load.wait()

    def projected(r, start):
        cols = pl.ds(pl.multiple_of(r * width, width), width)
        piece = hid[r].astype(F32)
        scaled = (piece * norm_gain_ref[:, cols]).astype(BF16)
        term = dot(scaled, iw[cols, :])
        logits = dot_nt(bw_ref[:, cols], scaled)
        square = jnp.sum(piece * piece, axis=1, keepdims=True)
        if start is None:
            macc[...] = term
            return logits, square
        macc[...] += term
        return start[0] + logits, start[1] + square

    sources = [lax.rem(h - 1 - i + head_count, head_count) * 2 for i in range(head_count - 1)]
    parts = projected(shard, None)
    for k, lines in enumerate(chunks):
        for i in range(head_count - 1):
            to_heads[k * (head_count - 1) + i].wait_recv()
            piece = hid.at[sources[i] + s, lines]
            copy = remote(piece, piece, agf_sem, i * CHUNKS + k, partner)
            copy.start()
            to_partner.append(copy)
    for copy in to_partner[:CHUNKS]:
        copy.wait_recv()
    parts = projected(h * 2 + 1 - s, parts)
    for i in range(head_count - 1):
        parts = projected(sources[i] + s, parts)
    for copy in to_partner[CHUNKS:]:
        copy.wait_recv()
    for i in range(head_count - 1):
        parts = projected(sources[i] + 1 - s, parts)
    sends += to_heads + to_partner
    scale = lax.rsqrt(parts[1] / (2 * head_count * width) + EPSILON)
    group = 2 * DK + 2 * DV
    key_here = iw.shape[1] // group
    value_here = 2 * key_here

    row = lax.broadcasted_iota(jnp.int32, (rows, rows), 0)
    col = lax.broadcasted_iota(jnp.int32, (rows, rows), 1)
    same = (row < half) == (col < half)
    on_or_below = same & (row >= col)
    strictly = same & (row > col)
    eye = jnp.where(row == col, 1.0, 0.0)
    beta = jax.nn.sigmoid(parts[0].T * scale)
    lower = jnp.where(on_or_below, 1.0, 0.0)
    every = jnp.where(same, 1.0, 0.0)
    decays = ld_ref[...]

    def row_sums(picked):
        return lax.dot_general(
            decays,
            picked,
            (((1,), (1,)), ((), ())),
            precision=lax.Precision.HIGHEST,
            preferred_element_type=F32,
        )

    cum_row = row_sums(lower)
    sum_row = row_sums(every)
    cumulative = cum_row.T
    block_sum = sum_row.T
    growth = jnp.exp(cumulative)
    carry = jnp.exp(block_sum - cumulative)

    queries, grams, attends, values_of, keys_of = [], [], [], [], []
    for j in range(key_here):
        m = macc[:, j * group : (j + 1) * group] * scale
        q = unit(silu(m[:, :DK])) * DK**-0.5
        k = unit(silu(m[:, DK : 2 * DK]))
        v = silu(m[:, 2 * DK :])
        q16, k16 = q.astype(BF16), k.astype(BF16)
        queries.append(q)
        keys_of.append(k)
        values_of += [v[:, :DV], v[:, DV:]]
        grams.append(dot_nt(k16, k16))
        attends.append(dot_nt(q16, k16))
    systems, inverses, grids = [], [], []
    for n in range(value_here):
        gap = cumulative[:, n : n + 1] - cum_row[n : n + 1, :]
        grid = jnp.where(on_or_below, jnp.exp(jnp.where(on_or_below, gap, 0.0)), 0.0)
        system = jnp.where(strictly, beta[:, n : n + 1] * grams[n // 2] * grid, 0.0)
        grids.append((attends[n // 2] * grid).astype(BF16))
        systems.append(system)
        inverses.append(eye - jnp.where((row >> 1) == (col >> 1), system, 0.0))
    level = 1
    while (1 << level) < half:
        mask = ((row >> (level + 1)) == (col >> (level + 1))) & ((row >> level) != (col >> level))
        halves = [inverse.astype(BF16) for inverse in inverses]
        firsts = [
            dot(jnp.where(mask, system, 0.0).astype(BF16), inverse).astype(BF16)
            for system, inverse in zip(systems, halves)
        ]
        inverses = [
            full - dot(inverse, product)
            for full, inverse, product in zip(inverses, halves, firsts)
        ]
        level += 1
    last = ctx_count - 1
    nxt = {"ctx": lax.min(c + 1, last)}
    prv = {"ctx": lax.max(c - 1, 0)}

    def early_copy(n):
        return remote(early_out.at[n], early_in.at[n], early_sem, n, nxt)

    def late_copy(n):
        return remote(late_out.at[n], late_in.at[n], late_sem, n, prv)

    solutions, carries = [], []
    for n in range(value_here):
        beta_n = beta[:, n : n + 1]
        right = jnp.concatenate(
            [beta_n * values_of[n], (beta_n * growth[:, n : n + 1]) * keys_of[n // 2]], axis=1
        )
        solutions.append(dot(inverses[n].astype(BF16), right.astype(BF16)).astype(BF16))
        carries.append((keys_of[n // 2] * carry[:, n : n + 1]).astype(BF16))

    def piece_rows(p):
        return slice(p * DV // PIECES, (p + 1) * DV // PIECES)

    def block_ends(n, b):
        lines = slice(b * half, (b + 1) * half)
        ends = dot_tn(solutions[n][lines], carries[n][lines])
        offs[b, n] = ends[:DV]
        whole = jnp.exp(block_sum[b * half : b * half + 1, n : n + 1])
        trans[b, n] = (whole * eye[:DK, :DK] - ends[DV:]).astype(BF16)
        if b == 0:
            for p in range(PIECES):
                early_out[n * PIECES + p] = ends[piece_rows(p)].astype(BF16)

    def local_terms(n):
        inner = dot(grids[n], solutions[n])
        local_out[n] = inner[:, :DV]
        read[n] = (growth[:, n : n + 1] * queries[n // 2] - inner[:, DV:]).astype(BF16)

    def normed(n, b, out):
        lines = slice(b * half, (b + 1) * half)
        mean = jnp.mean(out * out, axis=1, keepdims=True)
        out = out * lax.rsqrt(mean + EPSILON) * delta_gain_ref[...]
        if isinstance(n, int):
            delta_ref[lines, n * DV : (n + 1) * DV] = out.astype(BF16)
        else:
            delta_ref[lines, pl.ds(pl.multiple_of(n * DV, DV), DV)] = out.astype(BF16)

    def finish(n, b, state):
        lines = slice(b * half, (b + 1) * half)
        normed(n, b, local_out[n, lines, :] + dot_nt(read[n, lines, :], state))

    def passed(n, p, b, state):
        return (dot(state, trans[b, n]) + offs[b, n, piece_rows(p), :]).astype(BF16)

    def whole_state(ref, n):
        return jnp.concatenate([ref[n * PIECES + p] for p in range(PIECES)], axis=0)

    if ctx_count == 4:
        four_blocks(
            c,
            half,
            value_here,
            early_copy,
            block_ends,
            local_terms,
            normed,
            finish,
            passed,
            whole_state,
            trans,
            offs,
            early_in,
            early_out,
            local_out,
            read,
            *direct,
        )
        for copy in sends:
            copy.wait_send()
        return

    for n in range(value_here):
        block_ends(n, 0)

    @pl.when(c == 0)
    def _():
        for n in range(value_here * PIECES):
            early_copy(n).start()

    for n in range(value_here):
        block_ends(n, 1)
        local_terms(n)

    @pl.when(c > 0)
    def _():
        def early_turn(n, carried):
            for p in range(PIECES):
                at = n * PIECES + p
                early_copy(at).wait_recv()
                end = passed(n, p, 0, early_in[at])

                @pl.when(c < last)
                def _():
                    early_out[at] = end
                    early_copy(at).start()

                @pl.when(c == last)
                def _():
                    late_in[at] = end
                    late_out[at] = passed(n, p, 1, end)
                    late_copy(at).start()

            return carried

        lax.fori_loop(0, value_here, early_turn, 0)

    for n in range(value_here):
        finish(n, 0, whole_state(early_in, n))

    @pl.when((c > 0) & (c < last))
    def _():
        def late_turn(n, carried):
            for p in range(PIECES):
                at = n * PIECES + p
                late_copy(at).wait_recv()
                late_out[at] = passed(n, p, 1, late_in[at])
                late_copy(at).start()
            return carried

        lax.fori_loop(0, value_here, late_turn, 0)

    @pl.when(c == 0)
    def _():
        def last_turn(n, carried):
            for p in range(PIECES):
                late_copy(n * PIECES + p).wait_recv()
            finish(n, 1, whole_state(late_in, n))
            return carried

        lax.fori_loop(0, value_here, last_turn, 0)

    @pl.when(c > 0)
    def _():
        for n in range(value_here):
            finish(n, 1, whole_state(late_in, n))

    for copy in sends:
        copy.wait_send()

    def drain(n, carry):
        @pl.when(c < last)
        def _():
            early_copy(n).wait_send()

        @pl.when(c > 0)
        def _():
            late_copy(n).wait_send()

        return carry

    lax.fori_loop(0, value_here * PIECES, drain, 0)


def four_blocks(
    c,
    half,
    value_here,
    early_copy,
    block_ends,
    local_terms,
    normed,
    finish,
    passed,
    whole_state,
    trans,
    offs,
    early_in,
    early_out,
    local_out,
    read,
    ra,
    a_out,
    c_in,
    c_out,
    v_in,
    v_out,
    comp_in,
    comp_out,
    fifth,
    ra_sem,
    c_sem,
    v_sem,
    comp_sem,
):
    low, high = pl.ds(0, half), pl.ds(half, half)
    late = slice(half, 2 * half)

    def to(device):
        return {"ctx": device}

    def read_six(n):
        return remote(read.at[n, high], ra.at[n, low], ra_sem, n, to(2))

    def read_seven(n):
        return remote(read.at[n, high], ra.at[n, high], ra_sem, value_here + n, to(1))

    def read_back(n):
        return remote(a_out.at[n], ra.at[n, high], ra_sem, value_here + n, to(2))

    def constant(n):
        return remote(c_out.at[n], c_in.at[n], c_sem, n, to(0))

    def joint(n):
        return remote(comp_out.at[n], comp_in.at[n], comp_sem, n, to(2))

    def rows_six(n):
        return remote(v_out.at[n, low], v_in.at[n], v_sem, n, to(1))

    def rows_seven(n):
        return remote(v_out.at[n, high], v_in.at[n], v_sem, value_here + n, to(0))

    def each(body):
        def turn(n, carried):
            body(n)
            return carried

        lax.fori_loop(0, value_here, turn, 0)

    def halves(n):
        return [n * PIECES + p for p in range(PIECES)]

    for n in range(value_here):
        block_ends(n, 0)
    for n in range(value_here):
        block_ends(n, 1)

    @pl.when(c == 3)
    def _():
        def join(n):
            fourth = trans[1, n]
            comp_out[n, 0] = dot(trans[0, n], fourth).astype(BF16)
            comp_out[n, 1] = (dot(offs[0, n].astype(BF16), fourth) + offs[1, n]).astype(BF16)
            joint(n).start()

        each(join)

    for n in range(value_here):
        local_terms(n)

    @pl.when(c == 0)
    def _():
        def send(n):
            for at in halves(n):
                early_copy(at).start()
            read_seven(n).start()

        each(send)
        for n in range(value_here):
            normed(n, 0, local_out[n, :half, :])

        def last(n):
            constant(n).wait_recv()
            rows_seven(n).wait_recv()
            normed(n, 1, local_out[n, late, :] + c_in[n].astype(F32) + v_in[n].astype(F32))

        each(last)

        def drain(n):
            for at in halves(n):
                early_copy(at).wait_send()
            read_seven(n).wait_send()

        each(drain)

    @pl.when(c == 1)
    def _():
        each(lambda n: read_six(n).start())

        def turn(n):
            for p, at in enumerate(halves(n)):
                early_copy(at).wait_recv()
                early_out[at] = passed(n, p, 0, early_in[at])
                early_copy(at).start()
            read_seven(n).wait_recv()
            seven = ra[n, late, :]
            a_out[n] = dot_nt(seven, trans[1, n]).astype(BF16)
            read_back(n).start()
            c_out[n] = dot_nt(seven, offs[1, n].astype(BF16)).astype(BF16)
            constant(n).start()

        each(turn)
        for n in range(value_here):
            finish(n, 0, whole_state(early_in, n))

        def last(n):
            rows_six(n).wait_recv()
            normed(n, 1, local_out[n, late, :] + v_in[n].astype(F32))

        each(last)

        def drain(n):
            read_six(n).wait_send()
            for at in halves(n):
                early_copy(at).wait_send()
            read_back(n).wait_send()
            constant(n).wait_send()

        each(drain)

    @pl.when(c == 2)
    def _():
        def turn(n):
            for p, at in enumerate(halves(n)):
                early_copy(at).wait_recv()
                early_out[at] = passed(n, p, 0, early_in[at])
                early_copy(at).start()
            joint(n).wait_recv()
            state = dot(whole_state(early_out, n), comp_in[n, 0]) + comp_in[n, 1].astype(F32)
            state = state.astype(BF16)
            fifth[n] = state
            read_six(n).wait_recv()
            read_back(n).wait_recv()
            reads = ra[n]
            pulled = dot_nt(reads, trans[1, n]).astype(BF16)
            plain = dot_nt(reads, offs[1, n].astype(BF16))
            v_out[n] = (dot_nt(pulled, state) + plain).astype(BF16)
            rows_seven(n).start()
            rows_six(n).start()

        each(turn)
        for n in range(value_here):
            finish(n, 0, whole_state(early_in, n))
            finish(n, 1, fifth[n])

        def drain(n):
            for at in halves(n):
                early_copy(at).wait_send()
            rows_six(n).wait_send()
            rows_seven(n).wait_send()

        each(drain)

    @pl.when(c == 3)
    def _():
        def turn(n):
            for p, at in enumerate(halves(n)):
                early_copy(at).wait_recv()
                early_out[at] = passed(n, p, 0, early_in[at])
            finish(n, 0, whole_state(early_in, n))
            finish(n, 1, whole_state(early_out, n))
            joint(n).wait_send()

        each(turn)


def settle(first_ref, second_ref, first_out, second_out):
    first_out[...] = first_ref[...]
    second_out[...] = second_ref[...]


def local(
    ctx_count,
    head_count,
    att_query,
    att_gate,
    att_kv,
    residual,
    out_weight,
    norm_gain,
    in_weight,
    beta_weight,
    log_decay,
    delta_gain,
):
    rows = att_query.shape[0]
    width = residual.shape[1]
    value_here = log_decay.shape[1]
    vmem = pl.BlockSpec(memory_space=pltpu.VMEM)
    hbm = pl.BlockSpec(memory_space=pl.ANY)
    heads_less = max(head_count - 1, 1)
    pair = pltpu.SemaphoreType.DMA
    direct = []
    if ctx_count == 4:
        block = (value_here, rows // 2, DK)
        square = (value_here, DK, DK)
        both = (value_here, 2, DK, DK)
        direct = [
            pltpu.VMEM((value_here, rows, DK), BF16),
            *[pltpu.VMEM(block, BF16)] * 4,
            pltpu.VMEM((value_here, rows, DK), BF16),
            pltpu.VMEM(both, BF16),
            pltpu.VMEM(both, BF16),
            pltpu.VMEM(square, BF16),
            pair((2, 2 * value_here)),
            pair((2, value_here)),
            pair((2, 2 * value_here)),
            pair((2, value_here)),
        ]
    outputs = pl.pallas_call(
        functools.partial(kernel, ctx_count, head_count),
        out_shape=(
            jax.ShapeDtypeStruct((rows, width), BF16),
            jax.ShapeDtypeStruct((rows, value_here * DV), BF16),
        ),
        in_specs=[hbm] * 10,
        out_specs=(vmem, vmem),
        scratch_shapes=[
            pltpu.VMEM(att_query.shape, BF16),
            pltpu.VMEM(att_gate.shape, BF16),
            pltpu.VMEM(residual.shape, BF16),
            pltpu.VMEM((1, norm_gain.shape[0]), F32),
            pltpu.VMEM(beta_weight.shape[::-1], BF16),
            pltpu.VMEM(log_decay.shape[::-1], F32),
            pltpu.VMEM((1, DV), F32),
            pltpu.VMEM((2, ctx_count * rows, HD), BF16),
            pltpu.VMEM(out_weight.shape, BF16),
            pltpu.VMEM(in_weight.shape, BF16),
            pltpu.VMEM(att_query.shape, BF16),
            pltpu.VMEM((head_count, rows, width), BF16),
            pltpu.VMEM((head_count, rows, width), BF16),
            pltpu.VMEM((heads_less, rows, width), BF16),
            pltpu.VMEM((heads_less, rows, width), BF16),
            pltpu.VMEM((2 * head_count, rows, width), BF16),
            pltpu.VMEM((rows, in_weight.shape[1]), F32),
            pltpu.VMEM((2, value_here, DK, DK), BF16),
            pltpu.VMEM((2, value_here, DK, DV), F32),
            pltpu.VMEM((value_here * PIECES, DV // PIECES, DK), BF16),
            pltpu.VMEM((value_here * PIECES, DV // PIECES, DK), BF16),
            pltpu.VMEM((value_here * PIECES, DV // PIECES, DK), BF16),
            pltpu.VMEM((value_here * PIECES, DV // PIECES, DK), BF16),
            pltpu.VMEM((value_here, rows, DV), F32),
            pltpu.VMEM((value_here, rows, DK), BF16),
            pair((11,)),
            pair((2, ctx_count)),
            pair((2, ctx_count)),
            pair((2, head_count)),
            pair((2, head_count * CHUNKS)),
            pair((2, head_count * CHUNKS)),
            pair((2, head_count * CHUNKS)),
            pair((2, value_here * PIECES)),
            pair((2, value_here * PIECES)),
            *direct,
        ],
        compiler_params=pltpu.CompilerParams(collective_id=0, has_side_effects=True),
    )(
        att_query,
        att_gate,
        att_kv,
        residual,
        out_weight,
        norm_gain.reshape(1, -1),
        in_weight,
        beta_weight.T,
        log_decay.T,
        delta_gain.reshape(1, -1),
    )
    return pl.pallas_call(
        settle,
        out_shape=tuple(jax.ShapeDtypeStruct(x.shape, x.dtype) for x in outputs),
        in_specs=[vmem, vmem],
        out_specs=(vmem, vmem),
    )(*outputs)


def solution(mesh):
    return jax.shard_map(
        functools.partial(local, mesh.shape["ctx"], mesh.shape["head"]),
        mesh=mesh,
        in_specs=(
            P(("groups", "ctx"), ("head", "sub")),
            P(("groups", "ctx"), ("head", "sub")),
            P(("groups", "ctx"), None),
            P(("groups", "ctx"), ("head", "sub")),
            P(("head", "sub"), None),
            P(),
            P(None, ("head", "sub")),
            P(None, ("head", "sub")),
            P(("groups", "ctx"), ("head", "sub")),
            P(),
        ),
        out_specs=(P(("groups", "ctx"), ("head", "sub")), P(("groups", "ctx"), ("head", "sub"))),
        check_vma=False,
    )
```

```python
import functools

import jax
import jax.numpy as jnp
from jax import lax
from jax.experimental import pallas as pl
from jax.experimental.pallas import tpu as pltpu
from jax.sharding import PartitionSpec as P

HEADS = 16
KV_HEADS = 2
HD = 256
DK = 128
DV = 128
EPSILON = 1e-06
NEGATIVE = -1e30
CHUNKS = 2
PIECES = 2
F32 = jnp.float32
BF16 = jnp.bfloat16
MESH = pl.DeviceIdType.MESH


def dot(a, b):
    return jnp.dot(a, b, preferred_element_type=F32)


def dot_nt(a, b):
    return lax.dot_general(a, b, (((1,), (1,)), ((), ())), preferred_element_type=F32)


def dot_tn(a, b):
    return lax.dot_general(a, b, (((0,), (0,)), ((), ())), preferred_element_type=F32)


def silu(x):
    return x * jax.nn.sigmoid(x)


def unit(x):
    return x * lax.rsqrt(jnp.sum(x * x, axis=-1, keepdims=True) + EPSILON)


def remote(src, dst, sems, index, device):
    return pltpu.make_async_remote_copy(
        src_ref=src,
        dst_ref=dst,
        send_sem=sems.at[0, index],
        recv_sem=sems.at[1, index],
        device_id=device,
        device_id_type=MESH,
    )


def kernel(
    ctx_count,
    head_count,
    query_hbm,
    gate_hbm,
    kv_hbm,
    res_hbm,
    ow_hbm,
    norm_gain_hbm,
    iw_hbm,
    bw_hbm,
    ld_hbm,
    delta_gain_hbm,
    new_res_ref,
    delta_ref,
    query_ref,
    gate_ref,
    res_ref,
    norm_gain_ref,
    bw_ref,
    ld_ref,
    delta_gain_ref,
    kv,
    ow,
    iw,
    att,
    rs_send,
    rs_recv,
    x_send,
    x_recv,
    hid,
    macc,
    grid_ref,
    trans,
    offs,
    early_in,
    late_in,
    early_out,
    late_out,
    local_out,
    read,
    load_sem,
    kv_sem,
    kvf_sem,
    rs_sem,
    x_sem,
    ag_sem,
    agf_sem,
    early_sem,
    late_sem,
    *direct,
):
    c = lax.axis_index("ctx")
    h = lax.axis_index("head")
    s = lax.axis_index("sub")
    rows = query_ref.shape[0]
    half = rows // 2
    heads_here = query_ref.shape[1] // HD
    shard = h * 2 + s
    width = res_ref.shape[1]
    partner = {"sub": 1 - s}
    kv_number = shard * heads_here // (HEADS // KV_HEADS)

    early_all = ctx_count * half

    def early_block(device):
        return pl.ds(pl.multiple_of(device * half, half), half)

    def late_block(device):
        return pl.ds(pl.multiple_of(early_all + device * half, half), half)

    loads = []
    for e, place in enumerate([early_block(c), late_block(c)]):
        for part in range(2):
            start = pl.multiple_of(kv_number * 2 * HD + part * HD, HD)
            loads.append(
                pltpu.make_async_copy(
                    kv_hbm.at[e * half : (e + 1) * half, pl.ds(start, HD)],
                    kv.at[part, place],
                    load_sem.at[9 + 2 * e + part],
                )
            )
    ow_load = pltpu.make_async_copy(ow_hbm, ow, load_sem.at[0])
    iw_load = pltpu.make_async_copy(iw_hbm, iw, load_sem.at[1])
    small = [
        pltpu.make_async_copy(source, target, load_sem.at[2 + i])
        for i, (source, target) in enumerate(
            [
                (ld_hbm, ld_ref),
                (query_hbm, query_ref),
                (gate_hbm, gate_ref),
                (res_hbm, res_ref),
                (norm_gain_hbm, norm_gain_ref),
                (bw_hbm, bw_ref),
                (delta_gain_hbm, delta_gain_ref),
            ]
        )
    ]
    barrier = pltpu.get_barrier_semaphore()
    for d in range(1, ctx_count):
        pl.semaphore_signal(
            barrier, inc=1, device_id={"ctx": lax.rem(c + d, ctx_count)}, device_id_type=MESH
        )
    for d in range(1, head_count):
        pl.semaphore_signal(
            barrier, inc=1, device_id={"head": lax.rem(h + d, head_count)}, device_id_type=MESH
        )
    pl.semaphore_signal(barrier, inc=1, device_id=partner, device_id_type=MESH)
    for load in loads + small:
        load.start()

    @pl.when(c == 0)
    def _():
        early_in[...] = jnp.zeros_like(early_in)

    for d in range(1, ctx_count):

        @pl.when(c >= d)
        def _():
            kv[:, late_block(c - d), :] = jnp.zeros((2, half, HD), BF16)

    pl.semaphore_wait(barrier, ctx_count + head_count - 1)

    sends = []
    for load in loads:
        load.wait()
    others = range(1, ctx_count)

    def late_kv(d):
        piece = kv.at[s, late_block(c)]
        return remote(piece, piece, kv_sem, ctx_count + d - 1, {"ctx": lax.max(c - d, 0)})

    def late_forward(d):
        piece = kv.at[s, late_block(lax.min(c + d, ctx_count - 1))]
        return remote(piece, piece, kvf_sem, ctx_count + d - 1, partner)

    gathers = []
    for d in others:
        piece = kv.at[s, early_block(c)]
        copy = remote(piece, piece, kv_sem, d - 1, {"ctx": lax.rem(c + d, ctx_count)})
        copy.start()
        gathers.append(copy)
    for d in others:

        @pl.when(c >= d)
        def _():
            late_kv(d).start()

    ow_load.start()
    row = lax.broadcasted_iota(jnp.int32, (rows, rows), 0)
    col = lax.broadcasted_iota(jnp.int32, (rows, rows), 1)
    same = (row < half) == (col < half)
    on_or_below = same & (row >= col)
    strictly = same & (row > col)
    eye = jnp.where(row == col, 1.0, 0.0)
    small[0].wait()
    lower = jnp.where(on_or_below, 1.0, 0.0)
    every = jnp.where(same, 1.0, 0.0)
    decays = ld_ref[...]

    def row_sums(picked):
        return lax.dot_general(
            decays,
            picked,
            (((1,), (1,)), ((), ())),
            precision=lax.Precision.HIGHEST,
            preferred_element_type=F32,
        )

    cum_row = row_sums(lower)
    sum_row = row_sums(every)
    cumulative = cum_row.T
    block_sum = sum_row.T
    growth = jnp.exp(cumulative)
    carry = jnp.exp(block_sum - cumulative)
    for n in range(ld_ref.shape[0]):
        gap = cumulative[:, n : n + 1] - cum_row[n : n + 1, :]
        grid_ref[n] = jnp.where(on_or_below, jnp.exp(jnp.where(on_or_below, gap, 0.0)), 0.0)

    forwards = []
    for d in others:
        gathers[d - 1].wait_recv()
        piece = kv.at[s, early_block(lax.rem(c - d + ctx_count, ctx_count))]
        copy = remote(piece, piece, kvf_sem, d - 1, partner)
        copy.start()
        forwards.append(copy)
    for d in others:

        @pl.when(c + d < ctx_count)
        def _():
            late_kv(d).wait_recv()
            late_forward(d).start()

    iw_load.start()
    for copy in forwards:
        copy.wait_recv()
    for d in others:

        @pl.when(c + d < ctx_count)
        def _():
            late_forward(d).wait_recv()

    sends += gathers + forwards

    for load in small[1:]:
        load.wait()

    total_rows = ctx_count * rows
    q_row = lax.broadcasted_iota(jnp.int32, (rows, total_rows), 0)
    k_row = lax.broadcasted_iota(jnp.int32, (rows, total_rows), 1)
    k_block = k_row >> (half.bit_length() - 1)
    last_block = 2 * ctx_count - 1
    q_pos = jnp.where(q_row < half, c, last_block - c) * half + (q_row & (half - 1))
    k_block = jnp.where(k_row < early_all, k_block, last_block + ctx_count - k_block)
    k_pos = k_block * half + (k_row & (half - 1))
    visible = q_pos >= k_pos
    keys = kv[0]
    values = kv[1]
    for n in range(heads_here):
        cols = slice(n * HD, (n + 1) * HD)
        scores = dot_nt(query_ref[:, cols], keys) * (HD**-0.5)
        scores = jnp.where(visible, scores, NEGATIVE)
        weights = jnp.exp(scores - jnp.max(scores, axis=1, keepdims=True))
        total = jnp.sum(weights, axis=1, keepdims=True)
        mixed = dot(weights.astype(BF16), values) / total
        att[:, cols] = (mixed * jax.nn.sigmoid(gate_ref[:, cols].astype(F32))).astype(BF16)

    ow_load.wait()
    attended = att[...]

    def out_slice(number):
        return dot(attended, ow[:, pl.ds(pl.multiple_of(number * width, width), width)])

    chunks = [slice(k * rows // CHUNKS, (k + 1) * rows // CHUNKS) for k in range(CHUNKS)]
    peers = [lax.rem(h + 1 + i, head_count) for i in range(head_count)]
    pair_copies = []
    for i in range(head_count):
        rs_send[i] = out_slice(peers[i] * 2 + 1 - s).astype(BF16)
        copy = remote(rs_send.at[i], rs_recv.at[i], rs_sem, i, partner)
        copy.start()
        pair_copies.append(copy)
    head_copies = []
    for i in range(head_count):
        part = out_slice(peers[i] * 2 + s)
        pair_copies[i].wait_recv()
        part = part + rs_recv[i].astype(F32)
        if i < head_count - 1:
            x_send[i] = part.astype(BF16)
            for k, lines in enumerate(chunks):
                copy = remote(
                    x_send.at[i, lines], x_recv.at[i, lines], x_sem, i * CHUNKS + k, {"head": peers[i]}
                )
                copy.start()
                head_copies.append(copy)
    part = part + res_ref[...].astype(F32)
    sends += pair_copies + head_copies
    to_heads = []
    to_partner = []
    for k, lines in enumerate(chunks):
        own = part[lines]
        for i in range(head_count - 1):
            head_copies[i * CHUNKS + k].wait_recv()
            own = own + x_recv[i, lines].astype(F32)
        own16 = own.astype(BF16)
        new_res_ref[lines, :] = own16
        hid[shard, lines] = own16
        mine = hid.at[shard, lines]
        for i in range(head_count - 1):
            copy = remote(mine, mine, ag_sem, i * CHUNKS + k, {"head": peers[i]})
            copy.start()
            to_heads.append(copy)
        copy = remote(mine, mine, agf_sem, (head_count - 1) * CHUNKS + k, partner)
        copy.start()
        to_partner.append(copy)
    iw_load.wait()

    def projected(r, start):
        cols = pl.ds(pl.multiple_of(r * width, width), width)
        piece = hid[r].astype(F32)
        scaled = (piece * norm_gain_ref[:, cols]).astype(BF16)
        term = dot(scaled, iw[cols, :])
        logits = dot_nt(bw_ref[:, cols], scaled)
        square = jnp.sum(piece * piece, axis=1, keepdims=True)
        if start is None:
            macc[...] = term
            return logits, square
        macc[...] += term
        return start[0] + logits, start[1] + square

    sources = [lax.rem(h - 1 - i + head_count, head_count) * 2 for i in range(head_count - 1)]
    parts = projected(shard, None)
    for k, lines in enumerate(chunks):
        for i in range(head_count - 1):
            to_heads[k * (head_count - 1) + i].wait_recv()
            piece = hid.at[sources[i] + s, lines]
            copy = remote(piece, piece, agf_sem, i * CHUNKS + k, partner)
            copy.start()
            to_partner.append(copy)
    for copy in to_partner[:CHUNKS]:
        copy.wait_recv()
    parts = projected(h * 2 + 1 - s, parts)
    for i in range(head_count - 1):
        parts = projected(sources[i] + s, parts)
    for copy in to_partner[CHUNKS:]:
        copy.wait_recv()
    for i in range(head_count - 1):
        parts = projected(sources[i] + 1 - s, parts)
    sends += to_heads + to_partner
    scale = lax.rsqrt(parts[1] / (2 * head_count * width) + EPSILON)
    group = 2 * DK + 2 * DV
    key_here = iw.shape[1] // group
    value_here = 2 * key_here

    beta = jax.nn.sigmoid(parts[0].T * scale)
    queries, grams, attends, values_of, keys_of = [], [], [], [], []
    for j in range(key_here):
        m = macc[:, j * group : (j + 1) * group] * scale
        q = unit(silu(m[:, :DK])) * DK**-0.5
        k = unit(silu(m[:, DK : 2 * DK]))
        v = silu(m[:, 2 * DK :])
        q16, k16 = q.astype(BF16), k.astype(BF16)
        queries.append(q)
        keys_of.append(k)
        values_of += [v[:, :DV], v[:, DV:]]
        grams.append(dot_nt(k16, k16))
        attends.append(dot_nt(q16, k16))
    systems, inverses, grids = [], [], []
    for n in range(value_here):
        grid = grid_ref[n]
        system = jnp.where(strictly, beta[:, n : n + 1] * grams[n // 2] * grid, 0.0)
        grids.append((attends[n // 2] * grid).astype(BF16))
        systems.append(system)
        inverses.append(eye - jnp.where((row >> 1) == (col >> 1), system, 0.0))
    level = 1
    while (1 << level) < half:
        mask = ((row >> (level + 1)) == (col >> (level + 1))) & ((row >> level) != (col >> level))
        halves = [inverse.astype(BF16) for inverse in inverses]
        firsts = [
            dot(jnp.where(mask, system, 0.0).astype(BF16), inverse).astype(BF16)
            for system, inverse in zip(systems, halves)
        ]
        inverses = [
            full - dot(inverse, product)
            for full, inverse, product in zip(inverses, halves, firsts)
        ]
        level += 1
    last = ctx_count - 1
    nxt = {"ctx": lax.min(c + 1, last)}
    prv = {"ctx": lax.max(c - 1, 0)}

    def early_copy(n):
        return remote(early_out.at[n], early_in.at[n], early_sem, n, nxt)

    def late_copy(n):
        return remote(late_out.at[n], late_in.at[n], late_sem, n, prv)

    solutions, carries = [], []
    for n in range(value_here):
        beta_n = beta[:, n : n + 1]
        right = jnp.concatenate(
            [beta_n * values_of[n], (beta_n * growth[:, n : n + 1]) * keys_of[n // 2]], axis=1
        )
        solutions.append(dot(inverses[n].astype(BF16), right.astype(BF16)).astype(BF16))
        carries.append((keys_of[n // 2] * carry[:, n : n + 1]).astype(BF16))

    def piece_rows(p):
        return slice(p * DV // PIECES, (p + 1) * DV // PIECES)

    def block_ends(n, b):
        lines = slice(b * half, (b + 1) * half)
        ends = dot_tn(solutions[n][lines], carries[n][lines])
        offs[b, n] = ends[:DV]
        whole = jnp.exp(block_sum[b * half : b * half + 1, n : n + 1])
        trans[b, n] = (whole * eye[:DK, :DK] - ends[DV:]).astype(BF16)
        if b == 0:
            for p in range(PIECES):
                early_out[n * PIECES + p] = ends[piece_rows(p)].astype(BF16)

    def drain_sends():
        for copy in sends:
            copy.wait_send()
        for d in others:

            @pl.when(c >= d)
            def _():
                late_kv(d).wait_send()

            @pl.when(c + d < ctx_count)
            def _():
                late_forward(d).wait_send()

    def local_terms(n):
        inner = dot(grids[n], solutions[n])
        local_out[n] = inner[:, :DV]
        read[n] = (growth[:, n : n + 1] * queries[n // 2] - inner[:, DV:]).astype(BF16)

    def normed(n, b, out):
        lines = slice(b * half, (b + 1) * half)
        mean = jnp.mean(out * out, axis=1, keepdims=True)
        out = out * lax.rsqrt(mean + EPSILON) * delta_gain_ref[...]
        if isinstance(n, int):
            delta_ref[lines, n * DV : (n + 1) * DV] = out.astype(BF16)
        else:
            delta_ref[lines, pl.ds(pl.multiple_of(n * DV, DV), DV)] = out.astype(BF16)

    def finish(n, b, state):
        lines = slice(b * half, (b + 1) * half)
        normed(n, b, local_out[n, lines, :] + dot_nt(read[n, lines, :], state))

    def passed(n, p, b, state):
        return (dot(state, trans[b, n]) + offs[b, n, piece_rows(p), :]).astype(BF16)

    def whole_state(ref, n):
        return jnp.concatenate([ref[n * PIECES + p] for p in range(PIECES)], axis=0)

    if ctx_count == 4:
        four_blocks(
            c,
            half,
            value_here,
            early_copy,
            block_ends,
            local_terms,
            normed,
            finish,
            passed,
            whole_state,
            trans,
            offs,
            early_in,
            early_out,
            local_out,
            read,
            *direct,
        )
        drain_sends()
        return

    for n in range(value_here):
        block_ends(n, 0)

    @pl.when(c == 0)
    def _():
        for n in range(value_here * PIECES):
            early_copy(n).start()

    for n in range(value_here):
        block_ends(n, 1)
        local_terms(n)

    @pl.when(c > 0)
    def _():
        def early_turn(n, carried):
            for p in range(PIECES):
                at = n * PIECES + p
                early_copy(at).wait_recv()
                end = passed(n, p, 0, early_in[at])

                @pl.when(c < last)
                def _():
                    early_out[at] = end
                    early_copy(at).start()

                @pl.when(c == last)
                def _():
                    late_in[at] = end
                    late_out[at] = passed(n, p, 1, end)
                    late_copy(at).start()

            return carried

        lax.fori_loop(0, value_here, early_turn, 0)

    for n in range(value_here):
        finish(n, 0, whole_state(early_in, n))

    @pl.when((c > 0) & (c < last))
    def _():
        def late_turn(n, carried):
            for p in range(PIECES):
                at = n * PIECES + p
                late_copy(at).wait_recv()
                late_out[at] = passed(n, p, 1, late_in[at])
                late_copy(at).start()
            return carried

        lax.fori_loop(0, value_here, late_turn, 0)

    @pl.when(c == 0)
    def _():
        def last_turn(n, carried):
            for p in range(PIECES):
                late_copy(n * PIECES + p).wait_recv()
            finish(n, 1, whole_state(late_in, n))
            return carried

        lax.fori_loop(0, value_here, last_turn, 0)

    @pl.when(c > 0)
    def _():
        for n in range(value_here):
            finish(n, 1, whole_state(late_in, n))

    drain_sends()

    def drain(n, carry):
        @pl.when(c < last)
        def _():
            early_copy(n).wait_send()

        @pl.when(c > 0)
        def _():
            late_copy(n).wait_send()

        return carry

    lax.fori_loop(0, value_here * PIECES, drain, 0)


def four_blocks(
    c,
    half,
    value_here,
    early_copy,
    block_ends,
    local_terms,
    normed,
    finish,
    passed,
    whole_state,
    trans,
    offs,
    early_in,
    early_out,
    local_out,
    read,
    ra,
    a_out,
    c_in,
    c_out,
    v_in,
    v_out,
    comp_in,
    comp_out,
    fifth,
    ra_sem,
    c_sem,
    v_sem,
    comp_sem,
):
    low, high = pl.ds(0, half), pl.ds(half, half)
    late = slice(half, 2 * half)

    def to(device):
        return {"ctx": device}

    def read_six(n):
        return remote(read.at[n, high], ra.at[n, low], ra_sem, n, to(2))

    def read_seven(n):
        return remote(read.at[n, high], ra.at[n, high], ra_sem, value_here + n, to(1))

    def read_back(n):
        return remote(a_out.at[n], ra.at[n, high], ra_sem, value_here + n, to(2))

    def constant(n):
        return remote(c_out.at[n], c_in.at[n], c_sem, n, to(0))

    def joint(n):
        return remote(comp_out.at[n], comp_in.at[n], comp_sem, n, to(2))

    def rows_six(n):
        return remote(v_out.at[n, low], v_in.at[n], v_sem, n, to(1))

    def rows_seven(n):
        return remote(v_out.at[n, high], v_in.at[n], v_sem, value_here + n, to(0))

    def each(body):
        def turn(n, carried):
            body(n)
            return carried

        lax.fori_loop(0, value_here, turn, 0)

    def halves(n):
        return [n * PIECES + p for p in range(PIECES)]

    for n in range(value_here):
        block_ends(n, 0)
    for n in range(value_here):
        block_ends(n, 1)

    @pl.when(c == 3)
    def _():
        def join(n):
            fourth = trans[1, n]
            comp_out[n, 0] = dot(trans[0, n], fourth).astype(BF16)
            comp_out[n, 1] = (dot(offs[0, n].astype(BF16), fourth) + offs[1, n]).astype(BF16)
            joint(n).start()

        each(join)

    for n in range(value_here):
        local_terms(n)

    @pl.when(c == 0)
    def _():
        def send(n):
            for at in halves(n):
                early_copy(at).start()
            read_seven(n).start()

        each(send)
        for n in range(value_here):
            normed(n, 0, local_out[n, :half, :])

        def last(n):
            constant(n).wait_recv()
            rows_seven(n).wait_recv()
            normed(n, 1, local_out[n, late, :] + c_in[n].astype(F32) + v_in[n].astype(F32))

        each(last)

        def drain(n):
            for at in halves(n):
                early_copy(at).wait_send()
            read_seven(n).wait_send()

        each(drain)

    @pl.when(c == 1)
    def _():
        each(lambda n: read_six(n).start())

        def turn(n):
            for p, at in enumerate(halves(n)):
                early_copy(at).wait_recv()
                early_out[at] = passed(n, p, 0, early_in[at])
                early_copy(at).start()
            read_seven(n).wait_recv()
            seven = ra[n, late, :]
            a_out[n] = dot_nt(seven, trans[1, n]).astype(BF16)
            read_back(n).start()
            c_out[n] = dot_nt(seven, offs[1, n].astype(BF16)).astype(BF16)
            constant(n).start()

        each(turn)
        for n in range(value_here):
            finish(n, 0, whole_state(early_in, n))

        def last(n):
            rows_six(n).wait_recv()
            normed(n, 1, local_out[n, late, :] + v_in[n].astype(F32))

        each(last)

        def drain(n):
            read_six(n).wait_send()
            for at in halves(n):
                early_copy(at).wait_send()
            read_back(n).wait_send()
            constant(n).wait_send()

        each(drain)

    @pl.when(c == 2)
    def _():
        def turn(n):
            for p, at in enumerate(halves(n)):
                early_copy(at).wait_recv()
                early_out[at] = passed(n, p, 0, early_in[at])
                early_copy(at).start()
            joint(n).wait_recv()
            state = dot(whole_state(early_out, n), comp_in[n, 0]) + comp_in[n, 1].astype(F32)
            state = state.astype(BF16)
            fifth[n] = state
            read_six(n).wait_recv()
            read_back(n).wait_recv()
            reads = ra[n]
            pulled = dot_nt(reads, trans[1, n]).astype(BF16)
            plain = dot_nt(reads, offs[1, n].astype(BF16))
            v_out[n] = (dot_nt(pulled, state) + plain).astype(BF16)
            rows_seven(n).start()
            rows_six(n).start()

        each(turn)
        for n in range(value_here):
            finish(n, 0, whole_state(early_in, n))
            finish(n, 1, fifth[n])

        def drain(n):
            for at in halves(n):
                early_copy(at).wait_send()
            rows_six(n).wait_send()
            rows_seven(n).wait_send()

        each(drain)

    @pl.when(c == 3)
    def _():
        def turn(n):
            for p, at in enumerate(halves(n)):
                early_copy(at).wait_recv()
                early_out[at] = passed(n, p, 0, early_in[at])
            finish(n, 0, whole_state(early_in, n))
            finish(n, 1, whole_state(early_out, n))
            joint(n).wait_send()

        each(turn)


def settle(first_ref, second_ref, first_out, second_out, sems):
    copies = [
        pltpu.make_async_copy(first_ref, first_out, sems.at[0]),
        pltpu.make_async_copy(second_ref, second_out, sems.at[1]),
    ]
    for copy in copies:
        copy.start()
    for copy in copies:
        copy.wait()


def local(
    ctx_count,
    head_count,
    att_query,
    att_gate,
    att_kv,
    residual,
    out_weight,
    norm_gain,
    in_weight,
    beta_weight,
    log_decay,
    delta_gain,
):
    rows = att_query.shape[0]
    width = residual.shape[1]
    value_here = log_decay.shape[1]
    vmem = pl.BlockSpec(memory_space=pltpu.VMEM)
    hbm = pl.BlockSpec(memory_space=pl.ANY)
    heads_less = max(head_count - 1, 1)
    pair = pltpu.SemaphoreType.DMA
    direct = []
    if ctx_count == 4:
        block = (value_here, rows // 2, DK)
        square = (value_here, DK, DK)
        both = (value_here, 2, DK, DK)
        direct = [
            pltpu.VMEM((value_here, rows, DK), BF16),
            *[pltpu.VMEM(block, BF16)] * 4,
            pltpu.VMEM((value_here, rows, DK), BF16),
            pltpu.VMEM(both, BF16),
            pltpu.VMEM(both, BF16),
            pltpu.VMEM(square, BF16),
            pair((2, 2 * value_here)),
            pair((2, value_here)),
            pair((2, 2 * value_here)),
            pair((2, value_here)),
        ]
    outputs = pl.pallas_call(
        functools.partial(kernel, ctx_count, head_count),
        out_shape=(
            pltpu.VMEM((rows, width), BF16),
            pltpu.VMEM((rows, value_here * DV), BF16),
        ),
        in_specs=[hbm] * 10,
        out_specs=(vmem, vmem),
        scratch_shapes=[
            pltpu.VMEM(att_query.shape, BF16),
            pltpu.VMEM(att_gate.shape, BF16),
            pltpu.VMEM(residual.shape, BF16),
            pltpu.VMEM((1, norm_gain.shape[0]), F32),
            pltpu.VMEM(beta_weight.shape[::-1], BF16),
            pltpu.VMEM(log_decay.shape[::-1], F32),
            pltpu.VMEM((1, DV), F32),
            pltpu.VMEM((2, ctx_count * rows, HD), BF16),
            pltpu.VMEM(out_weight.shape, BF16),
            pltpu.VMEM(in_weight.shape, BF16),
            pltpu.VMEM(att_query.shape, BF16),
            pltpu.VMEM((head_count, rows, width), BF16),
            pltpu.VMEM((head_count, rows, width), BF16),
            pltpu.VMEM((heads_less, rows, width), BF16),
            pltpu.VMEM((heads_less, rows, width), BF16),
            pltpu.VMEM((2 * head_count, rows, width), BF16),
            pltpu.VMEM((rows, in_weight.shape[1]), F32),
            pltpu.VMEM((value_here, rows, rows), F32),
            pltpu.VMEM((2, value_here, DK, DK), BF16),
            pltpu.VMEM((2, value_here, DK, DV), F32),
            pltpu.VMEM((value_here * PIECES, DV // PIECES, DK), BF16),
            pltpu.VMEM((value_here * PIECES, DV // PIECES, DK), BF16),
            pltpu.VMEM((value_here * PIECES, DV // PIECES, DK), BF16),
            pltpu.VMEM((value_here * PIECES, DV // PIECES, DK), BF16),
            pltpu.VMEM((value_here, rows, DV), F32),
            pltpu.VMEM((value_here, rows, DK), BF16),
            pair((13,)),
            pair((2, 2 * ctx_count)),
            pair((2, 2 * ctx_count)),
            pair((2, head_count)),
            pair((2, head_count * CHUNKS)),
            pair((2, head_count * CHUNKS)),
            pair((2, head_count * CHUNKS)),
            pair((2, value_here * PIECES)),
            pair((2, value_here * PIECES)),
            *direct,
        ],
        compiler_params=pltpu.CompilerParams(collective_id=0, has_side_effects=True),
    )(
        att_query,
        att_gate,
        att_kv,
        residual,
        out_weight,
        norm_gain.reshape(1, -1),
        in_weight,
        beta_weight.T,
        log_decay.T,
        delta_gain.reshape(1, -1),
    )
    return pl.pallas_call(
        settle,
        out_shape=tuple(jax.ShapeDtypeStruct(x.shape, x.dtype) for x in outputs),
        in_specs=[vmem, vmem],
        out_specs=(hbm, hbm),
        scratch_shapes=[pair((2,))],
    )(*[pltpu.with_memory_space_constraint(x, pltpu.VMEM) for x in outputs])


def solution(mesh):
    return jax.shard_map(
        functools.partial(local, mesh.shape["ctx"], mesh.shape["head"]),
        mesh=mesh,
        in_specs=(
            P(("groups", "ctx"), ("head", "sub")),
            P(("groups", "ctx"), ("head", "sub")),
            P(("groups", "ctx"), None),
            P(("groups", "ctx"), ("head", "sub")),
            P(("head", "sub"), None),
            P(),
            P(None, ("head", "sub")),
            P(None, ("head", "sub")),
            P(("groups", "ctx"), ("head", "sub")),
            P(),
        ),
        out_specs=(P(("groups", "ctx"), ("head", "sub")), P(("groups", "ctx"), ("head", "sub"))),
        check_vma=False,
    )
```

```python
import functools

import jax
import jax.numpy as jnp
from jax import lax
from jax.experimental import pallas as pl
from jax.experimental.pallas import tpu as pltpu
from jax.sharding import PartitionSpec as P

HEADS = 16
KV_HEADS = 2
HD = 256
DK = 128
DV = 128
EPSILON = 1e-06
NEGATIVE = -1e30
CHUNKS = 2
PIECES = 2
STEPPED = 4
F32 = jnp.float32
BF16 = jnp.bfloat16
MESH = pl.DeviceIdType.MESH


def dot(a, b):
    return jnp.dot(a, b, preferred_element_type=F32)


def dot_nt(a, b):
    return lax.dot_general(a, b, (((1,), (1,)), ((), ())), preferred_element_type=F32)


def dot_tn(a, b):
    return lax.dot_general(a, b, (((0,), (0,)), ((), ())), preferred_element_type=F32)


def silu(x):
    return x * jax.nn.sigmoid(x)


def unit(x):
    return x * lax.rsqrt(jnp.sum(x * x, axis=-1, keepdims=True) + EPSILON)


def remote(src, dst, sems, index, device):
    return pltpu.make_async_remote_copy(
        src_ref=src,
        dst_ref=dst,
        send_sem=sems.at[0, index],
        recv_sem=sems.at[1, index],
        device_id=device,
        device_id_type=MESH,
    )


def kernel(
    ctx_count,
    head_count,
    query_hbm,
    gate_hbm,
    kv_hbm,
    res_hbm,
    ow_hbm,
    norm_gain_hbm,
    iw_hbm,
    bw_hbm,
    ld_hbm,
    delta_gain_hbm,
    new_res_ref,
    delta_ref,
    query_ref,
    gate_ref,
    res_ref,
    norm_gain_ref,
    bw_ref,
    ld_ref,
    delta_gain_ref,
    kv,
    ow,
    iw,
    att,
    rs_send,
    rs_recv,
    x_send,
    x_recv,
    hid,
    macc,
    grid_ref,
    trans,
    offs,
    early_in,
    late_in,
    early_out,
    late_out,
    local_out,
    read,
    load_sem,
    kv_sem,
    kvf_sem,
    rs_sem,
    x_sem,
    ag_sem,
    agf_sem,
    early_sem,
    late_sem,
    *direct,
):
    c = lax.axis_index("ctx")
    h = lax.axis_index("head")
    s = lax.axis_index("sub")
    rows = query_ref.shape[0]
    half = rows // 2
    heads_here = query_ref.shape[1] // HD
    shard = h * 2 + s
    width = res_ref.shape[1]
    partner = {"sub": 1 - s}
    kv_number = shard * heads_here // (HEADS // KV_HEADS)

    early_all = ctx_count * half

    def early_block(device):
        return pl.ds(pl.multiple_of(device * half, half), half)

    def late_block(device):
        return pl.ds(pl.multiple_of(early_all + device * half, half), half)

    loads = []
    for e, place in enumerate([early_block(c), late_block(c)]):
        for part in range(2):
            start = pl.multiple_of(kv_number * 2 * HD + part * HD, HD)
            loads.append(
                pltpu.make_async_copy(
                    kv_hbm.at[e * half : (e + 1) * half, pl.ds(start, HD)],
                    kv.at[part, place],
                    load_sem.at[9 + 2 * e + part],
                )
            )
    ow_load = pltpu.make_async_copy(ow_hbm, ow, load_sem.at[0])
    iw_load = pltpu.make_async_copy(iw_hbm, iw, load_sem.at[1])
    small = [
        pltpu.make_async_copy(source, target, load_sem.at[2 + i])
        for i, (source, target) in enumerate(
            [
                (ld_hbm, ld_ref),
                (query_hbm, query_ref),
                (gate_hbm, gate_ref),
                (res_hbm, res_ref),
                (norm_gain_hbm, norm_gain_ref),
                (bw_hbm, bw_ref),
                (delta_gain_hbm, delta_gain_ref),
            ]
        )
    ]
    barrier = pltpu.get_barrier_semaphore()
    for d in range(1, ctx_count):
        pl.semaphore_signal(
            barrier, inc=1, device_id={"ctx": lax.rem(c + d, ctx_count)}, device_id_type=MESH
        )
    for d in range(1, head_count):
        pl.semaphore_signal(
            barrier, inc=1, device_id={"head": lax.rem(h + d, head_count)}, device_id_type=MESH
        )
    pl.semaphore_signal(barrier, inc=1, device_id=partner, device_id_type=MESH)
    for load in loads + small:
        load.start()

    @pl.when(c == 0)
    def _():
        early_in[...] = jnp.zeros_like(early_in)

    for d in range(1, ctx_count):

        @pl.when(c >= d)
        def _():
            kv[:, late_block(c - d), :] = jnp.zeros((2, half, HD), BF16)

    pl.semaphore_wait(barrier, ctx_count + head_count - 1)

    sends = []
    for load in loads:
        load.wait()
    others = range(1, ctx_count)

    def late_kv(d):
        piece = kv.at[s, late_block(c)]
        return remote(piece, piece, kv_sem, ctx_count + d - 1, {"ctx": lax.max(c - d, 0)})

    def late_forward(d):
        piece = kv.at[s, late_block(lax.min(c + d, ctx_count - 1))]
        return remote(piece, piece, kvf_sem, ctx_count + d - 1, partner)

    gathers = []
    for d in others:
        piece = kv.at[s, early_block(c)]
        copy = remote(piece, piece, kv_sem, d - 1, {"ctx": lax.rem(c + d, ctx_count)})
        copy.start()
        gathers.append(copy)
    for d in others:

        @pl.when(c >= d)
        def _():
            late_kv(d).start()

    ow_load.start()
    row = lax.broadcasted_iota(jnp.int32, (rows, rows), 0)
    col = lax.broadcasted_iota(jnp.int32, (rows, rows), 1)
    same = (row < half) == (col < half)
    on_or_below = same & (row >= col)
    strictly = same & (row > col)
    eye = jnp.where(row == col, 1.0, 0.0)
    small[0].wait()
    lower = jnp.where(on_or_below, 1.0, 0.0)
    every = jnp.where(same, 1.0, 0.0)
    decays = ld_ref[...]

    def row_sums(picked):
        return lax.dot_general(
            decays,
            picked,
            (((1,), (1,)), ((), ())),
            precision=lax.Precision.HIGHEST,
            preferred_element_type=F32,
        )

    cum_row = row_sums(lower)
    sum_row = row_sums(every)
    cumulative = cum_row.T
    block_sum = sum_row.T
    growth = jnp.exp(cumulative)
    carry = jnp.exp(block_sum - cumulative)
    for n in range(ld_ref.shape[0]):
        gap = cumulative[:, n : n + 1] - cum_row[n : n + 1, :]
        grid_ref[n] = jnp.where(on_or_below, jnp.exp(jnp.where(on_or_below, gap, 0.0)), 0.0)

    forwards = []
    for d in others:
        gathers[d - 1].wait_recv()
        piece = kv.at[s, early_block(lax.rem(c - d + ctx_count, ctx_count))]
        copy = remote(piece, piece, kvf_sem, d - 1, partner)
        copy.start()
        forwards.append(copy)
    for d in others:

        @pl.when(c + d < ctx_count)
        def _():
            late_kv(d).wait_recv()
            late_forward(d).start()

    iw_load.start()
    for copy in forwards:
        copy.wait_recv()
    for d in others:

        @pl.when(c + d < ctx_count)
        def _():
            late_forward(d).wait_recv()

    sends += gathers + forwards

    for load in small[1:]:
        load.wait()

    total_rows = ctx_count * rows
    q_row = lax.broadcasted_iota(jnp.int32, (rows, total_rows), 0)
    k_row = lax.broadcasted_iota(jnp.int32, (rows, total_rows), 1)
    k_block = k_row >> (half.bit_length() - 1)
    last_block = 2 * ctx_count - 1
    q_pos = jnp.where(q_row < half, c, last_block - c) * half + (q_row & (half - 1))
    k_block = jnp.where(k_row < early_all, k_block, last_block + ctx_count - k_block)
    k_pos = k_block * half + (k_row & (half - 1))
    visible = q_pos >= k_pos
    keys = kv[0]
    values = kv[1]
    for n in range(heads_here):
        cols = slice(n * HD, (n + 1) * HD)
        scores = dot_nt(query_ref[:, cols], keys) * (HD**-0.5)
        scores = jnp.where(visible, scores, NEGATIVE)
        weights = jnp.exp(scores - jnp.max(scores, axis=1, keepdims=True))
        total = jnp.sum(weights, axis=1, keepdims=True)
        mixed = dot(weights.astype(BF16), values) / total
        att[:, cols] = (mixed * jax.nn.sigmoid(gate_ref[:, cols].astype(F32))).astype(BF16)

    ow_load.wait()
    attended = att[...]

    def out_slice(number):
        return dot(attended, ow[:, pl.ds(pl.multiple_of(number * width, width), width)])

    chunks = [slice(k * rows // CHUNKS, (k + 1) * rows // CHUNKS) for k in range(CHUNKS)]
    peers = [lax.rem(h + 1 + i, head_count) for i in range(head_count)]
    pair_copies = []
    for i in range(head_count):
        rs_send[i] = out_slice(peers[i] * 2 + 1 - s).astype(BF16)
        copy = remote(rs_send.at[i], rs_recv.at[i], rs_sem, i, partner)
        copy.start()
        pair_copies.append(copy)
    head_copies = []
    for i in range(head_count):
        part = out_slice(peers[i] * 2 + s)
        pair_copies[i].wait_recv()
        part = part + rs_recv[i].astype(F32)
        if i < head_count - 1:
            x_send[i] = part.astype(BF16)
            for k, lines in enumerate(chunks):
                copy = remote(
                    x_send.at[i, lines], x_recv.at[i, lines], x_sem, i * CHUNKS + k, {"head": peers[i]}
                )
                copy.start()
                head_copies.append(copy)
    part = part + res_ref[...].astype(F32)
    sends += pair_copies + head_copies
    to_heads = []
    to_partner = []
    for k, lines in enumerate(chunks):
        own = part[lines]
        for i in range(head_count - 1):
            head_copies[i * CHUNKS + k].wait_recv()
            own = own + x_recv[i, lines].astype(F32)
        own16 = own.astype(BF16)
        new_res_ref[lines, :] = own16
        hid[shard, lines] = own16
        mine = hid.at[shard, lines]
        for i in range(head_count - 1):
            copy = remote(mine, mine, ag_sem, i * CHUNKS + k, {"head": peers[i]})
            copy.start()
            to_heads.append(copy)
        copy = remote(mine, mine, agf_sem, (head_count - 1) * CHUNKS + k, partner)
        copy.start()
        to_partner.append(copy)
    iw_load.wait()

    def projected(r, start):
        cols = pl.ds(pl.multiple_of(r * width, width), width)
        piece = hid[r].astype(F32)
        scaled = (piece * norm_gain_ref[:, cols]).astype(BF16)
        term = dot(scaled, iw[cols, :])
        logits = dot_nt(bw_ref[:, cols], scaled)
        square = jnp.sum(piece * piece, axis=1, keepdims=True)
        if start is None:
            macc[...] = term
            return logits, square
        macc[...] += term
        return start[0] + logits, start[1] + square

    sources = [lax.rem(h - 1 - i + head_count, head_count) * 2 for i in range(head_count - 1)]
    parts = projected(shard, None)
    for k, lines in enumerate(chunks):
        for i in range(head_count - 1):
            to_heads[k * (head_count - 1) + i].wait_recv()
            piece = hid.at[sources[i] + s, lines]
            copy = remote(piece, piece, agf_sem, i * CHUNKS + k, partner)
            copy.start()
            to_partner.append(copy)
    for copy in to_partner[:CHUNKS]:
        copy.wait_recv()
    parts = projected(h * 2 + 1 - s, parts)
    for i in range(head_count - 1):
        parts = projected(sources[i] + s, parts)
    for copy in to_partner[CHUNKS:]:
        copy.wait_recv()
    for i in range(head_count - 1):
        parts = projected(sources[i] + 1 - s, parts)
    sends += to_heads + to_partner
    scale = lax.rsqrt(parts[1] / (2 * head_count * width) + EPSILON)
    group = 2 * DK + 2 * DV
    key_here = iw.shape[1] // group
    value_here = 2 * key_here

    beta = jax.nn.sigmoid(parts[0].T * scale)
    queries, grams, attends, values_of, keys_of = [], [], [], [], []
    for j in range(key_here):
        m = macc[:, j * group : (j + 1) * group] * scale
        q = unit(silu(m[:, :DK])) * DK**-0.5
        k = unit(silu(m[:, DK : 2 * DK]))
        v = silu(m[:, 2 * DK :])
        q16, k16 = q.astype(BF16), k.astype(BF16)
        queries.append(q)
        keys_of.append(k)
        values_of += [v[:, :DV], v[:, DV:]]
        grams.append(dot_nt(k16, k16))
        attends.append(dot_nt(q16, k16))
    systems, inverses, grids = [], [], []
    for n in range(value_here):
        grid = grid_ref[n]
        system = jnp.where(strictly, beta[:, n : n + 1] * grams[n // 2] * grid, 0.0)
        grids.append((attends[n // 2] * grid).astype(BF16))
        systems.append(system)
        inverses.append(eye - jnp.where((row >> 1) == (col >> 1), system, 0.0))
    level = 1
    while (1 << level) < half:
        mask = ((row >> (level + 1)) == (col >> (level + 1))) & ((row >> level) != (col >> level))
        halves = [inverse.astype(BF16) for inverse in inverses]
        firsts = [
            dot(jnp.where(mask, system, 0.0).astype(BF16), inverse).astype(BF16)
            for system, inverse in zip(systems, halves)
        ]
        inverses = [
            full - dot(inverse, product)
            for full, inverse, product in zip(inverses, halves, firsts)
        ]
        level += 1
    last = ctx_count - 1
    nxt = {"ctx": lax.min(c + 1, last)}
    prv = {"ctx": lax.max(c - 1, 0)}

    def early_copy(n):
        return remote(early_out.at[n], early_in.at[n], early_sem, n, nxt)

    def late_copy(n):
        return remote(late_out.at[n], late_in.at[n], late_sem, n, prv)

    solutions, carries = [], []
    for n in range(value_here):
        beta_n = beta[:, n : n + 1]
        right = jnp.concatenate(
            [beta_n * values_of[n], (beta_n * growth[:, n : n + 1]) * keys_of[n // 2]], axis=1
        )
        solutions.append(dot(inverses[n].astype(BF16), right.astype(BF16)).astype(BF16))
        carries.append((keys_of[n // 2] * carry[:, n : n + 1]).astype(BF16))

    def piece_rows(p):
        return slice(p * DV // PIECES, (p + 1) * DV // PIECES)

    def block_ends(n, b):
        lines = slice(b * half, (b + 1) * half)
        ends = dot_tn(solutions[n][lines], carries[n][lines])
        offs[b, n] = ends[:DV]
        whole = jnp.exp(block_sum[b * half : b * half + 1, n : n + 1])
        trans[b, n] = (whole * eye[:DK, :DK] - ends[DV:]).astype(BF16)
        if b == 0:
            for p in range(PIECES):
                early_out[n * PIECES + p] = ends[piece_rows(p)].astype(BF16)

    def drain_sends():
        for copy in sends:
            copy.wait_send()
        for d in others:

            @pl.when(c >= d)
            def _():
                late_kv(d).wait_send()

            @pl.when(c + d < ctx_count)
            def _():
                late_forward(d).wait_send()

    def local_terms(n):
        inner = dot(grids[n], solutions[n])
        local_out[n] = inner[:, :DV]
        read[n] = (growth[:, n : n + 1] * queries[n // 2] - inner[:, DV:]).astype(BF16)

    def normed(n, b, out):
        lines = slice(b * half, (b + 1) * half)
        mean = jnp.mean(out * out, axis=1, keepdims=True)
        out = out * lax.rsqrt(mean + EPSILON) * delta_gain_ref[...]
        if isinstance(n, int):
            delta_ref[lines, n * DV : (n + 1) * DV] = out.astype(BF16)
        else:
            delta_ref[lines, pl.ds(pl.multiple_of(n * DV, DV), DV)] = out.astype(BF16)

    def finish(n, b, state):
        lines = slice(b * half, (b + 1) * half)
        normed(n, b, local_out[n, lines, :] + dot_nt(read[n, lines, :], state))

    def passed(n, p, b, state):
        return (dot(state, trans[b, n]) + offs[b, n, piece_rows(p), :]).astype(BF16)

    def whole_state(ref, n):
        return jnp.concatenate([ref[n * PIECES + p] for p in range(PIECES)], axis=0)

    if ctx_count == 4:
        four_blocks(
            c,
            half,
            value_here,
            early_copy,
            late_copy,
            block_ends,
            local_terms,
            normed,
            finish,
            passed,
            whole_state,
            trans,
            offs,
            early_in,
            early_out,
            late_in,
            late_out,
            local_out,
            read,
            *direct,
        )
        drain_sends()
        return

    for n in range(value_here):
        block_ends(n, 0)

    @pl.when(c == 0)
    def _():
        for n in range(value_here * PIECES):
            early_copy(n).start()

    for n in range(value_here):
        block_ends(n, 1)
        local_terms(n)

    @pl.when(c > 0)
    def _():
        def early_turn(n, carried):
            for p in range(PIECES):
                at = n * PIECES + p
                early_copy(at).wait_recv()
                end = passed(n, p, 0, early_in[at])

                @pl.when(c < last)
                def _():
                    early_out[at] = end
                    early_copy(at).start()

                @pl.when(c == last)
                def _():
                    late_in[at] = end
                    late_out[at] = passed(n, p, 1, end)
                    late_copy(at).start()

            return carried

        lax.fori_loop(0, value_here, early_turn, 0)

    for n in range(value_here):
        finish(n, 0, whole_state(early_in, n))

    @pl.when((c > 0) & (c < last))
    def _():
        def late_turn(n, carried):
            for p in range(PIECES):
                at = n * PIECES + p
                late_copy(at).wait_recv()
                late_out[at] = passed(n, p, 1, late_in[at])
                late_copy(at).start()
            return carried

        lax.fori_loop(0, value_here, late_turn, 0)

    @pl.when(c == 0)
    def _():
        def last_turn(n, carried):
            for p in range(PIECES):
                late_copy(n * PIECES + p).wait_recv()
            finish(n, 1, whole_state(late_in, n))
            return carried

        lax.fori_loop(0, value_here, last_turn, 0)

    @pl.when(c > 0)
    def _():
        for n in range(value_here):
            finish(n, 1, whole_state(late_in, n))

    drain_sends()

    def drain(n, carry):
        @pl.when(c < last)
        def _():
            early_copy(n).wait_send()

        @pl.when(c > 0)
        def _():
            late_copy(n).wait_send()

        return carry

    lax.fori_loop(0, value_here * PIECES, drain, 0)


def four_blocks(
    c,
    half,
    value_here,
    early_copy,
    late_copy,
    block_ends,
    local_terms,
    normed,
    finish,
    passed,
    whole_state,
    trans,
    offs,
    early_in,
    early_out,
    late_in,
    late_out,
    local_out,
    read,
    ra,
    a_out,
    c_in,
    c_out,
    v_in,
    v_out,
    comp_in,
    comp_out,
    fifth,
    ra_sem,
    c_sem,
    v_sem,
    comp_sem,
):
    low, high = pl.ds(0, half), pl.ds(half, half)
    late = slice(half, 2 * half)

    def to(device):
        return {"ctx": device}

    def read_six(n):
        return remote(read.at[n, high], ra.at[n, low], ra_sem, n, to(2))

    def read_seven(n):
        return remote(read.at[n, high], ra.at[n, high], ra_sem, value_here + n, to(1))

    def read_back(n):
        return remote(a_out.at[n], ra.at[n, high], ra_sem, value_here + n, to(2))

    def constant(n):
        return remote(c_out.at[n], c_in.at[n], c_sem, n, to(0))

    def joint(n):
        return remote(comp_out.at[n], comp_in.at[n], comp_sem, n, to(2))

    def rows_six(n):
        return remote(v_out.at[n, low], v_in.at[n], v_sem, n, to(1))

    def rows_seven(n):
        return remote(v_out.at[n, high], v_in.at[n], v_sem, value_here + n, to(0))

    def each(body, first=0, end=value_here):
        def turn(n, carried):
            body(n)
            return carried

        lax.fori_loop(first, end, turn, 0)

    def stepped(body):
        each(body, 0, STEPPED)

    def pulled(body):
        each(body, STEPPED)

    def halves(n):
        return [n * PIECES + p for p in range(PIECES)]

    for n in range(value_here):
        block_ends(n, 0)

    def send(n):
        for at in halves(n):
            early_copy(at).start()

    @pl.when(c == 0)
    def _():
        for n in range(STEPPED):
            send(n)

    for n in range(value_here):
        block_ends(n, 1)

    @pl.when(c == 3)
    def _():
        def join(n):
            fourth = trans[1, n]
            comp_out[n, 0] = dot(trans[0, n], fourth).astype(BF16)
            comp_out[n, 1] = (dot(offs[0, n].astype(BF16), fourth) + offs[1, n]).astype(BF16)
            joint(n).start()

        each(join)

    for n in range(value_here):
        local_terms(n)

    @pl.when(c == 0)
    def _():
        def send_both(n):
            send(n)
            read_seven(n).start()

        pulled(send_both)
        for n in range(value_here):
            normed(n, 0, local_out[n, :half, :])

        def step(n):
            for at in halves(n):
                late_copy(at).wait_recv()
            finish(n, 1, whole_state(late_in, n))

        def last(n):
            constant(n).wait_recv()
            rows_seven(n).wait_recv()
            normed(n, 1, local_out[n, late, :] + c_in[n].astype(F32) + v_in[n].astype(F32))

        stepped(step)
        pulled(last)

        def drain(n):
            for at in halves(n):
                early_copy(at).wait_send()

        each(drain)
        pulled(lambda n: read_seven(n).wait_send())

    @pl.when(c == 1)
    def _():
        pulled(lambda n: read_six(n).start())

        def up(n):
            for p, at in enumerate(halves(n)):
                early_copy(at).wait_recv()
                early_out[at] = passed(n, p, 0, early_in[at])
                early_copy(at).start()

        def turn(n):
            up(n)
            read_seven(n).wait_recv()
            seven = ra[n, late, :]
            a_out[n] = dot_nt(seven, trans[1, n]).astype(BF16)
            read_back(n).start()
            c_out[n] = dot_nt(seven, offs[1, n].astype(BF16)).astype(BF16)
            constant(n).start()

        def down(n):
            for p, at in enumerate(halves(n)):
                late_copy(at).wait_recv()
                late_out[at] = passed(n, p, 1, late_in[at])
                late_copy(at).start()

        stepped(up)
        pulled(turn)
        stepped(down)
        for n in range(value_here):
            finish(n, 0, whole_state(early_in, n))
        for n in range(STEPPED):
            finish(n, 1, whole_state(late_in, n))

        def last(n):
            rows_six(n).wait_recv()
            normed(n, 1, local_out[n, late, :] + v_in[n].astype(F32))

        pulled(last)

        def drain(n):
            for at in halves(n):
                early_copy(at).wait_send()

        def drain_stepped(n):
            for at in halves(n):
                late_copy(at).wait_send()

        def drain_pulled(n):
            read_six(n).wait_send()
            read_back(n).wait_send()
            constant(n).wait_send()

        each(drain)
        stepped(drain_stepped)
        pulled(drain_pulled)

    @pl.when(c == 2)
    def _():
        def up(n):
            for p, at in enumerate(halves(n)):
                early_copy(at).wait_recv()
                early_out[at] = passed(n, p, 0, early_in[at])
                early_copy(at).start()
            joint(n).wait_recv()
            state = dot(whole_state(early_out, n), comp_in[n, 0]) + comp_in[n, 1].astype(F32)
            state = state.astype(BF16)
            fifth[n] = state
            return state

        def step(n):
            state = up(n)
            for p, at in enumerate(halves(n)):
                late_out[at] = passed(n, p, 1, state[p * DV // PIECES : (p + 1) * DV // PIECES])
                late_copy(at).start()

        def turn(n):
            state = up(n)
            read_six(n).wait_recv()
            read_back(n).wait_recv()
            reads = ra[n]
            back = dot_nt(reads, trans[1, n]).astype(BF16)
            plain = dot_nt(reads, offs[1, n].astype(BF16))
            v_out[n] = (dot_nt(back, state) + plain).astype(BF16)
            rows_seven(n).start()
            rows_six(n).start()

        stepped(step)
        pulled(turn)
        for n in range(value_here):
            finish(n, 0, whole_state(early_in, n))
            finish(n, 1, fifth[n])

        def drain(n):
            for at in halves(n):
                early_copy(at).wait_send()

        def drain_stepped(n):
            for at in halves(n):
                late_copy(at).wait_send()

        def drain_pulled(n):
            rows_six(n).wait_send()
            rows_seven(n).wait_send()

        each(drain)
        stepped(drain_stepped)
        pulled(drain_pulled)

    @pl.when(c == 3)
    def _():
        def turn(n):
            for p, at in enumerate(halves(n)):
                early_copy(at).wait_recv()
                early_out[at] = passed(n, p, 0, early_in[at])
            finish(n, 0, whole_state(early_in, n))
            finish(n, 1, whole_state(early_out, n))
            joint(n).wait_send()

        each(turn)


def settle(first_ref, second_ref, first_out, second_out, sems):
    copies = [
        pltpu.make_async_copy(first_ref, first_out, sems.at[0]),
        pltpu.make_async_copy(second_ref, second_out, sems.at[1]),
    ]
    for copy in copies:
        copy.start()
    for copy in copies:
        copy.wait()


def local(
    ctx_count,
    head_count,
    att_query,
    att_gate,
    att_kv,
    residual,
    out_weight,
    norm_gain,
    in_weight,
    beta_weight,
    log_decay,
    delta_gain,
):
    rows = att_query.shape[0]
    width = residual.shape[1]
    value_here = log_decay.shape[1]
    vmem = pl.BlockSpec(memory_space=pltpu.VMEM)
    hbm = pl.BlockSpec(memory_space=pl.ANY)
    heads_less = max(head_count - 1, 1)
    pair = pltpu.SemaphoreType.DMA
    direct = []
    if ctx_count == 4:
        block = (value_here, rows // 2, DK)
        square = (value_here, DK, DK)
        both = (value_here, 2, DK, DK)
        direct = [
            pltpu.VMEM((value_here, rows, DK), BF16),
            *[pltpu.VMEM(block, BF16)] * 4,
            pltpu.VMEM((value_here, rows, DK), BF16),
            pltpu.VMEM(both, BF16),
            pltpu.VMEM(both, BF16),
            pltpu.VMEM(square, BF16),
            pair((2, 2 * value_here)),
            pair((2, value_here)),
            pair((2, 2 * value_here)),
            pair((2, value_here)),
        ]
    outputs = pl.pallas_call(
        functools.partial(kernel, ctx_count, head_count),
        out_shape=(
            pltpu.VMEM((rows, width), BF16),
            pltpu.VMEM((rows, value_here * DV), BF16),
        ),
        in_specs=[hbm] * 10,
        out_specs=(vmem, vmem),
        scratch_shapes=[
            pltpu.VMEM(att_query.shape, BF16),
            pltpu.VMEM(att_gate.shape, BF16),
            pltpu.VMEM(residual.shape, BF16),
            pltpu.VMEM((1, norm_gain.shape[0]), F32),
            pltpu.VMEM(beta_weight.shape[::-1], BF16),
            pltpu.VMEM(log_decay.shape[::-1], F32),
            pltpu.VMEM((1, DV), F32),
            pltpu.VMEM((2, ctx_count * rows, HD), BF16),
            pltpu.VMEM(out_weight.shape, BF16),
            pltpu.VMEM(in_weight.shape, BF16),
            pltpu.VMEM(att_query.shape, BF16),
            pltpu.VMEM((head_count, rows, width), BF16),
            pltpu.VMEM((head_count, rows, width), BF16),
            pltpu.VMEM((heads_less, rows, width), BF16),
            pltpu.VMEM((heads_less, rows, width), BF16),
            pltpu.VMEM((2 * head_count, rows, width), BF16),
            pltpu.VMEM((rows, in_weight.shape[1]), F32),
            pltpu.VMEM((value_here, rows, rows), F32),
            pltpu.VMEM((2, value_here, DK, DK), BF16),
            pltpu.VMEM((2, value_here, DK, DV), F32),
            pltpu.VMEM((value_here * PIECES, DV // PIECES, DK), BF16),
            pltpu.VMEM((value_here * PIECES, DV // PIECES, DK), BF16),
            pltpu.VMEM((value_here * PIECES, DV // PIECES, DK), BF16),
            pltpu.VMEM((value_here * PIECES, DV // PIECES, DK), BF16),
            pltpu.VMEM((value_here, rows, DV), F32),
            pltpu.VMEM((value_here, rows, DK), BF16),
            pair((13,)),
            pair((2, 2 * ctx_count)),
            pair((2, 2 * ctx_count)),
            pair((2, head_count)),
            pair((2, head_count * CHUNKS)),
            pair((2, head_count * CHUNKS)),
            pair((2, head_count * CHUNKS)),
            pair((2, value_here * PIECES)),
            pair((2, value_here * PIECES)),
            *direct,
        ],
        compiler_params=pltpu.CompilerParams(collective_id=0, has_side_effects=True),
    )(
        att_query,
        att_gate,
        att_kv,
        residual,
        out_weight,
        norm_gain.reshape(1, -1),
        in_weight,
        beta_weight.T,
        log_decay.T,
        delta_gain.reshape(1, -1),
    )
    return pl.pallas_call(
        settle,
        out_shape=tuple(jax.ShapeDtypeStruct(x.shape, x.dtype) for x in outputs),
        in_specs=[vmem, vmem],
        out_specs=(hbm, hbm),
        scratch_shapes=[pair((2,))],
    )(*[pltpu.with_memory_space_constraint(x, pltpu.VMEM) for x in outputs])


def solution(mesh):
    return jax.shard_map(
        functools.partial(local, mesh.shape["ctx"], mesh.shape["head"]),
        mesh=mesh,
        in_specs=(
            P(("groups", "ctx"), ("head", "sub")),
            P(("groups", "ctx"), ("head", "sub")),
            P(("groups", "ctx"), None),
            P(("groups", "ctx"), ("head", "sub")),
            P(("head", "sub"), None),
            P(),
            P(None, ("head", "sub")),
            P(None, ("head", "sub")),
            P(("groups", "ctx"), ("head", "sub")),
            P(),
        ),
        out_specs=(P(("groups", "ctx"), ("head", "sub")), P(("groups", "ctx"), ("head", "sub"))),
        check_vma=False,
    )
```

```python
import functools

import jax
import jax.numpy as jnp
from jax import lax
from jax.experimental import pallas as pl
from jax.experimental.pallas import tpu as pltpu
from jax.sharding import PartitionSpec as P

HEADS = 16
KV_HEADS = 2
HD = 256
DK = 128
DV = 128
EPSILON = 1e-06
NEGATIVE = -1e30
CHUNKS = 2
PIECES = 2
STEPPED = 4
F32 = jnp.float32
BF16 = jnp.bfloat16
MESH = pl.DeviceIdType.MESH


def dot(a, b):
    return jnp.dot(a, b, preferred_element_type=F32)


def dot_nt(a, b):
    return lax.dot_general(a, b, (((1,), (1,)), ((), ())), preferred_element_type=F32)


def dot_tn(a, b):
    return lax.dot_general(a, b, (((0,), (0,)), ((), ())), preferred_element_type=F32)


def silu(x):
    return x * jax.nn.sigmoid(x)


def unit(x):
    return x * lax.rsqrt(jnp.sum(x * x, axis=-1, keepdims=True) + EPSILON)


def remote(src, dst, sems, index, device):
    return pltpu.make_async_remote_copy(
        src_ref=src,
        dst_ref=dst,
        send_sem=sems.at[0, index],
        recv_sem=sems.at[1, index],
        device_id=device,
        device_id_type=MESH,
    )


def kernel(
    ctx_count,
    head_count,
    query_hbm,
    gate_hbm,
    kv_hbm,
    res_hbm,
    ow_hbm,
    norm_gain_hbm,
    iw_hbm,
    bw_hbm,
    ld_hbm,
    delta_gain_hbm,
    new_res_ref,
    delta_ref,
    query_ref,
    gate_ref,
    res_ref,
    norm_gain_ref,
    bw_ref,
    ld_ref,
    delta_gain_ref,
    kv,
    ow,
    iw,
    att,
    rs_send,
    rs_recv,
    x_send,
    x_recv,
    hid,
    macc,
    grid_ref,
    trans,
    offs,
    early_in,
    late_in,
    early_out,
    late_out,
    local_out,
    read,
    load_sem,
    kv_sem,
    kvf_sem,
    rs_sem,
    x_sem,
    ag_sem,
    agf_sem,
    early_sem,
    late_sem,
    *direct,
):
    c = lax.axis_index("ctx")
    h = lax.axis_index("head")
    s = lax.axis_index("sub")
    rows = query_ref.shape[0]
    half = rows // 2
    heads_here = query_ref.shape[1] // HD
    shard = h * 2 + s
    width = res_ref.shape[1]
    partner = {"sub": 1 - s}
    kv_number = shard * heads_here // (HEADS // KV_HEADS)

    def lines_of(device, full):
        return pl.ds(pl.multiple_of(device * rows, rows), rows if full else half)

    loads = []
    for part in range(2):
        start = pl.multiple_of(kv_number * 2 * HD + part * HD, HD)
        loads.append(
            pltpu.make_async_copy(
                kv_hbm.at[:, pl.ds(start, HD)],
                kv.at[part, lines_of(c, True)],
                load_sem.at[9 + part],
            )
        )
    ow_load = pltpu.make_async_copy(ow_hbm, ow, load_sem.at[0])
    iw_load = pltpu.make_async_copy(iw_hbm, iw, load_sem.at[1])
    small = [
        pltpu.make_async_copy(source, target, load_sem.at[2 + i])
        for i, (source, target) in enumerate(
            [
                (ld_hbm, ld_ref),
                (query_hbm, query_ref),
                (gate_hbm, gate_ref),
                (res_hbm, res_ref),
                (norm_gain_hbm, norm_gain_ref),
                (bw_hbm, bw_ref),
                (delta_gain_hbm, delta_gain_ref),
            ]
        )
    ]
    barrier = pltpu.get_barrier_semaphore()
    for d in range(1, ctx_count):
        pl.semaphore_signal(
            barrier, inc=1, device_id={"ctx": lax.rem(c + d, ctx_count)}, device_id_type=MESH
        )
    for d in range(1, head_count):
        pl.semaphore_signal(
            barrier, inc=1, device_id={"head": lax.rem(h + d, head_count)}, device_id_type=MESH
        )
    pl.semaphore_signal(barrier, inc=1, device_id=partner, device_id_type=MESH)
    for load in loads + small:
        load.start()

    @pl.when(c == 0)
    def _():
        early_in[...] = jnp.zeros_like(early_in)

    for d in range(1, ctx_count):

        @pl.when(c >= d)
        def _():
            hidden_rows = pl.ds(pl.multiple_of((c - d) * rows + half, half), half)
            kv[:, hidden_rows, :] = jnp.zeros((2, half, HD), BF16)

    pl.semaphore_wait(barrier, ctx_count + head_count - 1)

    sends = []
    for load in loads:
        load.wait()
    others = range(1, ctx_count)

    def gather(d, full):
        piece = kv.at[s, lines_of(c, full)]
        return remote(piece, piece, kv_sem, d - 1, {"ctx": lax.rem(c + d, ctx_count)})

    def forward(d, full):
        piece = kv.at[s, lines_of(lax.rem(c - d + ctx_count, ctx_count), full)]
        return remote(piece, piece, kvf_sem, d - 1, partner)

    def sent(d, body):
        pl.when(c + d >= ctx_count)(lambda: body(True))
        pl.when(c + d < ctx_count)(lambda: body(False))

    def received(d, body):
        pl.when(c < d)(lambda: body(True))
        pl.when(c >= d)(lambda: body(False))

    for d in others:
        sent(d, lambda full: gather(d, full).start())

    ow_load.start()
    row = lax.broadcasted_iota(jnp.int32, (rows, rows), 0)
    col = lax.broadcasted_iota(jnp.int32, (rows, rows), 1)
    same = (row < half) == (col < half)
    on_or_below = same & (row >= col)
    strictly = same & (row > col)
    eye = jnp.where(row == col, 1.0, 0.0)
    small[0].wait()
    lower = jnp.where(on_or_below, 1.0, 0.0)
    every = jnp.where(same, 1.0, 0.0)
    decays = ld_ref[...]

    def row_sums(picked):
        return lax.dot_general(
            decays,
            picked,
            (((1,), (1,)), ((), ())),
            precision=lax.Precision.HIGHEST,
            preferred_element_type=F32,
        )

    cum_row = row_sums(lower)
    sum_row = row_sums(every)
    cumulative = cum_row.T
    block_sum = sum_row.T
    growth = jnp.exp(cumulative)
    carry = jnp.exp(block_sum - cumulative)
    for n in range(ld_ref.shape[0]):
        gap = cumulative[:, n : n + 1] - cum_row[n : n + 1, :]
        grid_ref[n] = jnp.where(on_or_below, jnp.exp(jnp.where(on_or_below, gap, 0.0)), 0.0)

    def pass_on(d, full):
        gather(d, full).wait_recv()
        forward(d, full).start()

    for d in others:
        received(d, lambda full: pass_on(d, full))
    iw_load.start()
    for d in others:
        received(d, lambda full: forward(d, full).wait_recv())

    for load in small[1:]:
        load.wait()

    total_rows = ctx_count * rows
    q_row = lax.broadcasted_iota(jnp.int32, (rows, total_rows), 0)
    k_row = lax.broadcasted_iota(jnp.int32, (rows, total_rows), 1)
    shift = rows.bit_length() - 1
    k_dev = k_row >> shift
    k_in = k_row & (rows - 1)
    last_block = 2 * ctx_count - 1
    q_pos = jnp.where(q_row < half, c, last_block - c) * half + (q_row & (half - 1))
    k_pos = jnp.where(k_in < half, k_dev, last_block - k_dev) * half + (k_in & (half - 1))
    visible = q_pos >= k_pos
    keys = kv[0]
    values = kv[1]
    for n in range(heads_here):
        cols = slice(n * HD, (n + 1) * HD)
        scores = dot_nt(query_ref[:, cols], keys) * (HD**-0.5)
        scores = jnp.where(visible, scores, NEGATIVE)
        weights = jnp.exp(scores - jnp.max(scores, axis=1, keepdims=True))
        total = jnp.sum(weights, axis=1, keepdims=True)
        mixed = dot(weights.astype(BF16), values) / total
        att[:, cols] = (mixed * jax.nn.sigmoid(gate_ref[:, cols].astype(F32))).astype(BF16)

    ow_load.wait()
    attended = att[...]

    def out_slice(number):
        return dot(attended, ow[:, pl.ds(pl.multiple_of(number * width, width), width)])

    chunks = [slice(k * rows // CHUNKS, (k + 1) * rows // CHUNKS) for k in range(CHUNKS)]
    peers = [lax.rem(h + 1 + i, head_count) for i in range(head_count)]
    pair_copies = []
    for i in range(head_count):
        rs_send[i] = out_slice(peers[i] * 2 + 1 - s).astype(BF16)
        copy = remote(rs_send.at[i], rs_recv.at[i], rs_sem, i, partner)
        copy.start()
        pair_copies.append(copy)
    head_copies = []
    for i in range(head_count):
        part = out_slice(peers[i] * 2 + s)
        pair_copies[i].wait_recv()
        part = part + rs_recv[i].astype(F32)
        if i < head_count - 1:
            x_send[i] = part.astype(BF16)
            for k, lines in enumerate(chunks):
                copy = remote(
                    x_send.at[i, lines], x_recv.at[i, lines], x_sem, i * CHUNKS + k, {"head": peers[i]}
                )
                copy.start()
                head_copies.append(copy)
    part = part + res_ref[...].astype(F32)
    sends += pair_copies + head_copies
    to_heads = []
    to_partner = []
    for k, lines in enumerate(chunks):
        own = part[lines]
        for i in range(head_count - 1):
            head_copies[i * CHUNKS + k].wait_recv()
            own = own + x_recv[i, lines].astype(F32)
        own16 = own.astype(BF16)
        new_res_ref[lines, :] = own16
        hid[shard, lines] = own16
        mine = hid.at[shard, lines]
        for i in range(head_count - 1):
            copy = remote(mine, mine, ag_sem, i * CHUNKS + k, {"head": peers[i]})
            copy.start()
            to_heads.append(copy)
        copy = remote(mine, mine, agf_sem, (head_count - 1) * CHUNKS + k, partner)
        copy.start()
        to_partner.append(copy)
    iw_load.wait()

    def projected(r, start):
        cols = pl.ds(pl.multiple_of(r * width, width), width)
        piece = hid[r].astype(F32)
        scaled = (piece * norm_gain_ref[:, cols]).astype(BF16)
        term = dot(scaled, iw[cols, :])
        logits = dot_nt(bw_ref[:, cols], scaled)
        square = jnp.sum(piece * piece, axis=1, keepdims=True)
        if start is None:
            macc[...] = term
            return logits, square
        macc[...] += term
        return start[0] + logits, start[1] + square

    sources = [lax.rem(h - 1 - i + head_count, head_count) * 2 for i in range(head_count - 1)]
    parts = projected(shard, None)
    for k, lines in enumerate(chunks):
        for i in range(head_count - 1):
            to_heads[k * (head_count - 1) + i].wait_recv()
            piece = hid.at[sources[i] + s, lines]
            copy = remote(piece, piece, agf_sem, i * CHUNKS + k, partner)
            copy.start()
            to_partner.append(copy)
    for copy in to_partner[:CHUNKS]:
        copy.wait_recv()
    parts = projected(h * 2 + 1 - s, parts)
    for i in range(head_count - 1):
        parts = projected(sources[i] + s, parts)
    for copy in to_partner[CHUNKS:]:
        copy.wait_recv()
    for i in range(head_count - 1):
        parts = projected(sources[i] + 1 - s, parts)
    sends += to_heads + to_partner
    scale = lax.rsqrt(parts[1] / (2 * head_count * width) + EPSILON)
    group = 2 * DK + 2 * DV
    key_here = iw.shape[1] // group
    value_here = 2 * key_here

    beta = jax.nn.sigmoid(parts[0].T * scale)
    queries, grams, attends, values_of, keys_of = [], [], [], [], []
    for j in range(key_here):
        m = macc[:, j * group : (j + 1) * group] * scale
        q = unit(silu(m[:, :DK])) * DK**-0.5
        k = unit(silu(m[:, DK : 2 * DK]))
        v = silu(m[:, 2 * DK :])
        q16, k16 = q.astype(BF16), k.astype(BF16)
        queries.append(q)
        keys_of.append(k)
        values_of += [v[:, :DV], v[:, DV:]]
        grams.append(dot_nt(k16, k16))
        attends.append(dot_nt(q16, k16))
    systems, inverses, grids = [], [], []
    for n in range(value_here):
        grid = grid_ref[n]
        system = jnp.where(strictly, beta[:, n : n + 1] * grams[n // 2] * grid, 0.0)
        grids.append((attends[n // 2] * grid).astype(BF16))
        systems.append(system)
        inverses.append(eye - jnp.where((row >> 1) == (col >> 1), system, 0.0))
    level = 1
    while (1 << level) < half:
        mask = ((row >> (level + 1)) == (col >> (level + 1))) & ((row >> level) != (col >> level))
        halves = [inverse.astype(BF16) for inverse in inverses]
        firsts = [
            dot(jnp.where(mask, system, 0.0).astype(BF16), inverse).astype(BF16)
            for system, inverse in zip(systems, halves)
        ]
        inverses = [
            full - dot(inverse, product)
            for full, inverse, product in zip(inverses, halves, firsts)
        ]
        level += 1
    last = ctx_count - 1
    nxt = {"ctx": lax.min(c + 1, last)}
    prv = {"ctx": lax.max(c - 1, 0)}

    def early_copy(n):
        return remote(early_out.at[n], early_in.at[n], early_sem, n, nxt)

    def late_copy(n):
        return remote(late_out.at[n], late_in.at[n], late_sem, n, prv)

    solutions, carries = [], []
    for n in range(value_here):
        beta_n = beta[:, n : n + 1]
        right = jnp.concatenate(
            [beta_n * values_of[n], (beta_n * growth[:, n : n + 1]) * keys_of[n // 2]], axis=1
        )
        solutions.append(dot(inverses[n].astype(BF16), right.astype(BF16)).astype(BF16))
        carries.append((keys_of[n // 2] * carry[:, n : n + 1]).astype(BF16))

    def piece_rows(p):
        return slice(p * DV // PIECES, (p + 1) * DV // PIECES)

    def block_ends(n, b):
        lines = slice(b * half, (b + 1) * half)
        ends = dot_tn(solutions[n][lines], carries[n][lines])
        offs[b, n] = ends[:DV]
        whole = jnp.exp(block_sum[b * half : b * half + 1, n : n + 1])
        trans[b, n] = (whole * eye[:DK, :DK] - ends[DV:]).astype(BF16)
        if b == 0:
            for p in range(PIECES):
                early_out[n * PIECES + p] = ends[piece_rows(p)].astype(BF16)

    def drain_sends():
        for copy in sends:
            copy.wait_send()
        for d in others:
            sent(d, lambda full: gather(d, full).wait_send())
            received(d, lambda full: forward(d, full).wait_send())

    def local_terms(n):
        inner = dot(grids[n], solutions[n])
        local_out[n] = inner[:, :DV]
        read[n] = (growth[:, n : n + 1] * queries[n // 2] - inner[:, DV:]).astype(BF16)

    def normed(n, b, out):
        lines = slice(b * half, (b + 1) * half)
        mean = jnp.mean(out * out, axis=1, keepdims=True)
        out = out * lax.rsqrt(mean + EPSILON) * delta_gain_ref[...]
        if isinstance(n, int):
            delta_ref[lines, n * DV : (n + 1) * DV] = out.astype(BF16)
        else:
            delta_ref[lines, pl.ds(pl.multiple_of(n * DV, DV), DV)] = out.astype(BF16)

    def finish(n, b, state):
        lines = slice(b * half, (b + 1) * half)
        normed(n, b, local_out[n, lines, :] + dot_nt(read[n, lines, :], state))

    def passed(n, p, b, state):
        return (dot(state, trans[b, n]) + offs[b, n, piece_rows(p), :]).astype(BF16)

    def whole_state(ref, n):
        return jnp.concatenate([ref[n * PIECES + p] for p in range(PIECES)], axis=0)

    if ctx_count == 4:
        four_blocks(
            c,
            half,
            value_here,
            early_copy,
            late_copy,
            block_ends,
            local_terms,
            normed,
            finish,
            passed,
            whole_state,
            trans,
            offs,
            early_in,
            early_out,
            late_in,
            late_out,
            local_out,
            read,
            *direct,
        )
        drain_sends()
        return

    for n in range(value_here):
        block_ends(n, 0)

    @pl.when(c == 0)
    def _():
        for n in range(value_here * PIECES):
            early_copy(n).start()

    for n in range(value_here):
        block_ends(n, 1)
        local_terms(n)

    @pl.when(c > 0)
    def _():
        def early_turn(n, carried):
            for p in range(PIECES):
                at = n * PIECES + p
                early_copy(at).wait_recv()
                end = passed(n, p, 0, early_in[at])

                @pl.when(c < last)
                def _():
                    early_out[at] = end
                    early_copy(at).start()

                @pl.when(c == last)
                def _():
                    late_in[at] = end
                    late_out[at] = passed(n, p, 1, end)
                    late_copy(at).start()

            return carried

        lax.fori_loop(0, value_here, early_turn, 0)

    for n in range(value_here):
        finish(n, 0, whole_state(early_in, n))

    @pl.when((c > 0) & (c < last))
    def _():
        def late_turn(n, carried):
            for p in range(PIECES):
                at = n * PIECES + p
                late_copy(at).wait_recv()
                late_out[at] = passed(n, p, 1, late_in[at])
                late_copy(at).start()
            return carried

        lax.fori_loop(0, value_here, late_turn, 0)

    @pl.when(c == 0)
    def _():
        def last_turn(n, carried):
            for p in range(PIECES):
                late_copy(n * PIECES + p).wait_recv()
            finish(n, 1, whole_state(late_in, n))
            return carried

        lax.fori_loop(0, value_here, last_turn, 0)

    @pl.when(c > 0)
    def _():
        for n in range(value_here):
            finish(n, 1, whole_state(late_in, n))

    drain_sends()

    def drain(n, carry):
        @pl.when(c < last)
        def _():
            early_copy(n).wait_send()

        @pl.when(c > 0)
        def _():
            late_copy(n).wait_send()

        return carry

    lax.fori_loop(0, value_here * PIECES, drain, 0)


def four_blocks(
    c,
    half,
    value_here,
    early_copy,
    late_copy,
    block_ends,
    local_terms,
    normed,
    finish,
    passed,
    whole_state,
    trans,
    offs,
    early_in,
    early_out,
    late_in,
    late_out,
    local_out,
    read,
    ra,
    a_out,
    c_in,
    c_out,
    v_in,
    v_out,
    comp_in,
    comp_out,
    fifth,
    ra_sem,
    c_sem,
    v_sem,
    comp_sem,
):
    low, high = pl.ds(0, half), pl.ds(half, half)
    late = slice(half, 2 * half)

    def to(device):
        return {"ctx": device}

    def read_six(n):
        return remote(read.at[n, high], ra.at[n, low], ra_sem, n, to(2))

    def read_seven(n):
        return remote(read.at[n, high], ra.at[n, high], ra_sem, value_here + n, to(1))

    def read_back(n):
        return remote(a_out.at[n], ra.at[n, high], ra_sem, value_here + n, to(2))

    def constant(n):
        return remote(c_out.at[n], c_in.at[n], c_sem, n, to(0))

    def joint(n):
        return remote(comp_out.at[n], comp_in.at[n], comp_sem, n, to(2))

    def rows_six(n):
        return remote(v_out.at[n, low], v_in.at[n], v_sem, n, to(1))

    def rows_seven(n):
        return remote(v_out.at[n, high], v_in.at[n], v_sem, value_here + n, to(0))

    def each(body, first=0, end=value_here):
        def turn(n, carried):
            body(n)
            return carried

        lax.fori_loop(first, end, turn, 0)

    def stepped(body):
        each(body, 0, STEPPED)

    def pulled(body):
        each(body, STEPPED)

    def halves(n):
        return [n * PIECES + p for p in range(PIECES)]

    for n in range(value_here):
        block_ends(n, 0)

    def send(n):
        for at in halves(n):
            early_copy(at).start()

    @pl.when(c == 0)
    def _():
        for n in range(STEPPED):
            send(n)

    for n in range(value_here):
        block_ends(n, 1)

    @pl.when(c == 3)
    def _():
        def join(n):
            fourth = trans[1, n]
            comp_out[n, 0] = dot(trans[0, n], fourth).astype(BF16)
            comp_out[n, 1] = (dot(offs[0, n].astype(BF16), fourth) + offs[1, n]).astype(BF16)
            joint(n).start()

        each(join)

    for n in range(value_here):
        local_terms(n)

    @pl.when(c == 0)
    def _():
        def send_both(n):
            send(n)
            read_seven(n).start()

        pulled(send_both)
        for n in range(value_here):
            normed(n, 0, local_out[n, :half, :])

        def step(n):
            for at in halves(n):
                late_copy(at).wait_recv()
            finish(n, 1, whole_state(late_in, n))

        def last(n):
            constant(n).wait_recv()
            rows_seven(n).wait_recv()
            normed(n, 1, local_out[n, late, :] + c_in[n].astype(F32) + v_in[n].astype(F32))

        stepped(step)
        pulled(last)

        def drain(n):
            for at in halves(n):
                early_copy(at).wait_send()

        each(drain)
        pulled(lambda n: read_seven(n).wait_send())

    @pl.when(c == 1)
    def _():
        pulled(lambda n: read_six(n).start())

        def up(n):
            for p, at in enumerate(halves(n)):
                early_copy(at).wait_recv()
                early_out[at] = passed(n, p, 0, early_in[at])
                early_copy(at).start()

        def turn(n):
            up(n)
            read_seven(n).wait_recv()
            seven = ra[n, late, :]
            a_out[n] = dot_nt(seven, trans[1, n]).astype(BF16)
            read_back(n).start()
            c_out[n] = dot_nt(seven, offs[1, n].astype(BF16)).astype(BF16)
            constant(n).start()

        def down(n):
            for p, at in enumerate(halves(n)):
                late_copy(at).wait_recv()
                late_out[at] = passed(n, p, 1, late_in[at])
                late_copy(at).start()

        stepped(up)
        pulled(turn)
        stepped(down)
        for n in range(value_here):
            finish(n, 0, whole_state(early_in, n))
        for n in range(STEPPED):
            finish(n, 1, whole_state(late_in, n))

        def last(n):
            rows_six(n).wait_recv()
            normed(n, 1, local_out[n, late, :] + v_in[n].astype(F32))

        pulled(last)

        def drain(n):
            for at in halves(n):
                early_copy(at).wait_send()

        def drain_stepped(n):
            for at in halves(n):
                late_copy(at).wait_send()

        def drain_pulled(n):
            read_six(n).wait_send()
            read_back(n).wait_send()
            constant(n).wait_send()

        each(drain)
        stepped(drain_stepped)
        pulled(drain_pulled)

    @pl.when(c == 2)
    def _():
        def up(n):
            for p, at in enumerate(halves(n)):
                early_copy(at).wait_recv()
                early_out[at] = passed(n, p, 0, early_in[at])
                early_copy(at).start()
            joint(n).wait_recv()
            state = dot(whole_state(early_out, n), comp_in[n, 0]) + comp_in[n, 1].astype(F32)
            state = state.astype(BF16)
            fifth[n] = state
            return state

        def step(n):
            state = up(n)
            for p, at in enumerate(halves(n)):
                late_out[at] = passed(n, p, 1, state[p * DV // PIECES : (p + 1) * DV // PIECES])
                late_copy(at).start()

        def turn(n):
            state = up(n)
            read_six(n).wait_recv()
            read_back(n).wait_recv()
            reads = ra[n]
            back = dot_nt(reads, trans[1, n]).astype(BF16)
            plain = dot_nt(reads, offs[1, n].astype(BF16))
            v_out[n] = (dot_nt(back, state) + plain).astype(BF16)
            rows_seven(n).start()
            rows_six(n).start()

        stepped(step)
        pulled(turn)
        for n in range(value_here):
            finish(n, 0, whole_state(early_in, n))
            finish(n, 1, fifth[n])

        def drain(n):
            for at in halves(n):
                early_copy(at).wait_send()

        def drain_stepped(n):
            for at in halves(n):
                late_copy(at).wait_send()

        def drain_pulled(n):
            rows_six(n).wait_send()
            rows_seven(n).wait_send()

        each(drain)
        stepped(drain_stepped)
        pulled(drain_pulled)

    @pl.when(c == 3)
    def _():
        def turn(n):
            for p, at in enumerate(halves(n)):
                early_copy(at).wait_recv()
                early_out[at] = passed(n, p, 0, early_in[at])
            finish(n, 0, whole_state(early_in, n))
            finish(n, 1, whole_state(early_out, n))
            joint(n).wait_send()

        each(turn)


def settle(first_ref, second_ref, first_out, second_out, sems):
    copies = [
        pltpu.make_async_copy(first_ref, first_out, sems.at[0]),
        pltpu.make_async_copy(second_ref, second_out, sems.at[1]),
    ]
    for copy in copies:
        copy.start()
    for copy in copies:
        copy.wait()


def local(
    ctx_count,
    head_count,
    att_query,
    att_gate,
    att_kv,
    residual,
    out_weight,
    norm_gain,
    in_weight,
    beta_weight,
    log_decay,
    delta_gain,
):
    rows = att_query.shape[0]
    width = residual.shape[1]
    value_here = log_decay.shape[1]
    vmem = pl.BlockSpec(memory_space=pltpu.VMEM)
    hbm = pl.BlockSpec(memory_space=pl.ANY)
    heads_less = max(head_count - 1, 1)
    pair = pltpu.SemaphoreType.DMA
    direct = []
    if ctx_count == 4:
        block = (value_here, rows // 2, DK)
        square = (value_here, DK, DK)
        both = (value_here, 2, DK, DK)
        direct = [
            pltpu.VMEM((value_here, rows, DK), BF16),
            *[pltpu.VMEM(block, BF16)] * 4,
            pltpu.VMEM((value_here, rows, DK), BF16),
            pltpu.VMEM(both, BF16),
            pltpu.VMEM(both, BF16),
            pltpu.VMEM(square, BF16),
            pair((2, 2 * value_here)),
            pair((2, value_here)),
            pair((2, 2 * value_here)),
            pair((2, value_here)),
        ]
    outputs = pl.pallas_call(
        functools.partial(kernel, ctx_count, head_count),
        out_shape=(
            pltpu.VMEM((rows, width), BF16),
            pltpu.VMEM((rows, value_here * DV), BF16),
        ),
        in_specs=[hbm] * 10,
        out_specs=(vmem, vmem),
        scratch_shapes=[
            pltpu.VMEM(att_query.shape, BF16),
            pltpu.VMEM(att_gate.shape, BF16),
            pltpu.VMEM(residual.shape, BF16),
            pltpu.VMEM((1, norm_gain.shape[0]), F32),
            pltpu.VMEM(beta_weight.shape[::-1], BF16),
            pltpu.VMEM(log_decay.shape[::-1], F32),
            pltpu.VMEM((1, DV), F32),
            pltpu.VMEM((2, ctx_count * rows, HD), BF16),
            pltpu.VMEM(out_weight.shape, BF16),
            pltpu.VMEM(in_weight.shape, BF16),
            pltpu.VMEM(att_query.shape, BF16),
            pltpu.VMEM((head_count, rows, width), BF16),
            pltpu.VMEM((head_count, rows, width), BF16),
            pltpu.VMEM((heads_less, rows, width), BF16),
            pltpu.VMEM((heads_less, rows, width), BF16),
            pltpu.VMEM((2 * head_count, rows, width), BF16),
            pltpu.VMEM((rows, in_weight.shape[1]), F32),
            pltpu.VMEM((value_here, rows, rows), F32),
            pltpu.VMEM((2, value_here, DK, DK), BF16),
            pltpu.VMEM((2, value_here, DK, DV), F32),
            pltpu.VMEM((value_here * PIECES, DV // PIECES, DK), BF16),
            pltpu.VMEM((value_here * PIECES, DV // PIECES, DK), BF16),
            pltpu.VMEM((value_here * PIECES, DV // PIECES, DK), BF16),
            pltpu.VMEM((value_here * PIECES, DV // PIECES, DK), BF16),
            pltpu.VMEM((value_here, rows, DV), F32),
            pltpu.VMEM((value_here, rows, DK), BF16),
            pair((11,)),
            pair((2, ctx_count)),
            pair((2, ctx_count)),
            pair((2, head_count)),
            pair((2, head_count * CHUNKS)),
            pair((2, head_count * CHUNKS)),
            pair((2, head_count * CHUNKS)),
            pair((2, value_here * PIECES)),
            pair((2, value_here * PIECES)),
            *direct,
        ],
        compiler_params=pltpu.CompilerParams(collective_id=0, has_side_effects=True),
    )(
        att_query,
        att_gate,
        att_kv,
        residual,
        out_weight,
        norm_gain.reshape(1, -1),
        in_weight,
        beta_weight.T,
        log_decay.T,
        delta_gain.reshape(1, -1),
    )
    return pl.pallas_call(
        settle,
        out_shape=tuple(jax.ShapeDtypeStruct(x.shape, x.dtype) for x in outputs),
        in_specs=[vmem, vmem],
        out_specs=(hbm, hbm),
        scratch_shapes=[pair((2,))],
    )(*[pltpu.with_memory_space_constraint(x, pltpu.VMEM) for x in outputs])


def solution(mesh):
    return jax.shard_map(
        functools.partial(local, mesh.shape["ctx"], mesh.shape["head"]),
        mesh=mesh,
        in_specs=(
            P(("groups", "ctx"), ("head", "sub")),
            P(("groups", "ctx"), ("head", "sub")),
            P(("groups", "ctx"), None),
            P(("groups", "ctx"), ("head", "sub")),
            P(("head", "sub"), None),
            P(),
            P(None, ("head", "sub")),
            P(None, ("head", "sub")),
            P(("groups", "ctx"), ("head", "sub")),
            P(),
        ),
        out_specs=(P(("groups", "ctx"), ("head", "sub")), P(("groups", "ctx"), ("head", "sub"))),
        check_vma=False,
    )
```

```python
import functools

import jax
import jax.numpy as jnp
from jax import lax
from jax.experimental import pallas as pl
from jax.experimental.pallas import tpu as pltpu
from jax.sharding import PartitionSpec as P

HEADS = 16
KV_HEADS = 2
HD = 256
DK = 128
DV = 128
EPSILON = 1e-06
NEGATIVE = -1e30
CHUNKS = 2
PIECES = 1
STEPPED = 4
F32 = jnp.float32
BF16 = jnp.bfloat16
MESH = pl.DeviceIdType.MESH


def dot(a, b):
    return jnp.dot(a, b, preferred_element_type=F32)


def dot_nt(a, b):
    return lax.dot_general(a, b, (((1,), (1,)), ((), ())), preferred_element_type=F32)


def dot_tn(a, b):
    return lax.dot_general(a, b, (((0,), (0,)), ((), ())), preferred_element_type=F32)


def silu(x):
    return x * jax.nn.sigmoid(x)


def unit(x):
    return x * lax.rsqrt(jnp.sum(x * x, axis=-1, keepdims=True) + EPSILON)


def remote(src, dst, sems, index, device):
    return pltpu.make_async_remote_copy(
        src_ref=src,
        dst_ref=dst,
        send_sem=sems.at[0, index],
        recv_sem=sems.at[1, index],
        device_id=device,
        device_id_type=MESH,
    )


def kernel(
    ctx_count,
    head_count,
    query_hbm,
    gate_hbm,
    kv_hbm,
    res_hbm,
    ow_hbm,
    norm_gain_hbm,
    iw_hbm,
    bw_hbm,
    ld_hbm,
    delta_gain_hbm,
    new_res_ref,
    delta_ref,
    query_ref,
    gate_ref,
    res_ref,
    norm_gain_ref,
    bw_ref,
    ld_ref,
    delta_gain_ref,
    kv,
    ow,
    iw,
    att,
    rs_send,
    rs_recv,
    x_send,
    x_recv,
    hid,
    macc,
    grid_ref,
    bias_ref,
    open_ref,
    trans,
    offs,
    early_in,
    late_in,
    early_out,
    late_out,
    local_out,
    read,
    load_sem,
    kv_sem,
    kvf_sem,
    rs_sem,
    x_sem,
    ag_sem,
    agf_sem,
    early_sem,
    late_sem,
    *direct,
):
    c = lax.axis_index("ctx")
    h = lax.axis_index("head")
    s = lax.axis_index("sub")
    rows = query_ref.shape[0]
    half = rows // 2
    heads_here = query_ref.shape[1] // HD
    shard = h * 2 + s
    width = res_ref.shape[1]
    partner = {"sub": 1 - s}
    kv_number = shard * heads_here // (HEADS // KV_HEADS)

    def lines_of(device, full):
        return pl.ds(pl.multiple_of(device * rows, rows), rows if full else half)

    loads = []
    for part in range(2):
        start = pl.multiple_of(kv_number * 2 * HD + part * HD, HD)
        loads.append(
            pltpu.make_async_copy(
                kv_hbm.at[:, pl.ds(start, HD)],
                kv.at[part, lines_of(c, True)],
                load_sem.at[9 + part],
            )
        )
    ow_load = pltpu.make_async_copy(ow_hbm, ow, load_sem.at[0])
    iw_load = pltpu.make_async_copy(iw_hbm, iw, load_sem.at[1])
    small = [
        pltpu.make_async_copy(source, target, load_sem.at[2 + i])
        for i, (source, target) in enumerate(
            [
                (ld_hbm, ld_ref),
                (query_hbm, query_ref),
                (gate_hbm, gate_ref),
                (res_hbm, res_ref),
                (norm_gain_hbm, norm_gain_ref),
                (bw_hbm, bw_ref),
                (delta_gain_hbm, delta_gain_ref),
            ]
        )
    ]
    barrier = pltpu.get_barrier_semaphore()
    for d in range(1, ctx_count):
        pl.semaphore_signal(
            barrier, inc=1, device_id={"ctx": lax.rem(c + d, ctx_count)}, device_id_type=MESH
        )
    for d in range(1, head_count):
        pl.semaphore_signal(
            barrier, inc=1, device_id={"head": lax.rem(h + d, head_count)}, device_id_type=MESH
        )
    pl.semaphore_signal(barrier, inc=1, device_id=partner, device_id_type=MESH)
    for load in loads + small:
        load.start()

    @pl.when(c == 0)
    def _():
        early_in[...] = jnp.zeros_like(early_in)

    for d in range(1, ctx_count):

        @pl.when(c >= d)
        def _():
            hidden_rows = pl.ds(pl.multiple_of((c - d) * rows + half, half), half)
            kv[:, hidden_rows, :] = jnp.zeros((2, half, HD), BF16)

    pl.semaphore_wait(barrier, ctx_count + head_count - 1)

    sends = []
    for load in loads:
        load.wait()
    others = range(1, ctx_count)

    def gather(d, full):
        piece = kv.at[s, lines_of(c, full)]
        return remote(piece, piece, kv_sem, d - 1, {"ctx": lax.rem(c + d, ctx_count)})

    def forward(d, full):
        piece = kv.at[s, lines_of(lax.rem(c - d + ctx_count, ctx_count), full)]
        return remote(piece, piece, kvf_sem, d - 1, partner)

    def sent(d, body):
        pl.when(c + d >= ctx_count)(lambda: body(True))
        pl.when(c + d < ctx_count)(lambda: body(False))

    def received(d, body):
        pl.when(c < d)(lambda: body(True))
        pl.when(c >= d)(lambda: body(False))

    for d in others:
        sent(d, lambda full: gather(d, full).start())

    ow_load.start()
    row = lax.broadcasted_iota(jnp.int32, (rows, rows), 0)
    col = lax.broadcasted_iota(jnp.int32, (rows, rows), 1)
    same = (row < half) == (col < half)
    on_or_below = same & (row >= col)
    strictly = same & (row > col)
    eye = jnp.where(row == col, 1.0, 0.0)
    small[0].wait()
    lower = jnp.where(on_or_below, 1.0, 0.0)
    every = jnp.where(same, 1.0, 0.0)
    decays = ld_ref[...]

    def row_sums(picked):
        return lax.dot_general(
            decays,
            picked,
            (((1,), (1,)), ((), ())),
            precision=lax.Precision.HIGHEST,
            preferred_element_type=F32,
        )

    cum_row = row_sums(lower)
    sum_row = row_sums(every)
    cumulative = cum_row.T
    block_sum = sum_row.T
    growth = jnp.exp(cumulative)
    carry = jnp.exp(block_sum - cumulative)
    for n in range(ld_ref.shape[0]):
        gap = cumulative[:, n : n + 1] - cum_row[n : n + 1, :]
        grid_ref[n] = jnp.where(on_or_below, jnp.exp(jnp.where(on_or_below, gap, 0.0)), 0.0)

    for load in small[1:]:
        load.wait()
    total_rows = ctx_count * rows
    q_row = lax.broadcasted_iota(jnp.int32, (rows, total_rows), 0)
    k_row = lax.broadcasted_iota(jnp.int32, (rows, total_rows), 1)
    shift = rows.bit_length() - 1
    k_dev = k_row >> shift
    k_in = k_row & (rows - 1)
    last_block = 2 * ctx_count - 1
    q_pos = jnp.where(q_row < half, c, last_block - c) * half + (q_row & (half - 1))
    k_pos = jnp.where(k_in < half, k_dev, last_block - k_dev) * half + (k_in & (half - 1))
    bias_ref[...] = jnp.where(q_pos >= k_pos, 0.0, NEGATIVE)
    open_ref[...] = jax.nn.sigmoid(gate_ref[...].astype(F32))

    def pass_on(d, full):
        gather(d, full).wait_recv()
        forward(d, full).start()

    for d in others:
        pl.when(c + d < ctx_count)(lambda: pass_on(ctx_count - d, True))
        pl.when(c >= d)(lambda: pass_on(d, False))
    iw_load.start()
    for d in others:
        received(d, lambda full: forward(d, full).wait_recv())

    keys = kv[0]
    values = kv[1]
    for n in range(heads_here):
        cols = slice(n * HD, (n + 1) * HD)
        scores = dot_nt(query_ref[:, cols], keys) * (HD**-0.5) + bias_ref[...]
        weights = jnp.exp(scores - jnp.max(scores, axis=1, keepdims=True))
        total = jnp.sum(weights, axis=1, keepdims=True)
        mixed = dot(weights.astype(BF16), values) * (1.0 / total)
        att[:, cols] = (mixed * open_ref[:, cols]).astype(BF16)

    ow_load.wait()
    attended = att[...]

    def out_slice(number):
        return dot(attended, ow[:, pl.ds(pl.multiple_of(number * width, width), width)])

    chunks = [slice(k * rows // CHUNKS, (k + 1) * rows // CHUNKS) for k in range(CHUNKS)]
    peers = [lax.rem(h + 1 + i, head_count) for i in range(head_count)]
    pair_copies = []
    for i in range(head_count):
        rs_send[i] = out_slice(peers[i] * 2 + 1 - s).astype(BF16)
        copy = remote(rs_send.at[i], rs_recv.at[i], rs_sem, i, partner)
        copy.start()
        pair_copies.append(copy)
    head_copies = []
    for i in range(head_count):
        part = out_slice(peers[i] * 2 + s)
        pair_copies[i].wait_recv()
        part = part + rs_recv[i].astype(F32)
        if i < head_count - 1:
            x_send[i] = part.astype(BF16)
            for k, lines in enumerate(chunks):
                copy = remote(
                    x_send.at[i, lines], x_recv.at[i, lines], x_sem, i * CHUNKS + k, {"head": peers[i]}
                )
                copy.start()
                head_copies.append(copy)
    part = part + res_ref[...].astype(F32)
    sends += pair_copies + head_copies
    to_heads = []
    to_partner = []
    for k, lines in enumerate(chunks):
        own = part[lines]
        for i in range(head_count - 1):
            head_copies[i * CHUNKS + k].wait_recv()
            own = own + x_recv[i, lines].astype(F32)
        own16 = own.astype(BF16)
        new_res_ref[lines, :] = own16
        hid[shard, lines] = own16
        mine = hid.at[shard, lines]
        for i in range(head_count - 1):
            copy = remote(mine, mine, ag_sem, i * CHUNKS + k, {"head": peers[i]})
            copy.start()
            to_heads.append(copy)
        copy = remote(mine, mine, agf_sem, (head_count - 1) * CHUNKS + k, partner)
        copy.start()
        to_partner.append(copy)
    iw_load.wait()

    def projected(r, start):
        cols = pl.ds(pl.multiple_of(r * width, width), width)
        piece = hid[r].astype(F32)
        scaled = (piece * norm_gain_ref[:, cols]).astype(BF16)
        term = dot(scaled, iw[cols, :])
        logits = dot_nt(bw_ref[:, cols], scaled)
        square = jnp.sum(piece * piece, axis=1, keepdims=True)
        if start is None:
            macc[...] = term
            return logits, square
        macc[...] += term
        return start[0] + logits, start[1] + square

    sources = [lax.rem(h - 1 - i + head_count, head_count) * 2 for i in range(head_count - 1)]
    parts = projected(shard, None)
    for k, lines in enumerate(chunks):
        for i in range(head_count - 1):
            to_heads[k * (head_count - 1) + i].wait_recv()
            piece = hid.at[sources[i] + s, lines]
            copy = remote(piece, piece, agf_sem, i * CHUNKS + k, partner)
            copy.start()
            to_partner.append(copy)
    for copy in to_partner[:CHUNKS]:
        copy.wait_recv()
    parts = projected(h * 2 + 1 - s, parts)
    for i in range(head_count - 1):
        parts = projected(sources[i] + s, parts)
    for copy in to_partner[CHUNKS:]:
        copy.wait_recv()
    for i in range(head_count - 1):
        parts = projected(sources[i] + 1 - s, parts)
    sends += to_heads + to_partner
    scale = lax.rsqrt(parts[1] / (2 * head_count * width) + EPSILON)
    group = 2 * DK + 2 * DV
    key_here = iw.shape[1] // group
    value_here = 2 * key_here

    beta = jax.nn.sigmoid(parts[0].T * scale)
    queries, grams, attends, values_of, keys_of = [], [], [], [], []
    for j in range(key_here):
        m = macc[:, j * group : (j + 1) * group] * scale
        q = unit(silu(m[:, :DK])) * DK**-0.5
        k = unit(silu(m[:, DK : 2 * DK]))
        v = silu(m[:, 2 * DK :])
        q16, k16 = q.astype(BF16), k.astype(BF16)
        queries.append(q)
        keys_of.append(k)
        values_of += [v[:, :DV], v[:, DV:]]
        grams.append(dot_nt(k16, k16))
        attends.append(dot_nt(q16, k16))
    systems, inverses, grids = [], [], []
    for n in range(value_here):
        grid = grid_ref[n]
        system = jnp.where(strictly, beta[:, n : n + 1] * grams[n // 2] * grid, 0.0)
        grids.append((attends[n // 2] * grid).astype(BF16))
        systems.append(system)
        inverses.append(eye - jnp.where((row >> 1) == (col >> 1), system, 0.0))
    level = 1
    while (1 << level) < half:
        mask = ((row >> (level + 1)) == (col >> (level + 1))) & ((row >> level) != (col >> level))
        halves = [inverse.astype(BF16) for inverse in inverses]
        firsts = [
            dot(jnp.where(mask, system, 0.0).astype(BF16), inverse).astype(BF16)
            for system, inverse in zip(systems, halves)
        ]
        inverses = [
            full - dot(inverse, product)
            for full, inverse, product in zip(inverses, halves, firsts)
        ]
        level += 1
    last = ctx_count - 1
    nxt = {"ctx": lax.min(c + 1, last)}
    prv = {"ctx": lax.max(c - 1, 0)}

    def early_copy(n):
        return remote(early_out.at[n], early_in.at[n], early_sem, n, nxt)

    def late_copy(n):
        return remote(late_out.at[n], late_in.at[n], late_sem, n, prv)

    solutions, carries = {}, {}

    def solve(n):
        beta_n = beta[:, n : n + 1]
        right = jnp.concatenate(
            [beta_n * values_of[n], (beta_n * growth[:, n : n + 1]) * keys_of[n // 2]], axis=1
        )
        solutions[n] = dot(inverses[n].astype(BF16), right.astype(BF16)).astype(BF16)
        carries[n] = (keys_of[n // 2] * carry[:, n : n + 1]).astype(BF16)

    def piece_rows(p):
        return slice(p * DV // PIECES, (p + 1) * DV // PIECES)

    def block_ends(n, b):
        lines = slice(b * half, (b + 1) * half)
        ends = dot_tn(solutions[n][lines], carries[n][lines])
        offs[b, n] = ends[:DV]
        whole = jnp.exp(block_sum[b * half : b * half + 1, n : n + 1])
        trans[b, n] = (whole * eye[:DK, :DK] - ends[DV:]).astype(BF16)
        if b == 0:
            for p in range(PIECES):
                early_out[n * PIECES + p] = ends[piece_rows(p)].astype(BF16)

    def drain_sends():
        for copy in sends:
            copy.wait_send()
        for d in others:
            sent(d, lambda full: gather(d, full).wait_send())
            received(d, lambda full: forward(d, full).wait_send())

    def local_terms(n):
        inner = dot(grids[n], solutions[n])
        local_out[n] = inner[:, :DV]
        read[n] = (growth[:, n : n + 1] * queries[n // 2] - inner[:, DV:]).astype(BF16)

    def normed(n, b, out):
        lines = slice(b * half, (b + 1) * half)
        mean = jnp.mean(out * out, axis=1, keepdims=True)
        out = out * lax.rsqrt(mean + EPSILON) * delta_gain_ref[...]
        if isinstance(n, int):
            delta_ref[lines, n * DV : (n + 1) * DV] = out.astype(BF16)
        else:
            delta_ref[lines, pl.ds(pl.multiple_of(n * DV, DV), DV)] = out.astype(BF16)

    def finish(n, b, state):
        lines = slice(b * half, (b + 1) * half)
        normed(n, b, local_out[n, lines, :] + dot_nt(read[n, lines, :], state))

    def passed(n, p, b, state):
        return (dot(state, trans[b, n]) + offs[b, n, piece_rows(p), :]).astype(BF16)

    def whole_state(ref, n):
        return jnp.concatenate([ref[n * PIECES + p] for p in range(PIECES)], axis=0)

    if ctx_count == 4:
        four_blocks(
            c,
            half,
            value_here,
            early_copy,
            late_copy,
            solve,
            block_ends,
            local_terms,
            normed,
            finish,
            passed,
            whole_state,
            trans,
            offs,
            early_in,
            early_out,
            late_in,
            late_out,
            local_out,
            read,
            drain_sends,
            *direct,
        )
        return

    for n in range(value_here):
        solve(n)
    for n in range(value_here):
        block_ends(n, 0)

    @pl.when(c == 0)
    def _():
        for n in range(value_here * PIECES):
            early_copy(n).start()

    for n in range(value_here):
        block_ends(n, 1)
        local_terms(n)

    @pl.when(c > 0)
    def _():
        def early_turn(n, carried):
            for p in range(PIECES):
                at = n * PIECES + p
                early_copy(at).wait_recv()
                end = passed(n, p, 0, early_in[at])

                @pl.when(c < last)
                def _():
                    early_out[at] = end
                    early_copy(at).start()

                @pl.when(c == last)
                def _():
                    late_in[at] = end
                    late_out[at] = passed(n, p, 1, end)
                    late_copy(at).start()

            return carried

        lax.fori_loop(0, value_here, early_turn, 0)

    for n in range(value_here):
        finish(n, 0, whole_state(early_in, n))

    @pl.when((c > 0) & (c < last))
    def _():
        def late_turn(n, carried):
            for p in range(PIECES):
                at = n * PIECES + p
                late_copy(at).wait_recv()
                late_out[at] = passed(n, p, 1, late_in[at])
                late_copy(at).start()
            return carried

        lax.fori_loop(0, value_here, late_turn, 0)

    @pl.when(c == 0)
    def _():
        def last_turn(n, carried):
            for p in range(PIECES):
                late_copy(n * PIECES + p).wait_recv()
            finish(n, 1, whole_state(late_in, n))
            return carried

        lax.fori_loop(0, value_here, last_turn, 0)

    @pl.when(c > 0)
    def _():
        for n in range(value_here):
            finish(n, 1, whole_state(late_in, n))

    drain_sends()

    def drain(n, carry):
        @pl.when(c < last)
        def _():
            early_copy(n).wait_send()

        @pl.when(c > 0)
        def _():
            late_copy(n).wait_send()

        return carry

    lax.fori_loop(0, value_here * PIECES, drain, 0)


def four_blocks(
    c,
    half,
    value_here,
    early_copy,
    late_copy,
    solve,
    block_ends,
    local_terms,
    normed,
    finish,
    passed,
    whole_state,
    trans,
    offs,
    early_in,
    early_out,
    late_in,
    late_out,
    local_out,
    read,
    drain_sends,
    ra,
    a_out,
    c_in,
    c_out,
    v_in,
    v_out,
    comp_in,
    comp_out,
    fifth,
    ra_sem,
    c_sem,
    v_sem,
    comp_sem,
):
    low, high = pl.ds(0, half), pl.ds(half, half)
    late = slice(half, 2 * half)

    def to(device):
        return {"ctx": device}

    def read_six(n):
        return remote(read.at[n, high], ra.at[n, low], ra_sem, n, to(2))

    def read_seven(n):
        return remote(read.at[n, high], ra.at[n, high], ra_sem, value_here + n, to(1))

    def read_back(n):
        return remote(a_out.at[n], ra.at[n, high], ra_sem, value_here + n, to(2))

    def constant(n):
        return remote(c_out.at[n], c_in.at[n], c_sem, n, to(0))

    def joint(n):
        return remote(comp_out.at[n], comp_in.at[n], comp_sem, n, to(2))

    def rows_six(n):
        return remote(v_out.at[n, low], v_in.at[n], v_sem, n, to(1))

    def rows_seven(n):
        return remote(v_out.at[n, high], v_in.at[n], v_sem, value_here + n, to(0))

    def each(body, first=0, end=value_here):
        def turn(n, carried):
            body(n)
            return carried

        lax.fori_loop(first, end, turn, 0)

    def stepped(body):
        each(body, 0, STEPPED)

    def pulled(body):
        each(body, STEPPED)

    def halves(n):
        return [n * PIECES + p for p in range(PIECES)]

    def send(n):
        for at in halves(n):
            early_copy(at).start()

    def join(n):
        fourth = trans[1, n]
        comp_out[n, 0] = dot(trans[0, n], fourth).astype(BF16)
        comp_out[n, 1] = (dot(offs[0, n].astype(BF16), fourth) + offs[1, n]).astype(BF16)
        joint(n).start()

    for n in range(STEPPED):
        solve(n)
        block_ends(n, 0)

    @pl.when(c == 0)
    def _():
        for n in range(STEPPED):
            send(n)

    for n in range(STEPPED):
        block_ends(n, 1)

    @pl.when(c == 3)
    def _():
        stepped(join)

    for n in range(STEPPED, value_here):
        solve(n)
        block_ends(n, 0)
        block_ends(n, 1)

    @pl.when(c == 3)
    def _():
        pulled(join)

    for n in range(value_here):
        local_terms(n)

    @pl.when(c == 0)
    def _():
        def send_both(n):
            send(n)
            read_seven(n).start()

        pulled(send_both)

    @pl.when(c == 1)
    def _():
        pulled(lambda n: read_six(n).start())

    drain_sends()

    @pl.when(c == 0)
    def _():
        for n in range(value_here):
            normed(n, 0, local_out[n, :half, :])

        def step(n):
            for at in halves(n):
                late_copy(at).wait_recv()
            finish(n, 1, whole_state(late_in, n))

        def last(n):
            constant(n).wait_recv()
            rows_seven(n).wait_recv()
            normed(n, 1, local_out[n, late, :] + c_in[n].astype(F32) + v_in[n].astype(F32))

        def drain(n):
            for at in halves(n):
                early_copy(at).wait_send()

        stepped(step)
        each(drain)
        pulled(lambda n: read_seven(n).wait_send())
        pulled(last)

    @pl.when(c == 1)
    def _():
        def up(n):
            for p, at in enumerate(halves(n)):
                early_copy(at).wait_recv()
                early_out[at] = passed(n, p, 0, early_in[at])
                early_copy(at).start()

        def turn(n):
            up(n)
            read_seven(n).wait_recv()
            seven = ra[n, late, :]
            a_out[n] = dot_nt(seven, trans[1, n]).astype(BF16)
            read_back(n).start()
            c_out[n] = dot_nt(seven, offs[1, n].astype(BF16)).astype(BF16)
            constant(n).start()

        def down(n):
            for p, at in enumerate(halves(n)):
                late_copy(at).wait_recv()
                late_out[at] = passed(n, p, 1, late_in[at])
                late_copy(at).start()

        stepped(up)
        pulled(turn)
        stepped(down)
        for n in range(value_here):
            finish(n, 0, whole_state(early_in, n))
        for n in range(STEPPED):
            finish(n, 1, whole_state(late_in, n))

        def last(n):
            rows_six(n).wait_recv()
            normed(n, 1, local_out[n, late, :] + v_in[n].astype(F32))

        pulled(last)

        def drain(n):
            for at in halves(n):
                early_copy(at).wait_send()

        def drain_stepped(n):
            for at in halves(n):
                late_copy(at).wait_send()

        def drain_pulled(n):
            read_six(n).wait_send()
            read_back(n).wait_send()
            constant(n).wait_send()

        each(drain)
        stepped(drain_stepped)
        pulled(drain_pulled)

    @pl.when(c == 2)
    def _():
        def up(n):
            for p, at in enumerate(halves(n)):
                early_copy(at).wait_recv()
                early_out[at] = passed(n, p, 0, early_in[at])
                early_copy(at).start()
            joint(n).wait_recv()
            state = dot(whole_state(early_out, n), comp_in[n, 0]) + comp_in[n, 1].astype(F32)
            state = state.astype(BF16)
            fifth[n] = state
            return state

        def step(n):
            state = up(n)
            for p, at in enumerate(halves(n)):
                late_out[at] = passed(n, p, 1, state[p * DV // PIECES : (p + 1) * DV // PIECES])
                late_copy(at).start()

        def turn(n):
            state = up(n)
            read_six(n).wait_recv()
            read_back(n).wait_recv()
            reads = ra[n]
            back = dot_nt(reads, trans[1, n]).astype(BF16)
            plain = dot_nt(reads, offs[1, n].astype(BF16))
            v_out[n] = (dot_nt(back, state) + plain).astype(BF16)
            rows_seven(n).start()
            rows_six(n).start()

        stepped(step)
        pulled(turn)
        for n in range(value_here):
            finish(n, 0, whole_state(early_in, n))
            finish(n, 1, fifth[n])

        def drain(n):
            for at in halves(n):
                early_copy(at).wait_send()

        def drain_stepped(n):
            for at in halves(n):
                late_copy(at).wait_send()

        def drain_pulled(n):
            rows_six(n).wait_send()
            rows_seven(n).wait_send()

        each(drain)
        stepped(drain_stepped)
        pulled(drain_pulled)

    @pl.when(c == 3)
    def _():
        def turn(n):
            for p, at in enumerate(halves(n)):
                early_copy(at).wait_recv()
                early_out[at] = passed(n, p, 0, early_in[at])
            finish(n, 0, whole_state(early_in, n))
            finish(n, 1, whole_state(early_out, n))
            joint(n).wait_send()

        each(turn)


def settle(first_ref, second_ref, first_out, second_out, sems):
    copies = [
        pltpu.make_async_copy(first_ref, first_out, sems.at[0]),
        pltpu.make_async_copy(second_ref, second_out, sems.at[1]),
    ]
    for copy in copies:
        copy.start()
    for copy in copies:
        copy.wait()


def local(
    ctx_count,
    head_count,
    att_query,
    att_gate,
    att_kv,
    residual,
    out_weight,
    norm_gain,
    in_weight,
    beta_weight,
    log_decay,
    delta_gain,
):
    rows = att_query.shape[0]
    width = residual.shape[1]
    value_here = log_decay.shape[1]
    vmem = pl.BlockSpec(memory_space=pltpu.VMEM)
    hbm = pl.BlockSpec(memory_space=pl.ANY)
    heads_less = max(head_count - 1, 1)
    pair = pltpu.SemaphoreType.DMA
    direct = []
    if ctx_count == 4:
        block = (value_here, rows // 2, DK)
        square = (value_here, DK, DK)
        both = (value_here, 2, DK, DK)
        direct = [
            pltpu.VMEM((value_here, rows, DK), BF16),
            *[pltpu.VMEM(block, BF16)] * 4,
            pltpu.VMEM((value_here, rows, DK), BF16),
            pltpu.VMEM(both, BF16),
            pltpu.VMEM(both, BF16),
            pltpu.VMEM(square, BF16),
            pair((2, 2 * value_here)),
            pair((2, value_here)),
            pair((2, 2 * value_here)),
            pair((2, value_here)),
        ]
    outputs = pl.pallas_call(
        functools.partial(kernel, ctx_count, head_count),
        out_shape=(
            pltpu.VMEM((rows, width), BF16),
            pltpu.VMEM((rows, value_here * DV), BF16),
        ),
        in_specs=[hbm] * 10,
        out_specs=(vmem, vmem),
        scratch_shapes=[
            pltpu.VMEM(att_query.shape, BF16),
            pltpu.VMEM(att_gate.shape, BF16),
            pltpu.VMEM(residual.shape, BF16),
            pltpu.VMEM((1, norm_gain.shape[0]), F32),
            pltpu.VMEM(beta_weight.shape[::-1], BF16),
            pltpu.VMEM(log_decay.shape[::-1], F32),
            pltpu.VMEM((1, DV), F32),
            pltpu.VMEM((2, ctx_count * rows, HD), BF16),
            pltpu.VMEM(out_weight.shape, BF16),
            pltpu.VMEM(in_weight.shape, BF16),
            pltpu.VMEM(att_query.shape, BF16),
            pltpu.VMEM((head_count, rows, width), BF16),
            pltpu.VMEM((head_count, rows, width), BF16),
            pltpu.VMEM((heads_less, rows, width), BF16),
            pltpu.VMEM((heads_less, rows, width), BF16),
            pltpu.VMEM((2 * head_count, rows, width), BF16),
            pltpu.VMEM((rows, in_weight.shape[1]), F32),
            pltpu.VMEM((value_here, rows, rows), F32),
            pltpu.VMEM((rows, ctx_count * rows), F32),
            pltpu.VMEM(att_query.shape, F32),
            pltpu.VMEM((2, value_here, DK, DK), BF16),
            pltpu.VMEM((2, value_here, DK, DV), F32),
            pltpu.VMEM((value_here * PIECES, DV // PIECES, DK), BF16),
            pltpu.VMEM((value_here * PIECES, DV // PIECES, DK), BF16),
            pltpu.VMEM((value_here * PIECES, DV // PIECES, DK), BF16),
            pltpu.VMEM((value_here * PIECES, DV // PIECES, DK), BF16),
            pltpu.VMEM((value_here, rows, DV), F32),
            pltpu.VMEM((value_here, rows, DK), BF16),
            pair((11,)),
            pair((2, ctx_count)),
            pair((2, ctx_count)),
            pair((2, head_count)),
            pair((2, head_count * CHUNKS)),
            pair((2, head_count * CHUNKS)),
            pair((2, head_count * CHUNKS)),
            pair((2, value_here * PIECES)),
            pair((2, value_here * PIECES)),
            *direct,
        ],
        compiler_params=pltpu.CompilerParams(collective_id=0, has_side_effects=True),
    )(
        att_query,
        att_gate,
        att_kv,
        residual,
        out_weight,
        norm_gain.reshape(1, -1),
        in_weight,
        beta_weight.T,
        log_decay.T,
        delta_gain.reshape(1, -1),
    )
    return pl.pallas_call(
        settle,
        out_shape=tuple(jax.ShapeDtypeStruct(x.shape, x.dtype) for x in outputs),
        in_specs=[vmem, vmem],
        out_specs=(hbm, hbm),
        scratch_shapes=[pair((2,))],
    )(*[pltpu.with_memory_space_constraint(x, pltpu.VMEM) for x in outputs])


def solution(mesh):
    return jax.shard_map(
        functools.partial(local, mesh.shape["ctx"], mesh.shape["head"]),
        mesh=mesh,
        in_specs=(
            P(("groups", "ctx"), ("head", "sub")),
            P(("groups", "ctx"), ("head", "sub")),
            P(("groups", "ctx"), None),
            P(("groups", "ctx"), ("head", "sub")),
            P(("head", "sub"), None),
            P(),
            P(None, ("head", "sub")),
            P(None, ("head", "sub")),
            P(("groups", "ctx"), ("head", "sub")),
            P(),
        ),
        out_specs=(P(("groups", "ctx"), ("head", "sub")), P(("groups", "ctx"), ("head", "sub"))),
        check_vma=False,
    )
```

```python
import functools

import jax
import jax.numpy as jnp
from jax import lax
from jax.experimental import pallas as pl
from jax.experimental.pallas import tpu as pltpu
from jax.sharding import PartitionSpec as P

HEADS = 16
KV_HEADS = 2
HD = 256
DK = 128
DV = 128
EPSILON = 1e-06
NEGATIVE = -1e30
CHUNKS = 2
PIECES = 1
STEPPED = 4
F32 = jnp.float32
BF16 = jnp.bfloat16
MESH = pl.DeviceIdType.MESH


def dot(a, b):
    return jnp.dot(a, b, preferred_element_type=F32)


def dot_nt(a, b):
    return lax.dot_general(a, b, (((1,), (1,)), ((), ())), preferred_element_type=F32)


def dot_tn(a, b):
    return lax.dot_general(a, b, (((0,), (0,)), ((), ())), preferred_element_type=F32)


def silu(x):
    return x * jax.nn.sigmoid(x)


def unit(x):
    return x * lax.rsqrt(jnp.sum(x * x, axis=-1, keepdims=True) + EPSILON)


def remote(src, dst, sems, index, device):
    return pltpu.make_async_remote_copy(
        src_ref=src,
        dst_ref=dst,
        send_sem=sems.at[0, index],
        recv_sem=sems.at[1, index],
        device_id=device,
        device_id_type=MESH,
    )


def kernel(
    ctx_count,
    head_count,
    query_hbm,
    gate_hbm,
    kv_hbm,
    res_hbm,
    ow_hbm,
    norm_gain_hbm,
    iw_hbm,
    bw_hbm,
    ld_hbm,
    delta_gain_hbm,
    new_res_ref,
    delta_ref,
    query_ref,
    gate_ref,
    res_ref,
    norm_gain_ref,
    bw_ref,
    ld_ref,
    delta_gain_ref,
    kv,
    ow,
    iw,
    att,
    rs_send,
    rs_recv,
    x_send,
    x_recv,
    hid,
    macc,
    grid_ref,
    bias_ref,
    open_ref,
    trans,
    offs,
    early_in,
    late_in,
    early_out,
    late_out,
    local_out,
    read,
    load_sem,
    kv_sem,
    kvf_sem,
    rs_sem,
    x_sem,
    ag_sem,
    agf_sem,
    early_sem,
    late_sem,
    *direct,
):
    c = lax.axis_index("ctx")
    h = lax.axis_index("head")
    s = lax.axis_index("sub")
    rows = query_ref.shape[0]
    half = rows // 2
    heads_here = query_ref.shape[1] // HD
    shard = h * 2 + s
    width = res_ref.shape[1]
    partner = {"sub": 1 - s}
    kv_number = shard * heads_here // (HEADS // KV_HEADS)

    def lines_of(device, full):
        return pl.ds(pl.multiple_of(device * rows, rows), rows if full else half)

    loads = []
    for part in range(2):
        start = pl.multiple_of(kv_number * 2 * HD + part * HD, HD)
        loads.append(
            pltpu.make_async_copy(
                kv_hbm.at[:, pl.ds(start, HD)],
                kv.at[part, lines_of(c, True)],
                load_sem.at[9 + part],
            )
        )
    ow_load = pltpu.make_async_copy(ow_hbm, ow, load_sem.at[0])
    iw_load = pltpu.make_async_copy(iw_hbm, iw, load_sem.at[1])
    small = [
        pltpu.make_async_copy(source, target, load_sem.at[2 + i])
        for i, (source, target) in enumerate(
            [
                (ld_hbm, ld_ref),
                (query_hbm, query_ref),
                (gate_hbm, gate_ref),
                (res_hbm, res_ref),
                (norm_gain_hbm, norm_gain_ref),
                (bw_hbm, bw_ref),
                (delta_gain_hbm, delta_gain_ref),
            ]
        )
    ]
    barrier = pltpu.get_barrier_semaphore()
    for d in range(1, ctx_count):
        pl.semaphore_signal(
            barrier, inc=1, device_id={"ctx": lax.rem(c + d, ctx_count)}, device_id_type=MESH
        )
    for d in range(1, head_count):
        pl.semaphore_signal(
            barrier, inc=1, device_id={"head": lax.rem(h + d, head_count)}, device_id_type=MESH
        )
    pl.semaphore_signal(barrier, inc=1, device_id=partner, device_id_type=MESH)
    for load in loads + small:
        load.start()

    @pl.when(c == 0)
    def _():
        early_in[...] = jnp.zeros_like(early_in)

    for d in range(1, ctx_count):

        @pl.when(c >= d)
        def _():
            hidden_rows = pl.ds(pl.multiple_of((c - d) * rows + half, half), half)
            kv[:, hidden_rows, :] = jnp.zeros((2, half, HD), BF16)

    pl.semaphore_wait(barrier, ctx_count + head_count - 1)

    sends = []
    for load in loads:
        load.wait()
    others = range(1, ctx_count)

    def gather(d, full):
        piece = kv.at[s, lines_of(c, full)]
        return remote(piece, piece, kv_sem, d - 1, {"ctx": lax.rem(c + d, ctx_count)})

    def forward(d, full):
        piece = kv.at[s, lines_of(lax.rem(c - d + ctx_count, ctx_count), full)]
        return remote(piece, piece, kvf_sem, d - 1, partner)

    def sent(d, body):
        pl.when(c + d >= ctx_count)(lambda: body(True))
        pl.when(c + d < ctx_count)(lambda: body(False))

    def received(d, body):
        pl.when(c < d)(lambda: body(True))
        pl.when(c >= d)(lambda: body(False))

    for d in others:
        sent(d, lambda full: gather(d, full).start())

    ow_load.start()
    row = lax.broadcasted_iota(jnp.int32, (rows, rows), 0)
    col = lax.broadcasted_iota(jnp.int32, (rows, rows), 1)
    same = (row < half) == (col < half)
    on_or_below = same & (row >= col)
    strictly = same & (row > col)
    eye = jnp.where(row == col, 1.0, 0.0)
    small[0].wait()
    lower = jnp.where(on_or_below, 1.0, 0.0)
    every = jnp.where(same, 1.0, 0.0)
    decays = ld_ref[...]

    def row_sums(picked):
        return lax.dot_general(
            decays,
            picked,
            (((1,), (1,)), ((), ())),
            precision=lax.Precision.HIGHEST,
            preferred_element_type=F32,
        )

    cum_row = row_sums(lower)
    sum_row = row_sums(every)
    cumulative = cum_row.T
    block_sum = sum_row.T
    growth = jnp.exp(cumulative)
    carry = jnp.exp(block_sum - cumulative)
    for n in range(ld_ref.shape[0]):
        gap = cumulative[:, n : n + 1] - cum_row[n : n + 1, :]
        grid_ref[n] = jnp.where(on_or_below, jnp.exp(jnp.where(on_or_below, gap, 0.0)), 0.0)

    for load in small[1:]:
        load.wait()
    total_rows = ctx_count * rows
    q_row = lax.broadcasted_iota(jnp.int32, (rows, total_rows), 0)
    k_row = lax.broadcasted_iota(jnp.int32, (rows, total_rows), 1)
    shift = rows.bit_length() - 1
    k_dev = k_row >> shift
    k_in = k_row & (rows - 1)
    last_block = 2 * ctx_count - 1
    q_pos = jnp.where(q_row < half, c, last_block - c) * half + (q_row & (half - 1))
    k_pos = jnp.where(k_in < half, k_dev, last_block - k_dev) * half + (k_in & (half - 1))
    bias_ref[...] = jnp.where(q_pos >= k_pos, 0.0, NEGATIVE)
    open_ref[...] = jax.nn.sigmoid(gate_ref[...].astype(F32))

    def pass_on(d, full):
        gather(d, full).wait_recv()
        forward(d, full).start()

    for d in others:
        pl.when(c + d < ctx_count)(lambda: pass_on(ctx_count - d, True))
        pl.when(c >= d)(lambda: pass_on(d, False))
    iw_load.start()
    for d in others:
        received(d, lambda full: forward(d, full).wait_recv())

    keys = kv[0]
    values = kv[1]
    for n in range(heads_here):
        cols = slice(n * HD, (n + 1) * HD)
        scores = dot_nt(query_ref[:, cols], keys) * (HD**-0.5) + bias_ref[...]
        weights = jnp.exp(scores - jnp.max(scores, axis=1, keepdims=True))
        total = jnp.sum(weights, axis=1, keepdims=True)
        mixed = dot(weights.astype(BF16), values) * (1.0 / total)
        att[:, cols] = (mixed * open_ref[:, cols]).astype(BF16)

    ow_load.wait()
    attended = att[...]

    def out_slice(number):
        return dot(attended, ow[:, pl.ds(pl.multiple_of(number * width, width), width)])

    chunks = [slice(k * rows // CHUNKS, (k + 1) * rows // CHUNKS) for k in range(CHUNKS)]
    peers = [lax.rem(h + 1 + i, head_count) for i in range(head_count)]
    pair_copies = []
    for i in range(head_count):
        rs_send[i] = out_slice(peers[i] * 2 + 1 - s).astype(BF16)
        copy = remote(rs_send.at[i], rs_recv.at[i], rs_sem, i, partner)
        copy.start()
        pair_copies.append(copy)
    head_copies = []
    for i in range(head_count):
        part = out_slice(peers[i] * 2 + s)
        pair_copies[i].wait_recv()
        part = part + rs_recv[i].astype(F32)
        if i < head_count - 1:
            x_send[i] = part.astype(BF16)
            for k, lines in enumerate(chunks):
                copy = remote(
                    x_send.at[i, lines], x_recv.at[i, lines], x_sem, i * CHUNKS + k, {"head": peers[i]}
                )
                copy.start()
                head_copies.append(copy)
    part = part + res_ref[...].astype(F32)
    sends += pair_copies + head_copies
    to_heads = []
    to_partner = []
    for k, lines in enumerate(chunks):
        own = part[lines]
        for i in range(head_count - 1):
            head_copies[i * CHUNKS + k].wait_recv()
            own = own + x_recv[i, lines].astype(F32)
        own16 = own.astype(BF16)
        new_res_ref[lines, :] = own16
        hid[shard, lines] = own16
        mine = hid.at[shard, lines]
        for i in range(head_count - 1):
            copy = remote(mine, mine, ag_sem, i * CHUNKS + k, {"head": peers[i]})
            copy.start()
            to_heads.append(copy)
        copy = remote(mine, mine, agf_sem, (head_count - 1) * CHUNKS + k, partner)
        copy.start()
        to_partner.append(copy)
    iw_load.wait()

    def projected(r, start):
        cols = pl.ds(pl.multiple_of(r * width, width), width)
        piece = hid[r].astype(F32)
        scaled = (piece * norm_gain_ref[:, cols]).astype(BF16)
        term = dot(scaled, iw[cols, :])
        logits = dot_nt(bw_ref[:, cols], scaled)
        square = jnp.sum(piece * piece, axis=1, keepdims=True)
        if start is None:
            macc[...] = term
            return logits, square
        macc[...] += term
        return start[0] + logits, start[1] + square

    sources = [lax.rem(h - 1 - i + head_count, head_count) * 2 for i in range(head_count - 1)]
    parts = projected(shard, None)
    for k, lines in enumerate(chunks):
        for i in range(head_count - 1):
            to_heads[k * (head_count - 1) + i].wait_recv()
            piece = hid.at[sources[i] + s, lines]
            copy = remote(piece, piece, agf_sem, i * CHUNKS + k, partner)
            copy.start()
            to_partner.append(copy)
    for copy in to_partner[:CHUNKS]:
        copy.wait_recv()
    parts = projected(h * 2 + 1 - s, parts)
    for i in range(head_count - 1):
        parts = projected(sources[i] + s, parts)
    for copy in to_partner[CHUNKS:]:
        copy.wait_recv()
    for i in range(head_count - 1):
        parts = projected(sources[i] + 1 - s, parts)
    sends += to_heads + to_partner
    scale = lax.rsqrt(parts[1] / (2 * head_count * width) + EPSILON)
    group = 2 * DK + 2 * DV
    key_here = iw.shape[1] // group
    value_here = 2 * key_here

    beta = jax.nn.sigmoid(parts[0].T * scale)
    queries, grams, attends, values_of, keys_of = [], [], [], [], []
    for j in range(key_here):
        m = macc[:, j * group : (j + 1) * group] * scale
        q = unit(silu(m[:, :DK])) * DK**-0.5
        k = unit(silu(m[:, DK : 2 * DK]))
        v = silu(m[:, 2 * DK :])
        q16, k16 = q.astype(BF16), k.astype(BF16)
        queries.append(q)
        keys_of.append(k)
        values_of += [v[:, :DV], v[:, DV:]]
        grams.append(dot_nt(k16, k16))
        attends.append(dot_nt(q16, k16))
    systems, inverses, grids = [], [], []
    for n in range(value_here):
        grid = grid_ref[n]
        system = jnp.where(strictly, beta[:, n : n + 1] * grams[n // 2] * grid, 0.0)
        grids.append((attends[n // 2] * grid).astype(BF16))
        systems.append(system)
        inverses.append(eye - jnp.where((row >> 1) == (col >> 1), system, 0.0))
    level = 1
    while (1 << level) < half:
        mask = ((row >> (level + 1)) == (col >> (level + 1))) & ((row >> level) != (col >> level))
        halves = [inverse.astype(BF16) for inverse in inverses]
        firsts = [
            dot(jnp.where(mask, system, 0.0).astype(BF16), inverse).astype(BF16)
            for system, inverse in zip(systems, halves)
        ]
        inverses = [
            full - dot(inverse, product)
            for full, inverse, product in zip(inverses, halves, firsts)
        ]
        level += 1
    last = ctx_count - 1
    nxt = {"ctx": lax.min(c + 1, last)}
    prv = {"ctx": lax.max(c - 1, 0)}

    def early_copy(n):
        return remote(early_out.at[n], early_in.at[n], early_sem, n, nxt)

    def late_copy(n):
        return remote(late_out.at[n], late_in.at[n], late_sem, n, prv)

    solutions, carries = {}, {}

    def solve(n):
        beta_n = beta[:, n : n + 1]
        right = jnp.concatenate(
            [beta_n * values_of[n], (beta_n * growth[:, n : n + 1]) * keys_of[n // 2]], axis=1
        )
        solutions[n] = dot(inverses[n].astype(BF16), right.astype(BF16)).astype(BF16)
        carries[n] = (keys_of[n // 2] * carry[:, n : n + 1]).astype(BF16)

    def piece_rows(p):
        return slice(p * DV // PIECES, (p + 1) * DV // PIECES)

    def block_ends(n, b):
        lines = slice(b * half, (b + 1) * half)
        ends = dot_tn(solutions[n][lines], carries[n][lines])
        offs[b, n] = ends[:DV]
        whole = jnp.exp(block_sum[b * half : b * half + 1, n : n + 1])
        trans[b, n] = (whole * eye[:DK, :DK] - ends[DV:]).astype(BF16)
        if b == 0:
            for p in range(PIECES):
                early_out[n * PIECES + p] = ends[piece_rows(p)].astype(BF16)

    def drain_sends():
        for copy in sends:
            copy.wait_send()
        for d in others:
            sent(d, lambda full: gather(d, full).wait_send())
            received(d, lambda full: forward(d, full).wait_send())

    def local_terms(n):
        inner = dot(grids[n], solutions[n])
        local_out[n] = inner[:, :DV]
        read[n] = (growth[:, n : n + 1] * queries[n // 2] - inner[:, DV:]).astype(BF16)

    def normed(n, b, out):
        lines = slice(b * half, (b + 1) * half)
        mean = jnp.mean(out * out, axis=1, keepdims=True)
        out = out * lax.rsqrt(mean + EPSILON) * delta_gain_ref[...]
        if isinstance(n, int):
            delta_ref[lines, n * DV : (n + 1) * DV] = out.astype(BF16)
        else:
            delta_ref[lines, pl.ds(pl.multiple_of(n * DV, DV), DV)] = out.astype(BF16)

    def finish(n, b, state):
        lines = slice(b * half, (b + 1) * half)
        normed(n, b, local_out[n, lines, :] + dot_nt(read[n, lines, :], state))

    def passed(n, p, b, state):
        return (dot(state, trans[b, n]) + offs[b, n, piece_rows(p), :]).astype(BF16)

    def whole_state(ref, n):
        return jnp.concatenate([ref[n * PIECES + p] for p in range(PIECES)], axis=0)

    if ctx_count == 4:
        four_blocks(
            c,
            half,
            value_here,
            early_copy,
            late_copy,
            solve,
            block_ends,
            local_terms,
            normed,
            finish,
            passed,
            whole_state,
            trans,
            offs,
            early_in,
            early_out,
            late_in,
            late_out,
            local_out,
            read,
            drain_sends,
            *direct,
        )
        return

    for n in range(value_here):
        solve(n)
    for n in range(value_here):
        block_ends(n, 0)

    @pl.when(c == 0)
    def _():
        for n in range(value_here * PIECES):
            early_copy(n).start()

    for n in range(value_here):
        block_ends(n, 1)
        local_terms(n)

    @pl.when(c > 0)
    def _():
        def early_turn(n, carried):
            for p in range(PIECES):
                at = n * PIECES + p
                early_copy(at).wait_recv()
                end = passed(n, p, 0, early_in[at])

                @pl.when(c < last)
                def _():
                    early_out[at] = end
                    early_copy(at).start()

                @pl.when(c == last)
                def _():
                    late_in[at] = end
                    late_out[at] = passed(n, p, 1, end)
                    late_copy(at).start()

            return carried

        lax.fori_loop(0, value_here, early_turn, 0)

    for n in range(value_here):
        finish(n, 0, whole_state(early_in, n))

    @pl.when((c > 0) & (c < last))
    def _():
        def late_turn(n, carried):
            for p in range(PIECES):
                at = n * PIECES + p
                late_copy(at).wait_recv()
                late_out[at] = passed(n, p, 1, late_in[at])
                late_copy(at).start()
            return carried

        lax.fori_loop(0, value_here, late_turn, 0)

    @pl.when(c == 0)
    def _():
        def last_turn(n, carried):
            for p in range(PIECES):
                late_copy(n * PIECES + p).wait_recv()
            finish(n, 1, whole_state(late_in, n))
            return carried

        lax.fori_loop(0, value_here, last_turn, 0)

    @pl.when(c > 0)
    def _():
        for n in range(value_here):
            finish(n, 1, whole_state(late_in, n))

    drain_sends()

    def drain(n, carry):
        @pl.when(c < last)
        def _():
            early_copy(n).wait_send()

        @pl.when(c > 0)
        def _():
            late_copy(n).wait_send()

        return carry

    lax.fori_loop(0, value_here * PIECES, drain, 0)


def four_blocks(
    c,
    half,
    value_here,
    early_copy,
    late_copy,
    solve,
    block_ends,
    local_terms,
    normed,
    finish,
    passed,
    whole_state,
    trans,
    offs,
    early_in,
    early_out,
    late_in,
    late_out,
    local_out,
    read,
    drain_sends,
    ra,
    a_out,
    c_in,
    c_out,
    v_in,
    v_out,
    comp_in,
    comp_out,
    fifth,
    ra_sem,
    c_sem,
    v_sem,
    comp_sem,
):
    low, high = pl.ds(0, half), pl.ds(half, half)
    late = slice(half, 2 * half)

    def to(device):
        return {"ctx": device}

    def read_six(n):
        return remote(read.at[n, high], ra.at[n, low], ra_sem, n, to(2))

    def read_seven(n):
        return remote(read.at[n, high], ra.at[n, high], ra_sem, value_here + n, to(1))

    def read_back(n):
        return remote(a_out.at[n], ra.at[n, high], ra_sem, value_here + n, to(2))

    def constant(n):
        return remote(c_out.at[n], c_in.at[n], c_sem, n, to(0))

    def joint(n):
        return remote(comp_out.at[n], comp_in.at[n], comp_sem, n, to(2))

    def rows_six(n):
        return remote(v_out.at[n, low], v_in.at[n], v_sem, n, to(1))

    def rows_seven(n):
        return remote(v_out.at[n, high], v_in.at[n], v_sem, value_here + n, to(0))

    def each(body, first=0, end=value_here):
        def turn(n, carried):
            body(n)
            return carried

        lax.fori_loop(first, end, turn, 0)

    def stepped(body):
        each(body, 0, STEPPED)

    def pulled(body):
        each(body, STEPPED)

    def halves(n):
        return [n * PIECES + p for p in range(PIECES)]

    def send(n):
        for at in halves(n):
            early_copy(at).start()

    def join(n):
        fourth = trans[1, n]
        comp_out[n, 0] = dot(trans[0, n], fourth).astype(BF16)
        comp_out[n, 1] = (dot(offs[0, n].astype(BF16), fourth) + offs[1, n]).astype(BF16)
        joint(n).start()

    bounds = [0, 2, STEPPED, STEPPED + 2, value_here]
    for first, end in zip(bounds[:-1], bounds[1:]):
        for n in range(first, end):
            solve(n)
            block_ends(n, 0)
            block_ends(n, 1)

        @pl.when(c == 0)
        def _():
            for n in range(first, min(end, STEPPED)):
                send(n)

        @pl.when(c == 3)
        def _():
            for n in range(first, end):
                join(n)

    for n in range(value_here):
        local_terms(n)

    @pl.when(c == 0)
    def _():
        def send_both(n):
            send(n)
            read_seven(n).start()

        pulled(send_both)

    @pl.when(c == 1)
    def _():
        pulled(lambda n: read_six(n).start())

    drain_sends()

    @pl.when(c == 0)
    def _():
        for n in range(value_here):
            normed(n, 0, local_out[n, :half, :])

        def step(n):
            for at in halves(n):
                late_copy(at).wait_recv()
            finish(n, 1, whole_state(late_in, n))

        def last(n):
            constant(n).wait_recv()
            rows_seven(n).wait_recv()
            normed(n, 1, local_out[n, late, :] + c_in[n].astype(F32) + v_in[n].astype(F32))

        def drain(n):
            for at in halves(n):
                early_copy(at).wait_send()

        stepped(step)
        each(drain)
        pulled(lambda n: read_seven(n).wait_send())
        pulled(last)

    @pl.when(c == 1)
    def _():
        def up(n):
            for p, at in enumerate(halves(n)):
                early_copy(at).wait_recv()
                early_out[at] = passed(n, p, 0, early_in[at])
                early_copy(at).start()

        def turn(n):
            up(n)
            read_seven(n).wait_recv()
            seven = ra[n, late, :]
            a_out[n] = dot_nt(seven, trans[1, n]).astype(BF16)
            read_back(n).start()
            c_out[n] = dot_nt(seven, offs[1, n].astype(BF16)).astype(BF16)
            constant(n).start()

        def down(n):
            for p, at in enumerate(halves(n)):
                late_copy(at).wait_recv()
                late_out[at] = passed(n, p, 1, late_in[at])
                late_copy(at).start()

        stepped(up)
        pulled(turn)
        stepped(down)
        for n in range(value_here):
            finish(n, 0, whole_state(early_in, n))
        for n in range(STEPPED):
            finish(n, 1, whole_state(late_in, n))

        def last(n):
            rows_six(n).wait_recv()
            normed(n, 1, local_out[n, late, :] + v_in[n].astype(F32))

        pulled(last)

        def drain(n):
            for at in halves(n):
                early_copy(at).wait_send()

        def drain_stepped(n):
            for at in halves(n):
                late_copy(at).wait_send()

        def drain_pulled(n):
            read_six(n).wait_send()
            read_back(n).wait_send()
            constant(n).wait_send()

        each(drain)
        stepped(drain_stepped)
        pulled(drain_pulled)

    @pl.when(c == 2)
    def _():
        def up(n):
            for p, at in enumerate(halves(n)):
                early_copy(at).wait_recv()
                early_out[at] = passed(n, p, 0, early_in[at])
                early_copy(at).start()
            joint(n).wait_recv()
            state = dot(whole_state(early_out, n), comp_in[n, 0]) + comp_in[n, 1].astype(F32)
            state = state.astype(BF16)
            fifth[n] = state
            return state

        def step(n):
            state = up(n)
            for p, at in enumerate(halves(n)):
                late_out[at] = passed(n, p, 1, state[p * DV // PIECES : (p + 1) * DV // PIECES])
                late_copy(at).start()

        def turn(n):
            state = up(n)
            read_six(n).wait_recv()
            read_back(n).wait_recv()
            reads = ra[n]
            back = dot_nt(reads, trans[1, n]).astype(BF16)
            plain = dot_nt(reads, offs[1, n].astype(BF16))
            v_out[n] = (dot_nt(back, state) + plain).astype(BF16)
            rows_seven(n).start()
            rows_six(n).start()

        stepped(step)
        pulled(turn)
        for n in range(value_here):
            finish(n, 0, whole_state(early_in, n))
            finish(n, 1, fifth[n])

        def drain(n):
            for at in halves(n):
                early_copy(at).wait_send()

        def drain_stepped(n):
            for at in halves(n):
                late_copy(at).wait_send()

        def drain_pulled(n):
            rows_six(n).wait_send()
            rows_seven(n).wait_send()

        each(drain)
        stepped(drain_stepped)
        pulled(drain_pulled)

    @pl.when(c == 3)
    def _():
        def turn(n):
            for p, at in enumerate(halves(n)):
                early_copy(at).wait_recv()
                early_out[at] = passed(n, p, 0, early_in[at])
            finish(n, 0, whole_state(early_in, n))
            finish(n, 1, whole_state(early_out, n))
            joint(n).wait_send()

        each(turn)


def settle(first_ref, second_ref, first_out, second_out, sems):
    copies = [
        pltpu.make_async_copy(first_ref, first_out, sems.at[0]),
        pltpu.make_async_copy(second_ref, second_out, sems.at[1]),
    ]
    for copy in copies:
        copy.start()
    for copy in copies:
        copy.wait()


def local(
    ctx_count,
    head_count,
    att_query,
    att_gate,
    att_kv,
    residual,
    out_weight,
    norm_gain,
    in_weight,
    beta_weight,
    log_decay,
    delta_gain,
):
    rows = att_query.shape[0]
    width = residual.shape[1]
    value_here = log_decay.shape[1]
    vmem = pl.BlockSpec(memory_space=pltpu.VMEM)
    hbm = pl.BlockSpec(memory_space=pl.ANY)
    heads_less = max(head_count - 1, 1)
    pair = pltpu.SemaphoreType.DMA
    direct = []
    if ctx_count == 4:
        block = (value_here, rows // 2, DK)
        square = (value_here, DK, DK)
        both = (value_here, 2, DK, DK)
        direct = [
            pltpu.VMEM((value_here, rows, DK), BF16),
            *[pltpu.VMEM(block, BF16)] * 4,
            pltpu.VMEM((value_here, rows, DK), BF16),
            pltpu.VMEM(both, BF16),
            pltpu.VMEM(both, BF16),
            pltpu.VMEM(square, BF16),
            pair((2, 2 * value_here)),
            pair((2, value_here)),
            pair((2, 2 * value_here)),
            pair((2, value_here)),
        ]
    outputs = pl.pallas_call(
        functools.partial(kernel, ctx_count, head_count),
        out_shape=(
            pltpu.VMEM((rows, width), BF16),
            pltpu.VMEM((rows, value_here * DV), BF16),
        ),
        in_specs=[hbm] * 10,
        out_specs=(vmem, vmem),
        scratch_shapes=[
            pltpu.VMEM(att_query.shape, BF16),
            pltpu.VMEM(att_gate.shape, BF16),
            pltpu.VMEM(residual.shape, BF16),
            pltpu.VMEM((1, norm_gain.shape[0]), F32),
            pltpu.VMEM(beta_weight.shape[::-1], BF16),
            pltpu.VMEM(log_decay.shape[::-1], F32),
            pltpu.VMEM((1, DV), F32),
            pltpu.VMEM((2, ctx_count * rows, HD), BF16),
            pltpu.VMEM(out_weight.shape, BF16),
            pltpu.VMEM(in_weight.shape, BF16),
            pltpu.VMEM(att_query.shape, BF16),
            pltpu.VMEM((head_count, rows, width), BF16),
            pltpu.VMEM((head_count, rows, width), BF16),
            pltpu.VMEM((heads_less, rows, width), BF16),
            pltpu.VMEM((heads_less, rows, width), BF16),
            pltpu.VMEM((2 * head_count, rows, width), BF16),
            pltpu.VMEM((rows, in_weight.shape[1]), F32),
            pltpu.VMEM((value_here, rows, rows), F32),
            pltpu.VMEM((rows, ctx_count * rows), F32),
            pltpu.VMEM(att_query.shape, F32),
            pltpu.VMEM((2, value_here, DK, DK), BF16),
            pltpu.VMEM((2, value_here, DK, DV), F32),
            pltpu.VMEM((value_here * PIECES, DV // PIECES, DK), BF16),
            pltpu.VMEM((value_here * PIECES, DV // PIECES, DK), BF16),
            pltpu.VMEM((value_here * PIECES, DV // PIECES, DK), BF16),
            pltpu.VMEM((value_here * PIECES, DV // PIECES, DK), BF16),
            pltpu.VMEM((value_here, rows, DV), F32),
            pltpu.VMEM((value_here, rows, DK), BF16),
            pair((11,)),
            pair((2, ctx_count)),
            pair((2, ctx_count)),
            pair((2, head_count)),
            pair((2, head_count * CHUNKS)),
            pair((2, head_count * CHUNKS)),
            pair((2, head_count * CHUNKS)),
            pair((2, value_here * PIECES)),
            pair((2, value_here * PIECES)),
            *direct,
        ],
        compiler_params=pltpu.CompilerParams(collective_id=0, has_side_effects=True),
    )(
        att_query,
        att_gate,
        att_kv,
        residual,
        out_weight,
        norm_gain.reshape(1, -1),
        in_weight,
        beta_weight.T,
        log_decay.T,
        delta_gain.reshape(1, -1),
    )
    return pl.pallas_call(
        settle,
        out_shape=tuple(jax.ShapeDtypeStruct(x.shape, x.dtype) for x in outputs),
        in_specs=[vmem, vmem],
        out_specs=(hbm, hbm),
        scratch_shapes=[pair((2,))],
    )(*[pltpu.with_memory_space_constraint(x, pltpu.VMEM) for x in outputs])


def solution(mesh):
    return jax.shard_map(
        functools.partial(local, mesh.shape["ctx"], mesh.shape["head"]),
        mesh=mesh,
        in_specs=(
            P(("groups", "ctx"), ("head", "sub")),
            P(("groups", "ctx"), ("head", "sub")),
            P(("groups", "ctx"), None),
            P(("groups", "ctx"), ("head", "sub")),
            P(("head", "sub"), None),
            P(),
            P(None, ("head", "sub")),
            P(None, ("head", "sub")),
            P(("groups", "ctx"), ("head", "sub")),
            P(),
        ),
        out_specs=(P(("groups", "ctx"), ("head", "sub")), P(("groups", "ctx"), ("head", "sub"))),
        check_vma=False,
    )
```

```python
import functools

import jax
import jax.numpy as jnp
from jax import lax
from jax.experimental import pallas as pl
from jax.experimental.pallas import tpu as pltpu
from jax.sharding import PartitionSpec as P

HEADS = 16
KV_HEADS = 2
HD = 256
DK = 128
DV = 128
EPSILON = 1e-06
NEGATIVE = -1e30
CHUNKS = 2
PIECES = 1
STEPPED = 4
F32 = jnp.float32
BF16 = jnp.bfloat16
MESH = pl.DeviceIdType.MESH


def dot(a, b):
    return jnp.dot(a, b, preferred_element_type=F32)


def dot_nt(a, b):
    return lax.dot_general(a, b, (((1,), (1,)), ((), ())), preferred_element_type=F32)


def dot_tn(a, b):
    return lax.dot_general(a, b, (((0,), (0,)), ((), ())), preferred_element_type=F32)


def silu(x):
    return x * jax.nn.sigmoid(x)


def unit(x):
    return x * lax.rsqrt(jnp.sum(x * x, axis=-1, keepdims=True) + EPSILON)


def remote(src, dst, sems, index, device):
    return pltpu.make_async_remote_copy(
        src_ref=src,
        dst_ref=dst,
        send_sem=sems.at[0, index],
        recv_sem=sems.at[1, index],
        device_id=device,
        device_id_type=MESH,
    )


def kernel(
    ctx_count,
    head_count,
    query_hbm,
    gate_hbm,
    kv_hbm,
    res_hbm,
    ow_hbm,
    norm_gain_hbm,
    iw_hbm,
    bw_hbm,
    ld_hbm,
    delta_gain_hbm,
    new_res_ref,
    delta_ref,
    query_ref,
    gate_ref,
    res_ref,
    norm_gain_ref,
    bw_ref,
    ld_ref,
    delta_gain_ref,
    kv,
    ow,
    iw,
    att,
    rs_send,
    rs_recv,
    x_send,
    x_recv,
    hid,
    macc,
    grid_ref,
    bias_ref,
    open_ref,
    trans,
    offs,
    early_in,
    late_in,
    early_out,
    late_out,
    local_out,
    read,
    load_sem,
    kv_sem,
    kvf_sem,
    rs_sem,
    x_sem,
    ag_sem,
    agf_sem,
    early_sem,
    late_sem,
    *direct,
):
    c = lax.axis_index("ctx")
    h = lax.axis_index("head")
    s = lax.axis_index("sub")
    rows = query_ref.shape[0]
    half = rows // 2
    heads_here = query_ref.shape[1] // HD
    shard = h * 2 + s
    width = res_ref.shape[1]
    partner = {"sub": 1 - s}
    kv_number = shard * heads_here // (HEADS // KV_HEADS)

    def lines_of(device, full):
        return pl.ds(pl.multiple_of(device * rows, rows), rows if full else half)

    loads = []
    for part in range(2):
        start = pl.multiple_of(kv_number * 2 * HD + part * HD, HD)
        loads.append(
            pltpu.make_async_copy(
                kv_hbm.at[:, pl.ds(start, HD)],
                kv.at[part, lines_of(c, True)],
                load_sem.at[9 + part],
            )
        )
    ow_load = pltpu.make_async_copy(ow_hbm, ow, load_sem.at[0])
    iw_load = pltpu.make_async_copy(iw_hbm, iw, load_sem.at[1])
    small = [
        pltpu.make_async_copy(source, target, load_sem.at[2 + i])
        for i, (source, target) in enumerate(
            [
                (ld_hbm, ld_ref),
                (query_hbm, query_ref),
                (gate_hbm, gate_ref),
                (res_hbm, res_ref),
                (norm_gain_hbm, norm_gain_ref),
                (bw_hbm, bw_ref),
                (delta_gain_hbm, delta_gain_ref),
            ]
        )
    ]
    barrier = pltpu.get_barrier_semaphore()
    for d in range(1, ctx_count):
        pl.semaphore_signal(
            barrier, inc=1, device_id={"ctx": lax.rem(c + d, ctx_count)}, device_id_type=MESH
        )
    for d in range(1, head_count):
        pl.semaphore_signal(
            barrier, inc=1, device_id={"head": lax.rem(h + d, head_count)}, device_id_type=MESH
        )
    pl.semaphore_signal(barrier, inc=1, device_id=partner, device_id_type=MESH)
    for load in loads + small:
        load.start()
    ow_load.start()
    iw_load.start()

    @pl.when(c == 0)
    def _():
        early_in[...] = jnp.zeros_like(early_in)

    for d in range(1, ctx_count):

        @pl.when(c >= d)
        def _():
            hidden_rows = pl.ds(pl.multiple_of((c - d) * rows + half, half), half)
            kv[:, hidden_rows, :] = jnp.zeros((2, half, HD), BF16)

    pl.semaphore_wait(barrier, ctx_count + head_count - 1)

    sends = []
    for load in loads:
        load.wait()
    others = range(1, ctx_count)

    def gather(d, full):
        piece = kv.at[s, lines_of(c, full)]
        return remote(piece, piece, kv_sem, d - 1, {"ctx": lax.rem(c + d, ctx_count)})

    def forward(d, full):
        piece = kv.at[s, lines_of(lax.rem(c - d + ctx_count, ctx_count), full)]
        return remote(piece, piece, kvf_sem, d - 1, partner)

    def sent(d, body):
        pl.when(c + d >= ctx_count)(lambda: body(True))
        pl.when(c + d < ctx_count)(lambda: body(False))

    def received(d, body):
        pl.when(c < d)(lambda: body(True))
        pl.when(c >= d)(lambda: body(False))

    for d in others:
        sent(d, lambda full: gather(d, full).start())

    row = lax.broadcasted_iota(jnp.int32, (rows, rows), 0)
    col = lax.broadcasted_iota(jnp.int32, (rows, rows), 1)
    same = (row < half) == (col < half)
    on_or_below = same & (row >= col)
    strictly = same & (row > col)
    eye = jnp.where(row == col, 1.0, 0.0)
    small[0].wait()
    lower = jnp.where(on_or_below, 1.0, 0.0)
    every = jnp.where(same, 1.0, 0.0)
    decays = ld_ref[...]

    def row_sums(picked):
        return lax.dot_general(
            decays,
            picked,
            (((1,), (1,)), ((), ())),
            precision=lax.Precision.HIGHEST,
            preferred_element_type=F32,
        )

    cum_row = row_sums(lower)
    sum_row = row_sums(every)
    cumulative = cum_row.T
    block_sum = sum_row.T
    growth = jnp.exp(cumulative)
    carry = jnp.exp(block_sum - cumulative)
    for n in range(ld_ref.shape[0]):
        gap = cumulative[:, n : n + 1] - cum_row[n : n + 1, :]
        grid_ref[n] = jnp.where(on_or_below, jnp.exp(jnp.where(on_or_below, gap, 0.0)), 0.0)

    for load in small[1:]:
        load.wait()
    total_rows = ctx_count * rows
    q_row = lax.broadcasted_iota(jnp.int32, (rows, total_rows), 0)
    k_row = lax.broadcasted_iota(jnp.int32, (rows, total_rows), 1)
    shift = rows.bit_length() - 1
    k_dev = k_row >> shift
    k_in = k_row & (rows - 1)
    last_block = 2 * ctx_count - 1
    q_pos = jnp.where(q_row < half, c, last_block - c) * half + (q_row & (half - 1))
    k_pos = jnp.where(k_in < half, k_dev, last_block - k_dev) * half + (k_in & (half - 1))
    bias_ref[...] = jnp.where(q_pos >= k_pos, 0.0, NEGATIVE)
    open_ref[...] = jax.nn.sigmoid(gate_ref[...].astype(F32))

    def pass_on(d, full):
        gather(d, full).wait_recv()
        forward(d, full).start()

    for d in others:
        received(d, lambda full: pass_on(d, full))
    for d in others:
        received(d, lambda full: forward(d, full).wait_recv())

    keys = kv[0]
    values = kv[1]
    for n in range(heads_here):
        cols = slice(n * HD, (n + 1) * HD)
        scores = dot_nt(query_ref[:, cols], keys) * (HD**-0.5) + bias_ref[...]
        weights = jnp.exp(scores - jnp.max(scores, axis=1, keepdims=True))
        total = jnp.sum(weights, axis=1, keepdims=True)
        mixed = dot(weights.astype(BF16), values) * (1.0 / total)
        att[:, cols] = (mixed * open_ref[:, cols]).astype(BF16)

    ow_load.wait()
    attended = att[...]

    def out_slice(number):
        return dot(attended, ow[:, pl.ds(pl.multiple_of(number * width, width), width)])

    chunks = [slice(k * rows // CHUNKS, (k + 1) * rows // CHUNKS) for k in range(CHUNKS)]
    peers = [lax.rem(h + 1 + i, head_count) for i in range(head_count)]
    pair_copies = []
    for i in range(head_count):
        rs_send[i] = out_slice(peers[i] * 2 + 1 - s).astype(BF16)
        copy = remote(rs_send.at[i], rs_recv.at[i], rs_sem, i, partner)
        copy.start()
        pair_copies.append(copy)
    head_copies = []
    for i in range(head_count):
        part = out_slice(peers[i] * 2 + s)
        pair_copies[i].wait_recv()
        part = part + rs_recv[i].astype(F32)
        if i < head_count - 1:
            x_send[i] = part.astype(BF16)
            for k, lines in enumerate(chunks):
                copy = remote(
                    x_send.at[i, lines], x_recv.at[i, lines], x_sem, i * CHUNKS + k, {"head": peers[i]}
                )
                copy.start()
                head_copies.append(copy)
    part = part + res_ref[...].astype(F32)
    sends += pair_copies + head_copies
    to_heads = []
    to_partner = []
    for k, lines in enumerate(chunks):
        own = part[lines]
        for i in range(head_count - 1):
            head_copies[i * CHUNKS + k].wait_recv()
            own = own + x_recv[i, lines].astype(F32)
        own16 = own.astype(BF16)
        new_res_ref[lines, :] = own16
        hid[shard, lines] = own16
        mine = hid.at[shard, lines]
        for i in range(head_count - 1):
            copy = remote(mine, mine, ag_sem, i * CHUNKS + k, {"head": peers[i]})
            copy.start()
            to_heads.append(copy)
        copy = remote(mine, mine, agf_sem, (head_count - 1) * CHUNKS + k, partner)
        copy.start()
        to_partner.append(copy)
    iw_load.wait()

    def projected(r, start):
        cols = pl.ds(pl.multiple_of(r * width, width), width)
        piece = hid[r].astype(F32)
        scaled = (piece * norm_gain_ref[:, cols]).astype(BF16)
        term = dot(scaled, iw[cols, :])
        logits = dot_nt(bw_ref[:, cols], scaled)
        square = jnp.sum(piece * piece, axis=1, keepdims=True)
        if start is None:
            macc[...] = term
            return logits, square
        macc[...] += term
        return start[0] + logits, start[1] + square

    sources = [lax.rem(h - 1 - i + head_count, head_count) * 2 for i in range(head_count - 1)]
    parts = projected(shard, None)
    own_copies = list(to_partner)
    for copy in own_copies:
        copy.wait_recv()
    parts = projected(h * 2 + 1 - s, parts)
    for k, lines in enumerate(chunks):
        for i in range(head_count - 1):
            to_heads[k * (head_count - 1) + i].wait_recv()
            piece = hid.at[sources[i] + s, lines]
            copy = remote(piece, piece, agf_sem, i * CHUNKS + k, partner)
            copy.start()
            to_partner.append(copy)
    for i in range(head_count - 1):
        parts = projected(sources[i] + s, parts)
    for copy in to_partner[CHUNKS:]:
        copy.wait_recv()
    for i in range(head_count - 1):
        parts = projected(sources[i] + 1 - s, parts)
    sends += to_heads + to_partner
    scale = lax.rsqrt(parts[1] / (2 * head_count * width) + EPSILON)
    group = 2 * DK + 2 * DV
    key_here = iw.shape[1] // group
    value_here = 2 * key_here

    beta = jax.nn.sigmoid(parts[0].T * scale)
    queries, grams, attends, values_of, keys_of = [], [], [], [], []
    for j in range(key_here):
        m = macc[:, j * group : (j + 1) * group] * scale
        q = unit(silu(m[:, :DK])) * DK**-0.5
        k = unit(silu(m[:, DK : 2 * DK]))
        v = silu(m[:, 2 * DK :])
        q16, k16 = q.astype(BF16), k.astype(BF16)
        queries.append(q)
        keys_of.append(k)
        values_of += [v[:, :DV], v[:, DV:]]
        grams.append(dot_nt(k16, k16))
        attends.append(dot_nt(q16, k16))
    systems, inverses, grids = [], [], []
    for n in range(value_here):
        grid = grid_ref[n]
        system = jnp.where(strictly, beta[:, n : n + 1] * grams[n // 2] * grid, 0.0)
        grids.append((attends[n // 2] * grid).astype(BF16))
        systems.append(system)
        inverses.append(eye - jnp.where((row >> 1) == (col >> 1), system, 0.0))
    level = 1
    while (1 << level) < half:
        mask = ((row >> (level + 1)) == (col >> (level + 1))) & ((row >> level) != (col >> level))
        halves = [inverse.astype(BF16) for inverse in inverses]
        firsts = [
            dot(jnp.where(mask, system, 0.0).astype(BF16), inverse).astype(BF16)
            for system, inverse in zip(systems, halves)
        ]
        inverses = [
            full - dot(inverse, product)
            for full, inverse, product in zip(inverses, halves, firsts)
        ]
        level += 1
    last = ctx_count - 1
    nxt = {"ctx": lax.min(c + 1, last)}
    prv = {"ctx": lax.max(c - 1, 0)}

    def early_copy(n):
        return remote(early_out.at[n], early_in.at[n], early_sem, n, nxt)

    def late_copy(n):
        return remote(late_out.at[n], late_in.at[n], late_sem, n, prv)

    solutions, carries = {}, {}

    def solve(n):
        beta_n = beta[:, n : n + 1]
        right = jnp.concatenate(
            [beta_n * values_of[n], (beta_n * growth[:, n : n + 1]) * keys_of[n // 2]], axis=1
        )
        solutions[n] = dot(inverses[n].astype(BF16), right.astype(BF16)).astype(BF16)
        carries[n] = (keys_of[n // 2] * carry[:, n : n + 1]).astype(BF16)

    def piece_rows(p):
        return slice(p * DV // PIECES, (p + 1) * DV // PIECES)

    def block_ends(n, b):
        lines = slice(b * half, (b + 1) * half)
        ends = dot_tn(solutions[n][lines], carries[n][lines])
        offs[b, n] = ends[:DV]
        whole = jnp.exp(block_sum[b * half : b * half + 1, n : n + 1])
        trans[b, n] = (whole * eye[:DK, :DK] - ends[DV:]).astype(BF16)
        if b == 0:
            for p in range(PIECES):
                early_out[n * PIECES + p] = ends[piece_rows(p)].astype(BF16)

    def drain_sends():
        for copy in sends:
            copy.wait_send()
        for d in others:
            sent(d, lambda full: gather(d, full).wait_send())
            received(d, lambda full: forward(d, full).wait_send())

    def local_terms(n):
        inner = dot(grids[n], solutions[n])
        local_out[n] = inner[:, :DV]
        read[n] = (growth[:, n : n + 1] * queries[n // 2] - inner[:, DV:]).astype(BF16)

    def normed(n, b, out):
        lines = slice(b * half, (b + 1) * half)
        mean = jnp.mean(out * out, axis=1, keepdims=True)
        out = out * lax.rsqrt(mean + EPSILON) * delta_gain_ref[...]
        if isinstance(n, int):
            delta_ref[lines, n * DV : (n + 1) * DV] = out.astype(BF16)
        else:
            delta_ref[lines, pl.ds(pl.multiple_of(n * DV, DV), DV)] = out.astype(BF16)

    def finish(n, b, state):
        lines = slice(b * half, (b + 1) * half)
        normed(n, b, local_out[n, lines, :] + dot_nt(read[n, lines, :], state))

    def passed(n, p, b, state):
        return (dot(state, trans[b, n]) + offs[b, n, piece_rows(p), :]).astype(BF16)

    def whole_state(ref, n):
        return jnp.concatenate([ref[n * PIECES + p] for p in range(PIECES)], axis=0)

    if ctx_count == 4:
        four_blocks(
            c,
            half,
            value_here,
            early_copy,
            late_copy,
            solve,
            block_ends,
            local_terms,
            normed,
            finish,
            passed,
            whole_state,
            trans,
            offs,
            early_in,
            early_out,
            late_in,
            late_out,
            local_out,
            read,
            drain_sends,
            *direct,
        )
        return

    for n in range(value_here):
        solve(n)
    for n in range(value_here):
        block_ends(n, 0)

    @pl.when(c == 0)
    def _():
        for n in range(value_here * PIECES):
            early_copy(n).start()

    for n in range(value_here):
        block_ends(n, 1)
        local_terms(n)

    @pl.when(c > 0)
    def _():
        def early_turn(n, carried):
            for p in range(PIECES):
                at = n * PIECES + p
                early_copy(at).wait_recv()
                end = passed(n, p, 0, early_in[at])

                @pl.when(c < last)
                def _():
                    early_out[at] = end
                    early_copy(at).start()

                @pl.when(c == last)
                def _():
                    late_in[at] = end
                    late_out[at] = passed(n, p, 1, end)
                    late_copy(at).start()

            return carried

        lax.fori_loop(0, value_here, early_turn, 0)

    for n in range(value_here):
        finish(n, 0, whole_state(early_in, n))

    @pl.when((c > 0) & (c < last))
    def _():
        def late_turn(n, carried):
            for p in range(PIECES):
                at = n * PIECES + p
                late_copy(at).wait_recv()
                late_out[at] = passed(n, p, 1, late_in[at])
                late_copy(at).start()
            return carried

        lax.fori_loop(0, value_here, late_turn, 0)

    @pl.when(c == 0)
    def _():
        def last_turn(n, carried):
            for p in range(PIECES):
                late_copy(n * PIECES + p).wait_recv()
            finish(n, 1, whole_state(late_in, n))
            return carried

        lax.fori_loop(0, value_here, last_turn, 0)

    @pl.when(c > 0)
    def _():
        for n in range(value_here):
            finish(n, 1, whole_state(late_in, n))

    drain_sends()

    def drain(n, carry):
        @pl.when(c < last)
        def _():
            early_copy(n).wait_send()

        @pl.when(c > 0)
        def _():
            late_copy(n).wait_send()

        return carry

    lax.fori_loop(0, value_here * PIECES, drain, 0)


def four_blocks(
    c,
    half,
    value_here,
    early_copy,
    late_copy,
    solve,
    block_ends,
    local_terms,
    normed,
    finish,
    passed,
    whole_state,
    trans,
    offs,
    early_in,
    early_out,
    late_in,
    late_out,
    local_out,
    read,
    drain_sends,
    ra,
    a_out,
    c_in,
    c_out,
    v_in,
    v_out,
    comp_in,
    comp_out,
    fifth,
    ra_sem,
    c_sem,
    v_sem,
    comp_sem,
):
    low, high = pl.ds(0, half), pl.ds(half, half)
    late = slice(half, 2 * half)

    def to(device):
        return {"ctx": device}

    def read_six(n):
        return remote(read.at[n, high], ra.at[n, low], ra_sem, n, to(2))

    def read_seven(n):
        return remote(read.at[n, high], ra.at[n, high], ra_sem, value_here + n, to(1))

    def read_back(n):
        return remote(a_out.at[n], ra.at[n, high], ra_sem, value_here + n, to(2))

    def constant(n):
        return remote(c_out.at[n], c_in.at[n], c_sem, n, to(0))

    def joint(n):
        return remote(comp_out.at[n], comp_in.at[n], comp_sem, n, to(2))

    def rows_six(n):
        return remote(v_out.at[n, low], v_in.at[n], v_sem, n, to(1))

    def rows_seven(n):
        return remote(v_out.at[n, high], v_in.at[n], v_sem, value_here + n, to(0))

    def each(body, first=0, end=value_here):
        for n in range(first, end):
            body(n)

    def stepped(body):
        each(body, 0, STEPPED)

    def pulled(body):
        each(body, STEPPED)

    def halves(n):
        return [n * PIECES + p for p in range(PIECES)]

    def send(n):
        for at in halves(n):
            early_copy(at).start()

    def join(n):
        fourth = trans[1, n]
        comp_out[n, 0] = dot(trans[0, n], fourth).astype(BF16)
        comp_out[n, 1] = (dot(offs[0, n].astype(BF16), fourth) + offs[1, n]).astype(BF16)
        joint(n).start()

    for n in range(STEPPED):
        solve(n)
        block_ends(n, 0)

    @pl.when(c == 0)
    def _():
        for n in range(STEPPED):
            send(n)

    for n in range(STEPPED):
        block_ends(n, 1)

    @pl.when(c == 3)
    def _():
        stepped(join)

    for n in range(STEPPED, value_here):
        solve(n)
        block_ends(n, 0)
        block_ends(n, 1)

    @pl.when(c == 3)
    def _():
        pulled(join)

    for n in range(value_here):
        local_terms(n)

    @pl.when(c == 0)
    def _():
        def send_both(n):
            send(n)
            read_seven(n).start()

        pulled(send_both)

    @pl.when(c == 1)
    def _():
        pulled(lambda n: read_six(n).start())

    drain_sends()

    @pl.when(c == 0)
    def _():
        for n in range(value_here):
            normed(n, 0, local_out[n, :half, :])

        def step(n):
            for at in halves(n):
                late_copy(at).wait_recv()
            finish(n, 1, whole_state(late_in, n))

        def last(n):
            constant(n).wait_recv()
            rows_seven(n).wait_recv()
            normed(n, 1, local_out[n, late, :] + c_in[n].astype(F32) + v_in[n].astype(F32))

        def drain(n):
            for at in halves(n):
                early_copy(at).wait_send()

        stepped(step)
        each(drain)
        pulled(lambda n: read_seven(n).wait_send())
        pulled(last)

    @pl.when(c == 1)
    def _():
        def up(n):
            for p, at in enumerate(halves(n)):
                early_copy(at).wait_recv()
                early_out[at] = passed(n, p, 0, early_in[at])
                early_copy(at).start()

        def turn(n):
            up(n)
            read_seven(n).wait_recv()
            seven = ra[n, late, :]
            a_out[n] = dot_nt(seven, trans[1, n]).astype(BF16)
            read_back(n).start()
            c_out[n] = dot_nt(seven, offs[1, n].astype(BF16)).astype(BF16)
            constant(n).start()

        def down(n):
            for p, at in enumerate(halves(n)):
                late_copy(at).wait_recv()
                late_out[at] = passed(n, p, 1, late_in[at])
                late_copy(at).start()

        stepped(up)
        pulled(turn)
        stepped(down)
        for n in range(value_here):
            finish(n, 0, whole_state(early_in, n))
        for n in range(STEPPED):
            finish(n, 1, whole_state(late_in, n))

        def last(n):
            rows_six(n).wait_recv()
            normed(n, 1, local_out[n, late, :] + v_in[n].astype(F32))

        pulled(last)

        def drain(n):
            for at in halves(n):
                early_copy(at).wait_send()

        def drain_stepped(n):
            for at in halves(n):
                late_copy(at).wait_send()

        def drain_pulled(n):
            read_six(n).wait_send()
            read_back(n).wait_send()
            constant(n).wait_send()

        each(drain)
        stepped(drain_stepped)
        pulled(drain_pulled)

    @pl.when(c == 2)
    def _():
        def up(n):
            for p, at in enumerate(halves(n)):
                early_copy(at).wait_recv()
                early_out[at] = passed(n, p, 0, early_in[at])
                early_copy(at).start()
            joint(n).wait_recv()
            state = dot(whole_state(early_out, n), comp_in[n, 0]) + comp_in[n, 1].astype(F32)
            state = state.astype(BF16)
            fifth[n] = state
            return state

        def step(n):
            state = up(n)
            for p, at in enumerate(halves(n)):
                late_out[at] = passed(n, p, 1, state[p * DV // PIECES : (p + 1) * DV // PIECES])
                late_copy(at).start()

        def turn(n):
            state = up(n)
            read_six(n).wait_recv()
            read_back(n).wait_recv()
            reads = ra[n]
            back = dot_nt(reads, trans[1, n]).astype(BF16)
            plain = dot_nt(reads, offs[1, n].astype(BF16))
            v_out[n] = (dot_nt(back, state) + plain).astype(BF16)
            rows_seven(n).start()
            rows_six(n).start()

        stepped(step)
        pulled(turn)
        for n in range(value_here):
            finish(n, 0, whole_state(early_in, n))
            finish(n, 1, fifth[n])

        def drain(n):
            for at in halves(n):
                early_copy(at).wait_send()

        def drain_stepped(n):
            for at in halves(n):
                late_copy(at).wait_send()

        def drain_pulled(n):
            rows_six(n).wait_send()
            rows_seven(n).wait_send()

        each(drain)
        stepped(drain_stepped)
        pulled(drain_pulled)

    @pl.when(c == 3)
    def _():
        def turn(n):
            for p, at in enumerate(halves(n)):
                early_copy(at).wait_recv()
                early_out[at] = passed(n, p, 0, early_in[at])
            finish(n, 0, whole_state(early_in, n))
            finish(n, 1, whole_state(early_out, n))
            joint(n).wait_send()

        each(turn)


def settle(first_ref, second_ref, first_out, second_out, sems):
    copies = [
        pltpu.make_async_copy(first_ref, first_out, sems.at[0]),
        pltpu.make_async_copy(second_ref, second_out, sems.at[1]),
    ]
    for copy in copies:
        copy.start()
    for copy in copies:
        copy.wait()


def local(
    ctx_count,
    head_count,
    att_query,
    att_gate,
    att_kv,
    residual,
    out_weight,
    norm_gain,
    in_weight,
    beta_weight,
    log_decay,
    delta_gain,
):
    rows = att_query.shape[0]
    width = residual.shape[1]
    value_here = log_decay.shape[1]
    vmem = pl.BlockSpec(memory_space=pltpu.VMEM)
    hbm = pl.BlockSpec(memory_space=pl.ANY)
    heads_less = max(head_count - 1, 1)
    pair = pltpu.SemaphoreType.DMA
    direct = []
    if ctx_count == 4:
        block = (value_here, rows // 2, DK)
        square = (value_here, DK, DK)
        both = (value_here, 2, DK, DK)
        direct = [
            pltpu.VMEM((value_here, rows, DK), BF16),
            *[pltpu.VMEM(block, BF16)] * 4,
            pltpu.VMEM((value_here, rows, DK), BF16),
            pltpu.VMEM(both, BF16),
            pltpu.VMEM(both, BF16),
            pltpu.VMEM(square, BF16),
            pair((2, 2 * value_here)),
            pair((2, value_here)),
            pair((2, 2 * value_here)),
            pair((2, value_here)),
        ]
    outputs = pl.pallas_call(
        functools.partial(kernel, ctx_count, head_count),
        out_shape=(
            pltpu.VMEM((rows, width), BF16),
            pltpu.VMEM((rows, value_here * DV), BF16),
        ),
        in_specs=[hbm] * 10,
        out_specs=(vmem, vmem),
        scratch_shapes=[
            pltpu.VMEM(att_query.shape, BF16),
            pltpu.VMEM(att_gate.shape, BF16),
            pltpu.VMEM(residual.shape, BF16),
            pltpu.VMEM((1, norm_gain.shape[0]), F32),
            pltpu.VMEM(beta_weight.shape[::-1], BF16),
            pltpu.VMEM(log_decay.shape[::-1], F32),
            pltpu.VMEM((1, DV), F32),
            pltpu.VMEM((2, ctx_count * rows, HD), BF16),
            pltpu.VMEM(out_weight.shape, BF16),
            pltpu.VMEM(in_weight.shape, BF16),
            pltpu.VMEM(att_query.shape, BF16),
            pltpu.VMEM((head_count, rows, width), BF16),
            pltpu.VMEM((head_count, rows, width), BF16),
            pltpu.VMEM((heads_less, rows, width), BF16),
            pltpu.VMEM((heads_less, rows, width), BF16),
            pltpu.VMEM((2 * head_count, rows, width), BF16),
            pltpu.VMEM((rows, in_weight.shape[1]), F32),
            pltpu.VMEM((value_here, rows, rows), F32),
            pltpu.VMEM((rows, ctx_count * rows), F32),
            pltpu.VMEM(att_query.shape, F32),
            pltpu.VMEM((2, value_here, DK, DK), BF16),
            pltpu.VMEM((2, value_here, DK, DV), F32),
            pltpu.VMEM((value_here * PIECES, DV // PIECES, DK), BF16),
            pltpu.VMEM((value_here * PIECES, DV // PIECES, DK), BF16),
            pltpu.VMEM((value_here * PIECES, DV // PIECES, DK), BF16),
            pltpu.VMEM((value_here * PIECES, DV // PIECES, DK), BF16),
            pltpu.VMEM((value_here, rows, DV), F32),
            pltpu.VMEM((value_here, rows, DK), BF16),
            pair((11,)),
            pair((2, ctx_count)),
            pair((2, ctx_count)),
            pair((2, head_count)),
            pair((2, head_count * CHUNKS)),
            pair((2, head_count * CHUNKS)),
            pair((2, head_count * CHUNKS)),
            pair((2, value_here * PIECES)),
            pair((2, value_here * PIECES)),
            *direct,
        ],
        compiler_params=pltpu.CompilerParams(collective_id=0, has_side_effects=True),
    )(
        att_query,
        att_gate,
        att_kv,
        residual,
        out_weight,
        norm_gain.reshape(1, -1),
        in_weight,
        beta_weight.T,
        log_decay.T,
        delta_gain.reshape(1, -1),
    )
    return pl.pallas_call(
        settle,
        out_shape=tuple(jax.ShapeDtypeStruct(x.shape, x.dtype) for x in outputs),
        in_specs=[vmem, vmem],
        out_specs=(hbm, hbm),
        scratch_shapes=[pair((2,))],
    )(*[pltpu.with_memory_space_constraint(x, pltpu.VMEM) for x in outputs])


def solution(mesh):
    return jax.shard_map(
        functools.partial(local, mesh.shape["ctx"], mesh.shape["head"]),
        mesh=mesh,
        in_specs=(
            P(("groups", "ctx"), ("head", "sub")),
            P(("groups", "ctx"), ("head", "sub")),
            P(("groups", "ctx"), None),
            P(("groups", "ctx"), ("head", "sub")),
            P(("head", "sub"), None),
            P(),
            P(None, ("head", "sub")),
            P(None, ("head", "sub")),
            P(("groups", "ctx"), ("head", "sub")),
            P(),
        ),
        out_specs=(P(("groups", "ctx"), ("head", "sub")), P(("groups", "ctx"), ("head", "sub"))),
        check_vma=False,
    )
```
